256 devices in a mesh: req: 32 (over x, y, core), tp: 8 (over z).
Axes of the slice: x: 4, y: 4, z: 8, core: 2. Of those that a mesh axis runs over, the one named last changes fastest.
Arguments:
- queries: bfloat16 [4096, 8192], P('req', 'tp'), may hold values from -80 to 80
- incoming_key_value: bfloat16 [2, 4096, 1024], P(None, 'req', 'tp'), may hold values from -4 to 4
- key_value_pages: bfloat16 [16384, 32, 2, 1024], P('req', None, None, 'tp'), may hold values from -4 to 4
- page_request_home: int32 [16384], P('req'), may hold values from 0 to 16383, as said below
- lengths: int32 [1024], P('req'), may hold values from 1 to 512, 262144 in all
- request_adapter_index: int32 [1024], P('req'), may hold values from 0 to 63
- adapter_storage_slot: int32 [64], replicated, may hold values from 0 to 63, each once
- adapter_down_factor: bfloat16 [64, 8192, 64], P('req', 'tp'), may hold values from -0.25 to 0.25
- adapter_up_factor: bfloat16 [64, 64, 8192], P('req'), may hold values from -0.75 to 0.75
- output_projection_weight: bfloat16 [8192, 8192], P('tp', 'req'), may hold values from -0.75 to 0.75
Outputs:
- attn_out: bfloat16 [4096, 8192], P('tp', 'req')
The draws below stay inside these ranges and needn't reach their ends.
Inputs may be any that keep to these rules, and one draw needn't show every extreme that they name: `page_request_home`: each value once. Pages p with p // 512 = a hold pages of requests i with i // 32 = b, b != a, for at most 2 pages p for every pair a, b; in every draw some a holds exactly 2 pages of every b != a.
All inputs are finite; a program needn't handle non-finite values. No bound on the sum of `lengths` on one device may be relied on, other than what follows from the above.
Results may differ from the reference program's by a relative error of at most 0.0058.
Values may be sent and summed in bfloat16 or wider, within the bound.
A program may use at most 128 MiB of HBM per device.

```python
import math
import jax
import jax.numpy as jnp
import numpy as np
from jax import lax

MODEL_WIDTH = 8192
QUERY_HEADS = 64
KEY_VALUE_HEADS = 8
HEAD_WIDTH = 128
ADAPTER_RANK = 64
R_DEV = 32
STEP_COUNT = 4
PAGE_LENGTH = 32
MAXP = 16
CAP = 2
REQUEST_TOTAL = 1024
TOKEN_TOTAL = 4096
ADAPTER_TOTAL = 64
PAGE_TOTAL = 16384
N_REQ = 32


def home_table(key):
    per_dev = R_DEV * MAXP
    band_slots = CAP * (N_REQ - 1)
    key_masks = jax.random.fold_in(key, 11)
    key_coins = jax.random.fold_in(key, 12)
    key_center = jax.random.fold_in(key, 13)
    key_shuffle = jax.random.fold_in(key, 14)
    xor_masks = jax.random.permutation(key_masks, N_REQ - 1).astype(jnp.int32) + 1
    slot_ids = jnp.arange(per_dev, dtype=jnp.int32)
    mask_of = jnp.where(slot_ids < band_slots, xor_masks[jnp.minimum(slot_ids // CAP, N_REQ - 2)], 0)
    device_ids = jnp.arange(N_REQ, dtype=jnp.int32)[:, None]
    partner = jnp.bitwise_xor(device_ids, mask_of[None, :])
    pair_low = jnp.minimum(device_ids, partner)
    coin_flips = jax.random.randint(key_coins, (N_REQ, per_dev), 0, 2)
    paired = jnp.take_along_axis(coin_flips, pair_low, axis=0)
    center = jax.random.randint(key_center, (), 0, N_REQ)
    forced = (device_ids == center) | (partner == center)
    swapped = ((paired == 1) | forced) & (mask_of[None, :] > 0)
    owner_dev = jnp.where(swapped, partner, device_ids)
    home_ids = owner_dev * per_dev + slot_ids[None, :]
    shuffle = jax.vmap(lambda subkey: jax.random.permutation(subkey, per_dev))(jax.random.split(key_shuffle, N_REQ))
    home_ids = jnp.take_along_axis(home_ids, shuffle.astype(jnp.int32), axis=1)
    return home_ids.reshape(N_REQ * per_dev).astype(jnp.int32)


def draw_page_request_home(key, part):
    return home_table(key)


def draw_key_value_pages(key, part):
    complete_shape = (PAGE_TOTAL, PAGE_LENGTH, 2, KEY_VALUE_HEADS * HEAD_WIDTH)
    values_base = jnp.clip(jax.random.normal(jax.random.fold_in(key, 21), complete_shape, jnp.float32), -4.0, 4.0)
    return values_base.astype(jnp.bfloat16)


def draw_queries(key, part):
    complete_shape = (TOKEN_TOTAL, QUERY_HEADS * HEAD_WIDTH)
    values_base = jnp.clip(jax.random.normal(jax.random.fold_in(key, 31), complete_shape, jnp.float32), -4.0, 4.0)
    return values_base.astype(jnp.bfloat16)


def touch_ends(entries, rng, low, largest):
    dims = entries.shape
    place = [jax.random.randint(jax.random.fold_in(rng, axis), (), 0, dims[axis]) for axis in range(len(dims))]
    entries = entries.at[tuple(place)].set(low)
    longest = dims.index(max(dims))
    place[longest] = (place[longest] + 1) % dims[longest]
    return entries.at[tuple(place)].set(largest)


def levels(rng, extent, cuts, smallest, high):
    gain = 1.0
    for dim, blocks in cuts:
        heights = jax.random.uniform(jax.random.fold_in(jax.random.fold_in(rng, 6), dim), (blocks,), jnp.float32, smallest / len(cuts), high / len(cuts))
        gain = gain * jnp.repeat(jnp.exp(heights), extent[dim] // blocks).reshape((-1,) + (1,) * (len(extent) - 1 - dim))
    return gain


def rank_bounds(number_of, skew):
    loads = [(1 << 20) // math.isqrt(grade ** skew) + 1 for grade in range(1, number_of + 1)]
    deviation = 1 + sum(loads) // (1 << 30)
    return np.cumsum(np.array([max(1, weight // deviation) for weight in loads]))


def skewed_ids(rng, dims, number_of, lean):
    listing = rank_bounds(number_of, lean)
    ticket = jax.random.randint(jax.random.fold_in(rng, 1), dims, 0, int(listing[number_of - 1]))
    standing = jnp.searchsorted(jnp.asarray(listing, jnp.int32), ticket, side="right")
    return jax.random.permutation(jax.random.fold_in(rng, 2), number_of)[standing].astype(jnp.int32)


def split_up(amount, total, reach, slope):
    loads = [(1 << 20) // math.isqrt(rank ** slope) + 1 for rank in range(2, amount + 1)]
    surplus, given = total - reach - (amount - 1), [1] * (amount - 1)
    while surplus > 0:
        free = [i for i in range(amount - 1) if given[i] < reach]
        pool, left = sum([loads[i] for i in free]), surplus
        for i in free:
            extra = min(reach - given[i], max(1, left * loads[i] // pool), surplus)
            given[i] = given[i] + extra
            surplus = surplus - extra
    return np.array([reach] + given)


def uneven(stream_key, amount, total, most, slope):
    if amount == 2:
        one = jax.random.randint(stream_key, (), max(1, total - most), min(most, total - 1) + 1)
        return jnp.stack([one, total - one])
    sizes = jnp.asarray(split_up(amount, total, most, slope), jnp.int32)
    twos = (amount - 1) // 2
    donor, sink = sizes[1:1 + 2 * twos:2], sizes[2:2 + 2 * twos:2]
    margin = jnp.minimum(donor - 1, most - sink)
    passed = jax.random.randint(jax.random.fold_in(stream_key, 1), (twos,), 0, 1 << 20) % (margin + 1)
    sizes = sizes.at[1:1 + 2 * twos:2].set(donor - passed).at[2:2 + 2 * twos:2].set(sink + passed)
    return sizes[jax.random.permutation(jax.random.fold_in(stream_key, 2), amount)]


def normal_values(rng, shape, scale, bound, shards=(), kind=jnp.bfloat16):
    drawn = scale * jax.random.normal(rng, shape, jnp.float32)
    if shards:
        drawn = drawn * levels(rng, shape, shards, -0.22, 0.18)
    return jnp.clip(drawn, -bound, bound).astype(kind)


def setup_inputs(seed: int = 0) -> dict:
    splits = jax.random.split(jax.random.key(seed), 11)
    queries = draw_queries(jax.random.fold_in(splits[10], 71), 0)
    incoming_key_value = normal_values(splits[1], (2, TOKEN_TOTAL, KEY_VALUE_HEADS * HEAD_WIDTH), 1.0, 4.0, ((1, 32), (2, 8)))
    key_value_pages = draw_key_value_pages(jax.random.fold_in(splits[10], 71), 0)
    page_request_home = draw_page_request_home(jax.random.fold_in(splits[10], 71), 0)
    lengths = uneven(splits[4], REQUEST_TOTAL, REQUEST_TOTAL * MAXP * PAGE_LENGTH // 2, MAXP * PAGE_LENGTH, 2).astype(jnp.int32)
    request_adapter_index = touch_ends(skewed_ids(splits[5], (REQUEST_TOTAL,), ADAPTER_TOTAL, 2), jax.random.fold_in(splits[5], 3), 0, ADAPTER_TOTAL - 1).astype(jnp.int32)
    adapter_storage_slot = jax.random.permutation(splits[6], ADAPTER_TOTAL).astype(jnp.int32)
    adapter_down_factor = normal_values(splits[7], (ADAPTER_TOTAL, QUERY_HEADS * HEAD_WIDTH, ADAPTER_RANK), (4.0 / (QUERY_HEADS * HEAD_WIDTH) ** 0.5), 0.25, ((0, 32), (1, 8)))
    adapter_up_factor = normal_values(splits[8], (ADAPTER_TOTAL, ADAPTER_RANK, MODEL_WIDTH), ADAPTER_RANK ** -0.5, 0.75, ((0, 32),))
    output_projection_weight = normal_values(splits[9], (QUERY_HEADS * HEAD_WIDTH, MODEL_WIDTH), (12.0 / (QUERY_HEADS * HEAD_WIDTH) ** 0.5), 0.75, ((0, 8), (1, 32)))
    return dict(queries=queries, incoming_key_value=incoming_key_value, key_value_pages=key_value_pages, page_request_home=page_request_home, lengths=lengths, request_adapter_index=request_adapter_index, adapter_storage_slot=adapter_storage_slot, adapter_down_factor=adapter_down_factor, adapter_up_factor=adapter_up_factor, output_projection_weight=output_projection_weight)


def reference(queries, incoming_key_value, key_value_pages, page_request_home, lengths, request_adapter_index, adapter_storage_slot, adapter_down_factor, adapter_up_factor, output_projection_weight):
    query_group_count = QUERY_HEADS // KEY_VALUE_HEADS
    cache_extent = MAXP * PAGE_LENGTH
    score_scale = 1.0 / math.sqrt(HEAD_WIDTH)
    inverse = jnp.zeros((PAGE_TOTAL,), jnp.int32).at[page_request_home].set(jnp.arange(PAGE_TOTAL, dtype=jnp.int32))
    req_slot = adapter_storage_slot[request_adapter_index]
    position = jnp.arange(cache_extent + STEP_COUNT, dtype=jnp.int32)
    step_index = jnp.arange(STEP_COUNT, dtype=jnp.int32)

    def single_request(request_number):
        page_locations = lax.dynamic_slice_in_dim(inverse, request_number * MAXP, MAXP)
        stored_entries = key_value_pages[page_locations].reshape(cache_extent, 2, KEY_VALUE_HEADS, HEAD_WIDTH)
        fresh_key_value = lax.dynamic_slice_in_dim(incoming_key_value, request_number * STEP_COUNT, STEP_COUNT, 1).reshape(2, STEP_COUNT, KEY_VALUE_HEADS, HEAD_WIDTH)
        fresh_key_value = jnp.transpose(fresh_key_value, (1, 0, 2, 3))
        all_keys = jnp.concatenate([stored_entries, fresh_key_value], axis=0).astype(jnp.float32)
        query_vectors = lax.dynamic_slice_in_dim(queries, request_number * STEP_COUNT, STEP_COUNT, 0)
        query_vectors = query_vectors.reshape(STEP_COUNT, KEY_VALUE_HEADS, query_group_count, HEAD_WIDTH).astype(jnp.float32)
        scores = jnp.einsum('sgqd,lgd->gqsl', query_vectors, all_keys[:, 0]) * score_scale
        usable = jnp.where(position[None, :] < cache_extent, position[None, :] < lengths[request_number], position[None, :] - cache_extent <= step_index[:, None])
        scores = jnp.where(usable[None, None], scores, -jnp.inf)
        row_top = lax.optimization_barrier(jnp.max(scores, axis=-1, keepdims=True))
        weights = jnp.exp(scores - row_top)
        probs = (weights / lax.optimization_barrier(jnp.sum(weights, axis=-1, keepdims=True))).astype(jnp.bfloat16)
        attention_mixed_output = jnp.einsum('gqsl,lgd->sgqd', probs.astype(jnp.float32), all_keys[:, 1])
        attention_mixed_output = attention_mixed_output.astype(jnp.bfloat16).reshape(STEP_COUNT, QUERY_HEADS * HEAD_WIDTH)
        slot_number = req_slot[request_number]
        reduced_features = jnp.dot(attention_mixed_output, adapter_down_factor[slot_number], preferred_element_type=jnp.float32).astype(jnp.bfloat16)
        adapter_correction = jnp.dot(reduced_features, adapter_up_factor[slot_number], preferred_element_type=jnp.float32)
        return (attention_mixed_output, adapter_correction)
    attention_all_rows, adapter_total_terms = lax.map(single_request, jnp.arange(REQUEST_TOTAL, dtype=jnp.int32))
    attention_all_rows = attention_all_rows.reshape(TOKEN_TOTAL, QUERY_HEADS * HEAD_WIDTH)
    plain_output_rows = jnp.dot(attention_all_rows, output_projection_weight, preferred_element_type=jnp.float32)
    return (plain_output_rows + adapter_total_terms.reshape(TOKEN_TOTAL, MODEL_WIDTH)).astype(jnp.bfloat16)
```

```python
import functools
import math

import jax
import jax.numpy as jnp
from jax import lax
from jax.experimental import pallas as pl
from jax.experimental.pallas import tpu as pltpu
from jax.sharding import PartitionSpec as P

QUERY_HEADS = 64
KEY_VALUE_HEADS = 8
GROUP = QUERY_HEADS // KEY_VALUE_HEADS
HEAD_WIDTH = 128
STEP_COUNT = 4
PAGE_LENGTH = 32
PAGE_ROWS = 2 * PAGE_LENGTH
MAXP = 16
CAP = 2
VMEM_BYTES = 60 * 1024 * 1024


def pick_kernel(source, pages, outbox, sem):
    count = outbox.shape[0] // PAGE_ROWS

    def copy(k):
        start = pl.multiple_of(source[k] * PAGE_ROWS, PAGE_ROWS)
        put = pl.multiple_of(k * PAGE_ROWS, PAGE_ROWS)
        return pltpu.make_async_copy(
            pages.at[pl.ds(start, PAGE_ROWS), :], outbox.at[pl.ds(put, PAGE_ROWS), :], sem
        )

    for k in range(count):
        copy(k).start()
    pltpu.make_async_copy(pages.at[pl.ds(0, count * PAGE_ROWS), :], outbox, sem).wait()


def pick(out_source, pages):
    count = out_source.shape[0]
    return pl.pallas_call(
        pick_kernel,
        out_shape=jax.ShapeDtypeStruct((count * PAGE_ROWS, HEAD_WIDTH), pages.dtype),
        grid_spec=pltpu.PrefetchScalarGridSpec(
            num_scalar_prefetch=1,
            grid=(1,),
            in_specs=[pl.BlockSpec(memory_space=pl.ANY)],
            out_specs=pl.BlockSpec((count * PAGE_ROWS, HEAD_WIDTH), lambda i, s: (0, 0)),
            scratch_shapes=[pltpu.SemaphoreType.DMA],
        ),
        name="pick",
    )(out_source, pages)


def exchange_kernel(
    n, outbox, labels, up, inbox, inlab, upin, sent, got, lab_sent, lab_got, up_sent, up_got, own_sem
):
    me = lax.axis_index("req")
    lane = lax.axis_index("tp")
    block = CAP * PAGE_ROWS
    rows, columns = upin.shape[1], upin.shape[2]

    barrier = pltpu.get_barrier_semaphore()

    def greet(d, carry):
        pl.semaphore_signal(barrier, inc=1, device_id={"req": lax.rem(me + d, n)})
        return carry

    lax.fori_loop(1, n, greet, 0)
    pl.semaphore_wait(barrier, n - 1)

    def up_part(peer):
        return up.at[
            pl.ds(pl.multiple_of(lane * rows, rows), rows),
            pl.ds(pl.multiple_of(peer * columns, columns), columns),
        ]

    def copies(d):
        peer = lax.rem(me + d, n)
        to = {"req": peer}
        return (
            pltpu.make_async_remote_copy(
                labels.at[peer], inlab.at[me], lab_sent.at[d - 1], lab_got.at[d - 1], device_id=to
            ),
            pltpu.make_async_remote_copy(
                outbox.at[pl.ds(pl.multiple_of(peer * block, block), block), :],
                inbox.at[pl.ds(pl.multiple_of(me * block, block), block), :],
                sent.at[d - 1],
                got.at[d - 1],
                device_id=to,
            ),
            pltpu.make_async_remote_copy(
                up_part(peer), upin.at[me], up_sent.at[d - 1], up_got.at[d - 1], device_id=to
            ),
        )

    own = pltpu.make_async_copy(up_part(me), upin.at[me], own_sem)
    own.start()

    def begin(d, carry):
        for copy in copies(d):
            copy.start()
        return carry

    lax.fori_loop(1, n, begin, 0)

    def finish(d, carry):
        for copy in copies(d):
            copy.wait()
        return carry

    lax.fori_loop(1, n, finish, 0)
    own.wait()


def exchange(outbox, labels, up, n, tp_count):
    rows, columns = up.shape[0] // tp_count, up.shape[1] // n
    any_space = pl.BlockSpec(memory_space=pl.ANY)
    return pl.pallas_call(
        functools.partial(exchange_kernel, n),
        out_shape=(
            jax.ShapeDtypeStruct(outbox.shape, outbox.dtype),
            jax.ShapeDtypeStruct(labels.shape, labels.dtype),
            jax.ShapeDtypeStruct((n, rows, columns), up.dtype),
        ),
        in_specs=[any_space] * 3,
        out_specs=[any_space] * 3,
        scratch_shapes=[pltpu.SemaphoreType.DMA((n - 1,))] * 6 + [pltpu.SemaphoreType.DMA],
        compiler_params=pltpu.CompilerParams(collective_id=0, has_side_effects=True),
        name="exchange",
    )(outbox, labels, up)


def attend_kernel(table, lengths, queries, fresh, pages, inbox, out, cands, outf, sem):
    n_local, n_in = pages.shape[0], inbox.shape[0]
    requests = fresh.shape[0]
    load_local = pltpu.make_async_copy(pages, cands.at[pl.ds(0, n_local), :], sem.at[0])
    load_in = pltpu.make_async_copy(inbox, cands.at[pl.ds(n_local, n_in), :], sem.at[1])
    load_local.start()
    load_in.start()
    load_local.wait()
    load_in.wait()
    old = MAXP * PAGE_ROWS
    width = old + HEAD_WIDTH
    rows = GROUP * STEP_COUNT
    column = lax.broadcasted_iota(jnp.int32, (rows, width), 1)
    step = lax.rem(lax.broadcasted_iota(jnp.int32, (rows, width), 0), STEP_COUNT)
    is_key = lax.rem(column, 2) == 0
    new_index = (column - old) // 2
    keep_new = is_key & (column >= old) & (new_index <= step)
    position = jnp.where(is_key & (column < old), column // 2, 1 << 20)
    scale = 1.0 / math.sqrt(HEAD_WIDTH)
    filler = jnp.zeros((HEAD_WIDTH - fresh.shape[1], HEAD_WIDTH), fresh.dtype)

    def one(request, query):
        pieces = []
        for j in range(MAXP):
            start = pl.multiple_of(table[request * MAXP + j] * PAGE_ROWS, PAGE_ROWS)
            pieces.append(cands[pl.ds(start, PAGE_ROWS), :])
        pieces.append(fresh[request])
        pieces.append(filler)
        stored = jnp.concatenate(pieces, axis=0)
        scores = (
            lax.dot_general(
                query, stored, (((1,), (1,)), ((), ())), preferred_element_type=jnp.float32
            )
            * scale
        )
        keep = keep_new | (position < lengths[request])
        scores = jnp.where(keep, scores, -jnp.inf)
        top = jnp.max(scores, axis=1, keepdims=True)
        weights = jnp.exp(scores - top)
        probs = weights / jnp.sum(weights, axis=1, keepdims=True)
        probs = pltpu.roll(probs, 1, 1).astype(jnp.bfloat16)
        return jnp.dot(probs, stored, preferred_element_type=jnp.float32)

    def pair(index, carry):
        base = pl.multiple_of(index * 2 * STEP_COUNT, 2 * STEP_COUNT)
        block = queries[pl.ds(base, 2 * STEP_COUNT), :].astype(jnp.float32)
        mixed = []
        for k in range(2):
            part = block[k * STEP_COUNT : (k + 1) * STEP_COUNT]
            query = jnp.concatenate(
                [part[:, h * HEAD_WIDTH : (h + 1) * HEAD_WIDTH] for h in range(GROUP)], axis=0
            ).astype(jnp.bfloat16)
            mixed.append(one(index * 2 + k, query))
        for h in range(GROUP):
            both = jnp.concatenate(
                [m[h * STEP_COUNT : (h + 1) * STEP_COUNT] for m in mixed], axis=0
            )
            outf[pl.ds(base, 2 * STEP_COUNT), h * HEAD_WIDTH : (h + 1) * HEAD_WIDTH] = both
        return carry

    lax.fori_loop(0, requests // 2, pair, 0)
    out[...] = outf[...].astype(out.dtype)


def attend(table, lengths, queries, fresh, pages, inbox):
    tokens, width = queries.shape
    hbm = pl.BlockSpec(memory_space=pltpu.HBM)
    vmem = pl.BlockSpec(memory_space=pltpu.VMEM)
    smem = pl.BlockSpec(memory_space=pltpu.SMEM)
    return pl.pallas_call(
        attend_kernel,
        out_shape=jax.ShapeDtypeStruct((tokens, width), queries.dtype),
        in_specs=[smem, smem, vmem, vmem, hbm, hbm],
        out_specs=vmem,
        scratch_shapes=[
            pltpu.VMEM((pages.shape[0] + inbox.shape[0], HEAD_WIDTH), pages.dtype),
            pltpu.VMEM((tokens, width), jnp.float32),
            pltpu.SemaphoreType.DMA((2,)),
        ],
        compiler_params=pltpu.CompilerParams(vmem_limit_bytes=32 * 1024 * 1024),
        name="attend",
    )(table, lengths, queries, fresh, pages, inbox)


def on_device(
    queries,
    incoming_key_value,
    key_value_pages,
    page_request_home,
    lengths,
    request_adapter_index,
    adapter_storage_slot,
    adapter_down_factor,
    adapter_up_factor,
    output_projection_weight,
):
    n = lax.axis_size("req")
    tp_count = lax.axis_size("tp")
    me = lax.axis_index("req")
    lane = lax.axis_index("tp")
    per_dev = key_value_pages.shape[0]
    requests = lengths.shape[0]
    total = n * per_dev
    pages = key_value_pages.reshape(per_dev * PAGE_ROWS, HEAD_WIDTH)

    numbers = jnp.arange(per_dev, dtype=jnp.int32)
    peers = jnp.arange(n, dtype=jnp.int32)
    owner = page_request_home // per_dev
    match = (owner[:, None] == peers[None, :]) & (owner != me)[:, None]
    key = (numbers * total + page_request_home)[:, None]
    low_key = jnp.min(jnp.where(match, key, jnp.int32(2**30)), axis=0)
    high_key = jnp.max(jnp.where(match, key, -1), axis=0)
    keys = jnp.stack([low_key, high_key], axis=1)
    there = jnp.stack([high_key >= 0, high_key > low_key], axis=1)
    out_source = jnp.where(there, keys // total, 0).reshape(-1)
    out_label = jnp.where(there, keys % total, -1)

    slot_count = adapter_storage_slot.shape[0]
    slots = jnp.arange(slot_count, dtype=jnp.int32)
    own_slot = jnp.sum(
        jnp.where(
            request_adapter_index[:, None] == slots[None, :], adapter_storage_slot[None, :], 0
        ),
        axis=1,
    )
    labels = jnp.concatenate(
        [
            out_label,
            jnp.zeros((n, 64 - CAP), jnp.int32),
            jnp.broadcast_to(own_slot[None, :], (n, requests)),
            jnp.zeros((n, 64 - requests), jnp.int32),
        ],
        axis=1,
    ).reshape(n, 1, 128)

    outbox = pick(out_source, pages)
    up = adapter_up_factor.reshape(-1, adapter_up_factor.shape[2])
    inbox, inlab, upin = exchange(outbox, labels, up, n, tp_count)
    up_all = lax.all_gather(upin, "tp", axis=0, tiled=False)

    mine = (peers == me)[:, None]
    arrived = jnp.where(mine, -1, inlab[:, 0, :CAP]).reshape(-1)
    own_label = jnp.where(owner == me, page_request_home - me * per_dev, -1)
    in_label = jnp.where(arrived >= 0, arrived - me * per_dev, -1)
    candidate = jnp.concatenate([own_label, in_label], axis=0)
    candidate_numbers = jnp.arange(candidate.shape[0], dtype=jnp.int32)
    table = jnp.sum(
        jnp.where(candidate[:, None] == numbers[None, :], candidate_numbers[:, None], 0), axis=0
    )
    req_slot = jnp.where(mine, own_slot[None, :], inlab[:, 0, 64 : 64 + requests]).reshape(-1)
    token_slot = jnp.repeat(req_slot, STEP_COUNT)

    fresh = jnp.transpose(incoming_key_value, (1, 0, 2)).reshape(
        requests, 2 * STEP_COUNT, HEAD_WIDTH
    )
    fresh = jnp.pad(fresh, ((0, 0), (0, 8), (0, 0)))
    mixed = attend(table, lengths, queries, fresh, pages, inbox)

    everyone = lax.all_gather(mixed, "req", axis=0, tiled=True)
    own_adapters, _, rank = adapter_down_factor.shape
    down = jnp.transpose(adapter_down_factor, (1, 0, 2)).reshape(-1, own_adapters * rank)
    columns = output_projection_weight.shape[1]
    weights = jnp.concatenate([output_projection_weight, down], axis=1)
    product = jnp.dot(everyone, weights, preferred_element_type=jnp.float32)
    spot = jnp.arange(columns + own_adapters * rank, dtype=jnp.int32)
    spot_slot = jnp.where(spot < columns, -1, me * own_adapters + (spot - columns) // rank)
    keep = (spot_slot[None, :] < 0) | (spot_slot[None, :] == token_slot[:, None])
    partial = jnp.where(keep, product, 0.0).astype(jnp.bfloat16)
    reduced = lax.psum_scatter(partial, "tp", scatter_dimension=0, tiled=True)
    low = reduced[:, columns : columns + rank]
    for k in range(1, own_adapters):
        low = low + reduced[:, columns + k * rank : columns + (k + 1) * rank]
    low = lax.psum(low, "req")
    block_rows = reduced.shape[0]
    up_columns = jnp.transpose(up_all, (1, 0, 2, 3)).reshape(slot_count * rank, columns)
    block_slot = lax.dynamic_slice_in_dim(token_slot, lane * block_rows, block_rows)
    selector = (block_slot[:, None] == slots[None, :]).astype(jnp.bfloat16)
    expanded = (selector[:, :, None] * low[:, None, :]).reshape(block_rows, slot_count * rank)
    extra = jnp.dot(expanded, up_columns, preferred_element_type=jnp.float32)
    return (reduced[:, :columns].astype(jnp.float32) + extra).astype(jnp.bfloat16)


def solution(mesh):
    return jax.shard_map(
        on_device,
        mesh=mesh,
        in_specs=(
            P("req", "tp"),
            P(None, "req", "tp"),
            P("req", None, None, "tp"),
            P("req"),
            P("req"),
            P("req"),
            P(),
            P("req", "tp", None),
            P("req", None, None),
            P("tp", "req"),
        ),
        out_specs=P("tp", "req"),
        check_vma=False,
    )
```

```python
import functools
import math

import jax
import jax.numpy as jnp
from jax import lax
from jax.experimental import pallas as pl
from jax.experimental.pallas import tpu as pltpu
from jax.sharding import PartitionSpec as P

QUERY_HEADS = 64
KEY_VALUE_HEADS = 8
GROUP = QUERY_HEADS // KEY_VALUE_HEADS
HEAD_WIDTH = 128
STEP_COUNT = 4
PAGE_LENGTH = 32
PAGE_ROWS = 2 * PAGE_LENGTH
MAXP = 16
CAP = 2
VMEM_BYTES = 60 * 1024 * 1024


def pick_kernel(source, pages, outbox, sem):
    count = outbox.shape[0] // PAGE_ROWS

    def copy(k):
        start = pl.multiple_of(source[k] * PAGE_ROWS, PAGE_ROWS)
        put = pl.multiple_of(k * PAGE_ROWS, PAGE_ROWS)
        return pltpu.make_async_copy(
            pages.at[pl.ds(start, PAGE_ROWS), :], outbox.at[pl.ds(put, PAGE_ROWS), :], sem
        )

    for k in range(count):
        copy(k).start()
    pltpu.make_async_copy(pages.at[pl.ds(0, count * PAGE_ROWS), :], outbox, sem).wait()


def pick(out_source, pages):
    count = out_source.shape[0]
    return pl.pallas_call(
        pick_kernel,
        out_shape=jax.ShapeDtypeStruct((count * PAGE_ROWS, HEAD_WIDTH), pages.dtype),
        grid_spec=pltpu.PrefetchScalarGridSpec(
            num_scalar_prefetch=1,
            grid=(1,),
            in_specs=[pl.BlockSpec(memory_space=pl.ANY)],
            out_specs=pl.BlockSpec((count * PAGE_ROWS, HEAD_WIDTH), lambda i, s: (0, 0)),
            scratch_shapes=[pltpu.SemaphoreType.DMA],
        ),
        name="pick",
    )(out_source, pages)


def exchange_kernel(
    n, planes, outbox, labels, up, inbox, inlab, upall,
    sent, got, lab_sent, lab_got, up_sent, up_got, ring_sent, ring_got, own_sem,
):
    me = lax.axis_index("req")
    lane = lax.axis_index("tp")
    block = CAP * PAGE_ROWS
    rows, columns = upall.shape[2], upall.shape[3]
    above, below = lax.rem(lane + 1, planes), lax.rem(lane + planes - 1, planes)

    barrier = pltpu.get_barrier_semaphore()

    def greet(d, carry):
        pl.semaphore_signal(barrier, inc=1, device_id={"req": lax.rem(me + d, n)})
        return carry

    lax.fori_loop(1, n, greet, 0)
    pl.semaphore_signal(barrier, inc=1, device_id={"tp": above})
    pl.semaphore_signal(barrier, inc=1, device_id={"tp": below})
    pl.semaphore_wait(barrier, n + 1)

    def up_part(peer):
        return up.at[
            pl.ds(pl.multiple_of(lane * rows, rows), rows),
            pl.ds(pl.multiple_of(peer * columns, columns), columns),
        ]

    def label_copy(d):
        peer = lax.rem(me + d, n)
        return pltpu.make_async_remote_copy(
            labels.at[peer],
            inlab.at[me],
            lab_sent.at[d - 1],
            lab_got.at[d - 1],
            device_id={"req": peer},
        )

    def up_copy(d):
        peer = lax.rem(me + d, n)
        return pltpu.make_async_remote_copy(
            up_part(peer),
            upall.at[me, lane],
            up_sent.at[d - 1],
            up_got.at[d - 1],
            device_id={"req": peer},
        )

    def page_copy(d):
        peer = lax.rem(me + d, n)
        return pltpu.make_async_remote_copy(
            outbox.at[pl.ds(pl.multiple_of(peer * block, block), block), :],
            inbox.at[pl.ds(pl.multiple_of(me * block, block), block), :],
            sent.at[d - 1],
            got.at[d - 1],
            device_id={"req": peer},
        )

    own = pltpu.make_async_copy(up_part(me), upall.at[me, lane], own_sem)
    own.start()

    def begin_up(d, carry):
        up_copy(d).start()
        return carry

    def begin_pages(d, carry):
        label_copy(d).start()
        page_copy(d).start()
        return carry

    def finish_up(d, carry):
        up_copy(d).wait()
        return carry

    def finish_pages(d, carry):
        label_copy(d).wait()
        page_copy(d).wait()
        return carry

    lax.fori_loop(1, n, begin_up, 0)
    lax.fori_loop(1, n, begin_pages, 0)
    lax.fori_loop(1, n, finish_up, 0)
    own.wait()

    hops = planes // 2

    def ring_copy(way, hop):
        peer = above if way == 0 else below
        origin = lax.rem(lane + planes + (hop if way == 1 else -hop), planes)
        part = upall.at[:, origin]
        if hop == hops - 1:
            part = upall.at[pl.ds(way * (n // 2), n // 2), origin]
        return pltpu.make_async_remote_copy(
            part, part, ring_sent.at[way, hop], ring_got.at[way, hop], device_id={"tp": peer}
        )

    for hop in range(hops):
        for way in range(2):
            if hop:
                ring_copy(way, hop - 1).wait_recv()
            ring_copy(way, hop).start()
    for way in range(2):
        ring_copy(way, hops - 1).wait_recv()
        for hop in range(hops):
            ring_copy(way, hop).wait_send()
    lax.fori_loop(1, n, finish_pages, 0)


def exchange(outbox, labels, up, n, planes):
    rows, columns = up.shape[0] // planes, up.shape[1] // n
    any_space = pl.BlockSpec(memory_space=pl.ANY)
    return pl.pallas_call(
        functools.partial(exchange_kernel, n, planes),
        out_shape=(
            jax.ShapeDtypeStruct(outbox.shape, outbox.dtype),
            jax.ShapeDtypeStruct(labels.shape, labels.dtype),
            jax.ShapeDtypeStruct((n, planes, rows, columns), up.dtype),
        ),
        in_specs=[any_space] * 3,
        out_specs=[any_space] * 3,
        scratch_shapes=[pltpu.SemaphoreType.DMA((n - 1,))] * 6
        + [pltpu.SemaphoreType.DMA((2, planes // 2))] * 2
        + [pltpu.SemaphoreType.DMA],
        compiler_params=pltpu.CompilerParams(collective_id=0, has_side_effects=True),
        name="exchange",
    )(outbox, labels, up)


def attend_kernel(table, lengths, queries, fresh, pages, inbox, out, cands, outf, sem):
    n_local, n_in = pages.shape[0], inbox.shape[0]
    requests = fresh.shape[0]
    load_local = pltpu.make_async_copy(pages, cands.at[pl.ds(0, n_local), :], sem.at[0])
    load_in = pltpu.make_async_copy(inbox, cands.at[pl.ds(n_local, n_in), :], sem.at[1])
    load_local.start()
    load_in.start()
    load_local.wait()
    load_in.wait()
    old = MAXP * PAGE_ROWS
    width = old + HEAD_WIDTH
    rows = GROUP * STEP_COUNT
    column = lax.broadcasted_iota(jnp.int32, (rows, width), 1)
    step = lax.rem(lax.broadcasted_iota(jnp.int32, (rows, width), 0), STEP_COUNT)
    is_key = lax.rem(column, 2) == 0
    new_index = (column - old) // 2
    keep_new = is_key & (column >= old) & (new_index <= step)
    position = jnp.where(is_key & (column < old), column // 2, 1 << 20)
    scale = 1.0 / math.sqrt(HEAD_WIDTH)
    filler = jnp.zeros((HEAD_WIDTH - fresh.shape[1], HEAD_WIDTH), fresh.dtype)

    def one(request, query):
        pieces = []
        for j in range(MAXP):
            start = pl.multiple_of(table[request * MAXP + j] * PAGE_ROWS, PAGE_ROWS)
            pieces.append(cands[pl.ds(start, PAGE_ROWS), :])
        pieces.append(fresh[request])
        pieces.append(filler)
        stored = jnp.concatenate(pieces, axis=0)
        scores = (
            lax.dot_general(
                query, stored, (((1,), (1,)), ((), ())), preferred_element_type=jnp.float32
            )
            * scale
        )
        keep = keep_new | (position < lengths[request])
        scores = jnp.where(keep, scores, -jnp.inf)
        top = jnp.max(scores, axis=1, keepdims=True)
        weights = jnp.exp(scores - top)
        probs = weights / jnp.sum(weights, axis=1, keepdims=True)
        probs = pltpu.roll(probs, 1, 1).astype(jnp.bfloat16)
        return jnp.dot(probs, stored, preferred_element_type=jnp.float32)

    def pair(index, carry):
        base = pl.multiple_of(index * 2 * STEP_COUNT, 2 * STEP_COUNT)
        block = queries[pl.ds(base, 2 * STEP_COUNT), :].astype(jnp.float32)
        mixed = []
        for k in range(2):
            part = block[k * STEP_COUNT : (k + 1) * STEP_COUNT]
            query = jnp.concatenate(
                [part[:, h * HEAD_WIDTH : (h + 1) * HEAD_WIDTH] for h in range(GROUP)], axis=0
            ).astype(jnp.bfloat16)
            mixed.append(one(index * 2 + k, query))
        for h in range(GROUP):
            both = jnp.concatenate(
                [m[h * STEP_COUNT : (h + 1) * STEP_COUNT] for m in mixed], axis=0
            )
            outf[pl.ds(base, 2 * STEP_COUNT), h * HEAD_WIDTH : (h + 1) * HEAD_WIDTH] = both
        return carry

    lax.fori_loop(0, requests // 2, pair, 0)
    out[...] = outf[...].astype(out.dtype)


def attend(table, lengths, queries, fresh, pages, inbox):
    tokens, width = queries.shape
    hbm = pl.BlockSpec(memory_space=pltpu.HBM)
    vmem = pl.BlockSpec(memory_space=pltpu.VMEM)
    smem = pl.BlockSpec(memory_space=pltpu.SMEM)
    return pl.pallas_call(
        attend_kernel,
        out_shape=jax.ShapeDtypeStruct((tokens, width), queries.dtype),
        in_specs=[smem, smem, vmem, vmem, hbm, hbm],
        out_specs=vmem,
        scratch_shapes=[
            pltpu.VMEM((pages.shape[0] + inbox.shape[0], HEAD_WIDTH), pages.dtype),
            pltpu.VMEM((tokens, width), jnp.float32),
            pltpu.SemaphoreType.DMA((2,)),
        ],
        compiler_params=pltpu.CompilerParams(vmem_limit_bytes=32 * 1024 * 1024),
        name="attend",
    )(table, lengths, queries, fresh, pages, inbox)


def project_kernel(
    mixed, weights, slots, up, out,
    everyone, part, lowpart, sendbuf, recvbuf, lowsend, lowrecv, sumsend, sumrecv, lowfull, extra,
    own_sem, s1_sent, s1_got, s2_sent, s2_got, relay_sent, relay_got, mate_sent, mate_got,
    main_sent, main_got, low_sent, low_got, sum_sent, sum_got,
):
    me = lax.axis_index("req")
    lane = lax.axis_index("tp")
    planes = 8
    core = lax.rem(me, 2)
    cx, cy = me // 8, lax.rem(me // 2, 4)
    first = cx * (1 - core) + cy * core
    second = cy * (1 - core) + cx * core
    chunk_rows = mixed.shape[0]
    half = chunk_rows // 2
    columns = out.shape[1]
    above, below = lax.rem(lane + 1, planes), lax.rem(lane + planes - 1, planes)
    mate = me + 1 - 2 * core

    def spot(f, s, c):
        f, s = lax.rem(f + 8, 4), lax.rem(s + 8, 4)
        return f * (8 - 6 * c) + s * (2 + 6 * c) + c

    def at(df, ds):
        return spot(first + df, second + ds, core)

    def mate_at(df, ds):
        return spot(second + df, first + ds, 1 - core)

    barrier = pltpu.get_barrier_semaphore()
    for d in range(1, 4):
        pl.semaphore_signal(barrier, inc=1, device_id={"req": at(d, 0)})
        pl.semaphore_signal(barrier, inc=1, device_id={"req": at(0, d)})
    pl.semaphore_signal(barrier, inc=1, device_id={"req": mate})
    pl.semaphore_signal(barrier, inc=1, device_id={"tp": above})
    pl.semaphore_signal(barrier, inc=1, device_id={"tp": below})
    pl.semaphore_wait(barrier, 9)

    def remote(src, dst, sent, got, **to):
        return pltpu.make_async_remote_copy(src, dst, sent, got, device_id=to)

    HALVES = (pl.ds(0, half), pl.ds(half, half))

    def offset(k):
        return k + (k // 2) * (5 - 2 * k)

    def step_one(way, src_owner, src):
        return remote(
            src,
            everyone.at[src_owner],
            s1_sent.at[way],
            s1_got.at[way],
            req=at(1 if way == 0 else -1, 0),
        )

    def step_one_half(way):
        owner = at(-1 if way == 0 else 1, 0)
        ref = everyone.at[owner, HALVES[way]]
        return remote(
            ref, ref, s1_sent.at[2 + way], s1_got.at[2 + way], req=at(1 if way == 0 else -1, 0)
        )

    def step_two(k, way, src=None):
        owner = at(offset(k), 0)
        ref = everyone.at[owner]
        return remote(
            ref if src is None else src,
            ref,
            s2_sent.at[k, way],
            s2_got.at[k, way],
            req=at(0, 1 if way == 0 else -1),
        )

    def relay(k, way):
        owner = at(offset(k), -1 if way == 0 else 1)
        ref = everyone.at[owner, HALVES[way]]
        return remote(
            ref, ref, relay_sent.at[k, way], relay_got.at[k, way], req=at(0, 1 if way == 0 else -1)
        )

    DS = (0, -1, 1, 2)

    def to_mate(k, j, src=None):
        ref = everyone.at[at(offset(k), DS[j])]
        return remote(
            ref if src is None else src, ref, mate_sent.at[j, k], mate_got.at[j, k], req=mate
        )

    def arrived(ref, sem):
        pltpu.make_async_copy(ref, ref, sem).wait()

    def got_mate(k, j):
        arrived(everyone.at[mate_at(offset(k), DS[j])], mate_got.at[j, k])

    row = lax.broadcasted_iota(jnp.int32, (chunk_rows, HEAD_WIDTH), 0)
    col = lax.broadcasted_iota(jnp.int32, (chunk_rows, HEAD_WIDTH), 1)
    diagonal = row == col
    narrow = lax.broadcasted_iota(jnp.int32, (half, HEAD_WIDTH), 1) < half
    upper = col // half

    def slot_column(r):
        values = jnp.where(diagonal, slots[r].astype(jnp.float32), 0.0)
        return jnp.sum(values, axis=1, keepdims=True).astype(jnp.int32)

    def batch(owners):
        rows = jnp.concatenate([everyone[r] for r in owners], axis=0)
        product = jnp.dot(rows, weights[...], preferred_element_type=jnp.float32)
        for i, r in enumerate(owners):
            block = product[i * chunk_rows : (i + 1) * chunk_rows]
            part[r] = block[:, :columns]
            low = jnp.where(slot_column(r) == 2 * me + upper, block[:, columns:], 0.0)
            low = low + pltpu.roll(low, half, 1)
            lowpart[r] = jnp.where(narrow, low[:half], low[half:])

    own = pltpu.make_async_copy(mixed, everyone.at[me], own_sem)
    own.start()
    step_one(0, me, mixed).start()
    step_one(1, me, mixed).start()
    step_two(0, 0, mixed).start()
    step_two(0, 1, mixed).start()
    to_mate(0, 0, mixed).start()

    def pass_on(k):
        step_two(k, 0).start()
        step_two(k, 1).start()
        to_mate(k, 0).start()

    arrived(everyone.at[at(-1, 0)], s1_got.at[0])
    step_one_half(0).start()
    pass_on(2)
    arrived(everyone.at[at(1, 0)], s1_got.at[1])
    step_one_half(1).start()
    pass_on(1)

    def turn(k):
        arrived(everyone.at[at(offset(k), -1)], s2_got.at[k, 0])
        relay(k, 0).start()
        to_mate(k, 1).start()
        arrived(everyone.at[at(offset(k), 1)], s2_got.at[k, 1])
        relay(k, 1).start()
        to_mate(k, 2).start()

    turn(0)
    for way in range(2):
        arrived(everyone.at[at(2, 0), HALVES[way]], s1_got.at[2 + way])
    pass_on(3)
    own.wait()

    def batch_one(b, carry):
        for k in range(2):
            got_mate(2 * b + k, 0)
        batch(
            [at(offset(2 * b + k), 0) for k in range(2)]
            + [mate_at(offset(2 * b + k), 0) for k in range(2)]
        )
        return carry

    lax.fori_loop(0, 2, batch_one, 0)

    def batch_two(k):
        got_mate(k, 1)
        got_mate(k, 2)
        o = offset(k)
        batch([at(o, -1), at(o, 1), mate_at(o, -1), mate_at(o, 1)])

    def around(k, carry):
        turn(k)
        batch_two(k - 1)
        return carry

    lax.fori_loop(1, 4, around, 0)

    def last(k):
        for way in range(2):
            arrived(everyone.at[at(offset(k), 2), HALVES[way]], relay_got.at[k, way])
        to_mate(k, 3).start()

    last(0)
    last(1)
    batch_two(3)
    last(2)
    last(3)

    def batch_three(b, carry):
        for k in range(2):
            got_mate(2 * b + k, 3)
        batch(
            [at(offset(2 * b + k), 2) for k in range(2)]
            + [mate_at(offset(2 * b + k), 2) for k in range(2)]
        )
        return carry

    lax.fori_loop(0, 2, batch_three, 0)

    hops = planes // 2
    subs = planes // 2

    def target(way, step):
        return lax.rem(lane + planes + (step - hops if way == 0 else hops - step), planes)

    def low_copy(way, step):
        peer = below if way == 0 else above
        src, dst = lowsend.at[way, step], lowrecv.at[way, step]
        if step == 0:
            part_of = pl.ds(way * (subs // 2), subs // 2)
            src, dst = lowsend.at[way, step, part_of], lowrecv.at[way, step, part_of]
        return remote(src, dst, low_sent.at[way, step], low_got.at[way, step], tp=peer)

    def low_step(step):
        for way in range(2):
            if step:
                low_copy(way, step - 1).wait_recv()
            q = target(way, step)
            for sub in range(subs):
                fresh_half = sub // (subs // 2) == way
                if step == 0 and not fresh_half:
                    continue
                value = lowpart[q * subs + sub]
                if step > 1 or (step == 1 and fresh_half):
                    value = value + lowrecv[way, step - 1, sub].astype(jnp.float32)
                lowsend[way, step, sub] = value.astype(jnp.bfloat16)
            low_copy(way, step).start()

    def main_copy(way, step, sub):
        peer = below if way == 0 else above
        src, dst = sendbuf.at[way, step, sub], recvbuf.at[way, step, sub]
        if step == 0:
            side = pl.ds(way * (columns // 2), columns // 2)
            src, dst = sendbuf.at[way, step, sub, :, side], recvbuf.at[way, step, sub, :, side]
        return remote(src, dst, main_sent.at[way, step, sub], main_got.at[way, step, sub], tp=peer)

    def main_step(step, sub):
        for way in range(2):
            q = target(way, step)
            side = slice(way * (columns // 2), (way + 1) * (columns // 2))
            if step == 0:
                sendbuf[way, step, sub, :, side] = part[q * subs + sub, :, side].astype(jnp.bfloat16)
            else:
                main_copy(way, step - 1, sub).wait_recv()
                value = part[q * subs + sub]
                if step == 1:
                    came = recvbuf[way, 0, sub, :, side].astype(jnp.float32)
                    other = slice((1 - way) * (columns // 2), (2 - way) * (columns // 2))
                    sendbuf[way, 1, sub, :, side] = (value[:, side] + came).astype(jnp.bfloat16)
                    sendbuf[way, 1, sub, :, other] = value[:, other].astype(jnp.bfloat16)
                else:
                    came = recvbuf[way, step - 1, sub].astype(jnp.float32)
                    sendbuf[way, step, sub] = (value + came).astype(jnp.bfloat16)
            main_copy(way, step, sub).start()

    def sum_mate():
        return remote(
            sumsend.at[0, 1 - core], sumrecv.at[0], sum_sent.at[0], sum_got.at[0], req=mate
        )

    def sum_axis(axis, d):
        peer = at(d, 0) if axis == 0 else at(0, d)
        i = 1 + 3 * axis + d - 1
        return remote(
            sumsend.at[1 + axis, 0], sumrecv.at[i], sum_sent.at[i], sum_got.at[i], req=peer
        )

    def sum_back():
        return remote(
            lowfull.at[core], lowfull.at[core], sum_sent.at[7], sum_got.at[7], req=mate
        )

    def low_end():
        for way in range(2):
            low_copy(way, hops - 1).wait_recv()
        for sub in range(subs):
            value = lowpart[lane * subs + sub]
            for way in range(2):
                value = value + lowrecv[way, hops - 1, sub].astype(jnp.float32)
            sumsend[0, sub // 2, pl.ds(half * (sub % 2), half)] = value.astype(jnp.bfloat16)
        sum_mate().start()

    def sum_first():
        sum_mate().wait_recv()
        value = sumsend[0, core].astype(jnp.float32) + sumrecv[0].astype(jnp.float32)
        sumsend[1, 0] = value.astype(jnp.bfloat16)
        for d in range(1, 4):
            sum_axis(0, d).start()

    def gathered(axis):
        value = sumsend[1 + axis, 0].astype(jnp.float32)
        for d in range(1, 4):
            sum_axis(axis, d).wait_recv()
            value = value + sumrecv[1 + 3 * axis + d - 1].astype(jnp.float32)
        return value.astype(jnp.bfloat16)

    def sum_second():
        sumsend[2, 0] = gathered(0)
        for d in range(1, 4):
            sum_axis(1, d).start()

    def sum_third():
        lowfull[core] = gathered(1)
        sum_back().start()

    def lora():
        arrived(lowfull.at[1 - core], sum_got.at[7])
        pieces, owners = [], []
        for sub in range(subs):
            packed = lowfull[sub // 2, pl.ds(half * (sub % 2), half)].astype(jnp.float32)
            turned = pltpu.roll(packed, half, 1)
            pieces.append(
                jnp.concatenate(
                    [jnp.where(narrow, packed, turned), jnp.where(narrow, turned, packed)], axis=0
                )
            )
            owners.append(slot_column(lane * subs + sub))
        low = jnp.concatenate(pieces, axis=0)
        owner = jnp.concatenate(owners, axis=0)
        side = lax.broadcasted_iota(jnp.int32, low.shape, 1) // half
        group = 8
        extra[...] = jnp.zeros(extra.shape, jnp.float32)

        def add(g, carry):
            wide = jnp.concatenate(
                [
                    jnp.where(owner == 2 * (g * group + m) + side, low, 0.0).astype(jnp.bfloat16)
                    for m in range(group)
                ],
                axis=1,
            )
            rows = group * HEAD_WIDTH
            block = up[pl.ds(pl.multiple_of(g * rows, rows), rows), :]
            extra[...] += jnp.dot(wide, block, preferred_element_type=jnp.float32)
            return carry

        lax.fori_loop(0, up.shape[0] // (group * HEAD_WIDTH), add, 0)

    low_step(0)
    for sub in range(subs):
        main_step(0, sub)
    low_step(1)
    main_step(1, 0)
    main_step(1, 1)
    low_step(2)
    main_step(1, 2)
    main_step(1, 3)
    low_step(3)
    main_step(2, 0)
    main_step(2, 1)
    low_end()
    main_step(2, 2)
    main_step(2, 3)
    sum_first()
    main_step(3, 0)
    main_step(3, 1)
    sum_second()
    main_step(3, 2)
    main_step(3, 3)
    sum_third()
    lora()
    for sub in range(subs):
        rows = pl.ds(sub * chunk_rows, chunk_rows)
        value = part[lane * subs + sub] + extra[rows, :]
        for way in range(2):
            main_copy(way, hops - 1, sub).wait_recv()
            value = value + recvbuf[way, hops - 1, sub].astype(jnp.float32)
        out[rows, :] = value.astype(out.dtype)

    for way in range(2):
        step_one(way, me, mixed).wait_send()
        step_one_half(way).wait_send()
        for k in range(4):
            step_two(k, way).wait_send()
            relay(k, way).wait_send()
        for step in range(hops):
            low_copy(way, step).wait_send()
            for sub in range(subs):
                main_copy(way, step, sub).wait_send()
    for k in range(4):
        for j in range(4):
            to_mate(k, j).wait_send()
    sum_mate().wait_send()
    for axis in range(2):
        for d in range(1, 4):
            sum_axis(axis, d).wait_send()
    sum_back().wait_send()


def project(mixed, weights, slots, up):
    rows, depth = mixed.shape
    n, columns, planes = slots.shape[0], up.shape[1], 8
    vmem = pl.BlockSpec(memory_space=pltpu.VMEM)
    dma = pltpu.SemaphoreType.DMA
    bf16, f32 = jnp.bfloat16, jnp.float32
    hops, subs, half = planes // 2, planes // 2, rows // 2
    return pl.pallas_call(
        project_kernel,
        out_shape=jax.ShapeDtypeStruct((n * rows // planes, columns), bf16),
        in_specs=[vmem] * 4,
        out_specs=vmem,
        scratch_shapes=[
            pltpu.VMEM((n, rows, depth), bf16),
            pltpu.VMEM((n, rows, columns), f32),
            pltpu.VMEM((n, half, HEAD_WIDTH), f32),
            pltpu.VMEM((2, hops, subs, rows, columns), bf16),
            pltpu.VMEM((2, hops, subs, rows, columns), bf16),
            pltpu.VMEM((2, hops, subs, half, HEAD_WIDTH), bf16),
            pltpu.VMEM((2, hops, subs, half, HEAD_WIDTH), bf16),
            pltpu.VMEM((3, 2, rows, HEAD_WIDTH), bf16),
            pltpu.VMEM((7, rows, HEAD_WIDTH), bf16),
            pltpu.VMEM((2, rows, HEAD_WIDTH), bf16),
            pltpu.VMEM((n * rows // planes, columns), f32),
            dma,
            dma((4,)), dma((4,)),
            dma((4, 2)), dma((4, 2)),
            dma((4, 2)), dma((4, 2)),
            dma((4, 4)), dma((4, 4)),
            dma((2, hops, subs)), dma((2, hops, subs)),
            dma((2, hops)), dma((2, hops)),
            dma((8,)), dma((8,)),
        ],
        compiler_params=pltpu.CompilerParams(
            collective_id=1, has_side_effects=True, vmem_limit_bytes=VMEM_BYTES
        ),
        name="project",
    )(mixed, weights, slots, up)


def on_device(
    queries,
    incoming_key_value,
    key_value_pages,
    page_request_home,
    lengths,
    request_adapter_index,
    adapter_storage_slot,
    adapter_down_factor,
    adapter_up_factor,
    output_projection_weight,
):
    n = lax.axis_size("req")
    tp_count = lax.axis_size("tp")
    me = lax.axis_index("req")
    per_dev = key_value_pages.shape[0]
    requests = lengths.shape[0]
    total = n * per_dev
    pages = key_value_pages.reshape(per_dev * PAGE_ROWS, HEAD_WIDTH)

    numbers = jnp.arange(per_dev, dtype=jnp.int32)
    peers = jnp.arange(n, dtype=jnp.int32)
    owner = page_request_home // per_dev
    match = (owner[:, None] == peers[None, :]) & (owner != me)[:, None]
    key = (numbers * total + page_request_home)[:, None]
    low_key = jnp.min(jnp.where(match, key, jnp.int32(2**30)), axis=0)
    high_key = jnp.max(jnp.where(match, key, -1), axis=0)
    keys = jnp.stack([low_key, high_key], axis=1)
    there = jnp.stack([high_key >= 0, high_key > low_key], axis=1)
    out_source = jnp.where(there, keys // total, 0).reshape(-1)
    out_label = jnp.where(there, keys % total, -1)

    slot_count = adapter_storage_slot.shape[0]
    slots = jnp.arange(slot_count, dtype=jnp.int32)
    own_slot = jnp.sum(
        jnp.where(
            request_adapter_index[:, None] == slots[None, :], adapter_storage_slot[None, :], 0
        ),
        axis=1,
    )
    labels = jnp.concatenate(
        [
            out_label,
            jnp.zeros((n, 64 - CAP), jnp.int32),
            jnp.broadcast_to(own_slot[None, :], (n, requests)),
            jnp.zeros((n, 64 - requests), jnp.int32),
        ],
        axis=1,
    ).reshape(n, 1, 128)

    outbox = pick(out_source, pages)
    up = adapter_up_factor.reshape(-1, adapter_up_factor.shape[2])
    inbox, inlab, upall = exchange(outbox, labels, up, n, tp_count)

    mine = (peers == me)[:, None]
    arrived = jnp.where(mine, -1, inlab[:, 0, :CAP]).reshape(-1)
    own_label = jnp.where(owner == me, page_request_home - me * per_dev, -1)
    in_label = jnp.where(arrived >= 0, arrived - me * per_dev, -1)
    candidate = jnp.concatenate([own_label, in_label], axis=0)
    candidate_numbers = jnp.arange(candidate.shape[0], dtype=jnp.int32)
    table = jnp.sum(
        jnp.where(candidate[:, None] == numbers[None, :], candidate_numbers[:, None], 0), axis=0
    )
    req_slot = jnp.where(mine, own_slot[None, :], inlab[:, 0, 64 : 64 + requests]).reshape(-1)
    token_slot = jnp.repeat(req_slot, STEP_COUNT)

    fresh = jnp.transpose(incoming_key_value, (1, 0, 2)).reshape(
        requests, 2 * STEP_COUNT, HEAD_WIDTH
    )
    fresh = jnp.pad(fresh, ((0, 0), (0, 8), (0, 0)))
    mixed = attend(table, lengths, queries, fresh, pages, inbox)

    own_adapters, _, rank = adapter_down_factor.shape
    down = jnp.transpose(adapter_down_factor, (1, 0, 2)).reshape(-1, own_adapters * rank)
    weights = jnp.concatenate([output_projection_weight, down], axis=1)
    return project(
        mixed,
        weights,
        token_slot.reshape(n, 1, requests * STEP_COUNT),
        upall.reshape(slot_count * rank, output_projection_weight.shape[1]),
    )


def solution(mesh):
    return jax.shard_map(
        on_device,
        mesh=mesh,
        in_specs=(
            P("req", "tp"),
            P(None, "req", "tp"),
            P("req", None, None, "tp"),
            P("req"),
            P("req"),
            P("req"),
            P(),
            P("req", "tp", None),
            P("req", None, None),
            P("tp", "req"),
        ),
        out_specs=P("tp", "req"),
        check_vma=False,
    )
```

```python
import functools
import math

import jax
import jax.numpy as jnp
from jax import lax
from jax.experimental import pallas as pl
from jax.experimental.pallas import tpu as pltpu
from jax.sharding import PartitionSpec as P

QUERY_HEADS = 64
KEY_VALUE_HEADS = 8
GROUP = QUERY_HEADS // KEY_VALUE_HEADS
HEAD_WIDTH = 128
STEP_COUNT = 4
PAGE_LENGTH = 32
PAGE_ROWS = 2 * PAGE_LENGTH
MAXP = 16
CAP = 2
VMEM_BYTES = 60 * 1024 * 1024


def pick_kernel(source, pages, outbox, sem):
    count = outbox.shape[0]
    for k in range(count):
        pltpu.make_async_copy(pages.at[source[k]], outbox.at[k], sem).start()
    pltpu.make_async_copy(pages.at[pl.ds(0, count)], outbox, sem).wait()


def pick(out_source, pages):
    shape = (out_source.shape[0],) + pages.shape[1:]
    return pl.pallas_call(
        pick_kernel,
        out_shape=jax.ShapeDtypeStruct(shape, pages.dtype),
        grid_spec=pltpu.PrefetchScalarGridSpec(
            num_scalar_prefetch=1,
            grid=(1,),
            in_specs=[pl.BlockSpec(memory_space=pl.ANY)],
            out_specs=pl.BlockSpec(shape, lambda i, s: (0, 0, 0)),
            scratch_shapes=[pltpu.SemaphoreType.DMA],
        ),
        name="pick",
    )(out_source, pages)


HALF_COUNT = 2


def layer_kernel(
    outbox, labels, local_table, lengths, queries, fresh, pages, up, weights, down,
    out,
    cands, inlab, tablev, table, outf, mixed, upall, everyone, part, lowpart,
    sendbuf, recvbuf, lowsend, lowrecv, sumsend, sumrecv, lowfull, extra,
    sent, got, lab_sent, lab_got, up_sent, up_got, ring_sent, ring_got, local_sem,
    s1_sent, s1_got, s2_sent, s2_got, relay_sent, relay_got, mate_sent, mate_got,
    main_sent, main_got, low_sent, low_got, sum_sent, sum_got,
):
    n, planes = upall.shape[0], upall.shape[1]
    me = lax.axis_index("req")
    lane = lax.axis_index("tp")
    core = lax.rem(me, 2)
    cx, cy = me // 8, lax.rem(me // 2, 4)
    first = cx * (1 - core) + cy * core
    second = cy * (1 - core) + cx * core
    above, below = lax.rem(lane + 1, planes), lax.rem(lane + planes - 1, planes)
    mate = me + 1 - 2 * core
    page_count = pages.shape[0]
    requests = fresh.shape[0]
    columns = out.shape[1]
    chunk_rows = queries.shape[0]
    half = chunk_rows // HALF_COUNT
    quarter = half // 2
    rank = HEAD_WIDTH // 2

    load = pltpu.make_async_copy(pages, cands.at[pl.ds(0, page_count)], local_sem.at[0])
    load.start()
    barrier = pltpu.get_barrier_semaphore()

    def greet(d, carry):
        pl.semaphore_signal(barrier, inc=1, device_id={"req": lax.rem(me + d, n)})
        return carry

    lax.fori_loop(1, n, greet, 0)
    pl.semaphore_signal(barrier, inc=1, device_id={"tp": above})
    pl.semaphore_signal(barrier, inc=1, device_id={"tp": below})
    inlab[me] = labels[me]
    pl.semaphore_wait(barrier, n + 1)

    def remote(src, dst, sent_sem, got_sem, **to):
        return pltpu.make_async_remote_copy(src, dst, sent_sem, got_sem, device_id=to)

    up_rows = upall.shape[2]

    def up_part(peer):
        return up.at[
            pl.ds(pl.multiple_of(lane * up_rows, up_rows), up_rows),
            pl.ds(pl.multiple_of(peer * columns, columns), columns),
        ]

    def label_copy(d):
        peer = lax.rem(me + d, n)
        return remote(
            labels.at[peer], inlab.at[me], lab_sent.at[d - 1], lab_got.at[d - 1], req=peer
        )

    def up_copy(d):
        peer = lax.rem(me + d, n)
        return remote(
            up_part(peer), upall.at[me, lane], up_sent.at[d - 1], up_got.at[d - 1], req=peer
        )

    def page_copy(d):
        peer = lax.rem(me + d, n)
        return remote(
            outbox.at[pl.ds(peer * CAP, CAP)],
            cands.at[pl.ds(page_count + me * CAP, CAP)],
            sent.at[d - 1],
            got.at[d - 1],
            req=peer,
        )

    own_up = pltpu.make_async_copy(up_part(me), upall.at[me, lane], local_sem.at[1])
    own_up.start()

    def begin_up(d, carry):
        label_copy(d).start()
        up_copy(d).start()
        return carry

    def begin_pages(d, carry):
        page_copy(d).start()
        return carry

    def finish_up(d, carry):
        up_copy(d).wait()
        return carry

    def finish_labels(d, carry):
        label_copy(d).wait()
        return carry

    def finish_pages(d, carry):
        page_copy(d).wait()
        return carry

    lax.fori_loop(1, n, begin_up, 0)
    lax.fori_loop(1, n, begin_pages, 0)

    hops = planes // 2

    def ring_copy(way, hop):
        peer = above if way == 0 else below
        origin = lax.rem(lane + planes + (hop if way == 1 else -hop), planes)
        piece = upall.at[:, origin]
        if hop == hops - 1:
            piece = upall.at[pl.ds(way * (n // 2), n // 2), origin]
        return pltpu.make_async_remote_copy(
            piece, piece, ring_sent.at[way, hop], ring_got.at[way, hop], device_id={"tp": peer}
        )

    def ring(hop):
        for way in range(2):
            if hop:
                ring_copy(way, hop - 1).wait_recv()
            if hop < hops:
                ring_copy(way, hop).start()

    lax.fori_loop(1, n, finish_up, 0)
    own_up.wait()
    ring(0)

    lax.fori_loop(1, n, finish_labels, 0)
    place = (
        lax.broadcasted_iota(jnp.int32, tablev.shape, 0) * HEAD_WIDTH
        + lax.broadcasted_iota(jnp.int32, tablev.shape, 1)
        + me * page_count
        + 1
    )

    def enter(source, entries):
        word = lax.shift_right_logical(inlab[source], jnp.full((1, HEAD_WIDTH), 6, jnp.int32))
        for k in range(CAP):
            index = page_count + source * CAP + k
            entries = entries + jnp.where(place == word[:, k : k + 1], index, 0)
        return entries

    tablev[...] = lax.fori_loop(0, n, enter, local_table[...])
    to_scalar = pltpu.make_async_copy(tablev, table, local_sem.at[2])
    to_scalar.start()
    lax.fori_loop(1, n // 2, finish_pages, 0)
    ring(1)
    lax.fori_loop(n // 2, n, finish_pages, 0)
    to_scalar.wait()
    load.wait()
    ring(2)

    old = MAXP * PAGE_ROWS
    width = old + HEAD_WIDTH
    rows_q = GROUP * STEP_COUNT
    column = lax.broadcasted_iota(jnp.int32, (rows_q, width), 1)
    step_of = lax.rem(lax.broadcasted_iota(jnp.int32, (rows_q, width), 0), STEP_COUNT)
    is_key = lax.rem(column, 2) == 0
    keep_new = is_key & (column >= old) & ((column - old) // 2 <= step_of)
    position = jnp.where(is_key & (column < old), column // 2, 1 << 20)
    scale = 1.0 / math.sqrt(HEAD_WIDTH)
    filler = jnp.zeros((HEAD_WIDTH - fresh.shape[1], HEAD_WIDTH), fresh.dtype)
    per_row = HEAD_WIDTH // MAXP

    def one(request, query):
        pieces = []
        for j in range(MAXP):
            page = table[request // per_row, lax.rem(request, per_row) * MAXP + j]
            pieces.append(cands[page])
        pieces.append(fresh[request])
        pieces.append(filler)
        stored = jnp.concatenate(pieces, axis=0)
        scores = (
            lax.dot_general(
                query, stored, (((1,), (1,)), ((), ())), preferred_element_type=jnp.float32
            )
            * scale
        )
        keep = keep_new | (position < lengths[request])
        scores = jnp.where(keep, scores, -jnp.inf)
        top = jnp.max(scores, axis=1, keepdims=True)
        exps = jnp.exp(scores - top)
        probs = exps / jnp.sum(exps, axis=1, keepdims=True)
        probs = pltpu.roll(probs, 1, 1).astype(jnp.bfloat16)
        return jnp.dot(probs, stored, preferred_element_type=jnp.float32)

    def pair(index, carry):
        base = pl.multiple_of(index * 2 * STEP_COUNT, 2 * STEP_COUNT)
        both_q = queries[pl.ds(base, 2 * STEP_COUNT), :].astype(jnp.float32)
        results = []
        for k in range(2):
            one_q = both_q[k * STEP_COUNT : (k + 1) * STEP_COUNT]
            query = jnp.concatenate(
                [one_q[:, h * HEAD_WIDTH : (h + 1) * HEAD_WIDTH] for h in range(GROUP)], axis=0
            ).astype(jnp.bfloat16)
            results.append(one(index * 2 + k, query))
        for h in range(GROUP):
            both = jnp.concatenate(
                [m[h * STEP_COUNT : (h + 1) * STEP_COUNT] for m in results], axis=0
            )
            outf[pl.ds(base, 2 * STEP_COUNT), h * HEAD_WIDTH : (h + 1) * HEAD_WIDTH] = both
        return carry

    def attend(start, stop):
        lax.fori_loop(start, stop, pair, 0)

    def spot(f, s, c):
        f, s = lax.rem(f + 8, 4), lax.rem(s + 8, 4)
        return f * (8 - 6 * c) + s * (2 + 6 * c) + c

    def at(df, ds):
        return spot(first + df, second + ds, core)

    def mate_at(df, ds):
        return spot(second + df, first + ds, 1 - core)

    OFFSET = (0, 1, -1, 2)
    DS = (0, -1, 1, 2)

    def whole(h):
        return pl.ds(h * half, half)

    def side_rows(h, way):
        return pl.ds(h * half + way * quarter, quarter)

    def step_one(h, way):
        to = at(1 if way == 0 else -1, 0)
        return remote(
            mixed.at[whole(h)], everyone.at[me, whole(h)],
            s1_sent.at[h, way], s1_got.at[h, way], req=to,
        )

    def step_one_half(h, way):
        ref = everyone.at[at(-1 if way == 0 else 1, 0), side_rows(h, way)]
        to = at(1 if way == 0 else -1, 0)
        return remote(ref, ref, s1_sent.at[h, 2 + way], s1_got.at[h, 2 + way], req=to)

    def step_two(h, k, way):
        ref = everyone.at[at(OFFSET[k], 0), whole(h)]
        src = mixed.at[whole(h)] if k == 0 else ref
        to = at(0, 1 if way == 0 else -1)
        return remote(src, ref, s2_sent.at[h, k, way], s2_got.at[h, k, way], req=to)

    def relay(h, k, way):
        ref = everyone.at[at(OFFSET[k], -1 if way == 0 else 1), side_rows(h, way)]
        to = at(0, 1 if way == 0 else -1)
        return remote(ref, ref, relay_sent.at[h, k, way], relay_got.at[h, k, way], req=to)

    def to_mate(h, k, j):
        ref = everyone.at[at(OFFSET[k], DS[j]), whole(h)]
        src = mixed.at[whole(h)] if k == 0 and j == 0 else ref
        return remote(src, ref, mate_sent.at[h, j, k], mate_got.at[h, j, k], req=mate)

    def arrived(ref, sem):
        pltpu.make_async_copy(ref, ref, sem).wait()

    def got_mate(h, k, j):
        arrived(everyone.at[mate_at(OFFSET[k], DS[j]), whole(h)], mate_got.at[h, j, k])

    def own_copy(h):
        return pltpu.make_async_copy(
            mixed.at[whole(h)], everyone.at[me, whole(h)], local_sem.at[3 + h]
        )

    def open_gather(h):
        rows = pl.ds(h * half, half)
        mixed[rows, :] = outf[rows, :].astype(mixed.dtype)
        for way in range(2):
            step_one(h, way).start()
        for way in range(2):
            step_two(h, 0, way).start()
        to_mate(h, 0, 0).start()
        own_copy(h).start()

    def pass_on(h, k):
        step_two(h, k, 0).start()
        step_two(h, k, 1).start()
        to_mate(h, k, 0).start()

    def near(h):
        for way, k in ((0, 2), (1, 1)):
            arrived(everyone.at[at(OFFSET[k], 0), whole(h)], s1_got.at[h, way])
            step_one_half(h, way).start()
            pass_on(h, k)

    def far(h):
        for way in range(2):
            arrived(everyone.at[at(2, 0), side_rows(h, way)], s1_got.at[h, 2 + way])
        pass_on(h, 3)

    def turn(h, k):
        for way, j in ((0, 1), (1, 2)):
            arrived(everyone.at[at(OFFSET[k], DS[j]), whole(h)], s2_got.at[h, k, way])
            relay(h, k, way).start()
            to_mate(h, k, j).start()

    def last(h, k):
        for way in range(2):
            arrived(everyone.at[at(OFFSET[k], 2), side_rows(h, way)], relay_got.at[h, k, way])
        to_mate(h, k, 3).start()

    row64 = lax.broadcasted_iota(jnp.int32, (half, HEAD_WIDTH), 0)
    col64 = lax.broadcasted_iota(jnp.int32, (half, HEAD_WIDTH), 1)
    narrow = lax.broadcasted_iota(jnp.int32, (quarter, HEAD_WIDTH), 1) < rank
    upper = col64 // rank

    def slot_column(r, h):
        values = (inlab[r] & 63).astype(jnp.float32)
        values = jnp.where(row64 + h * half == col64, values, 0.0)
        return jnp.sum(values, axis=1, keepdims=True).astype(jnp.int32)

    def batch(h, kjs):
        for k, j in kjs:
            got_mate(h, k, j)
        owners = [at(OFFSET[k], DS[j]) for k, j in kjs]
        owners += [mate_at(OFFSET[k], DS[j]) for k, j in kjs]
        rows = jnp.concatenate([everyone[r, whole(h)] for r in owners], axis=0)
        product = jnp.dot(rows, weights[...], preferred_element_type=jnp.float32)
        lows = jnp.dot(rows, down[...], preferred_element_type=jnp.float32)
        for i, r in enumerate(owners):
            cut = slice(i * half, (i + 1) * half)
            part[r, whole(h)] = product[cut]
            low = jnp.where(slot_column(r, h) == 2 * me + upper, lows[cut], 0.0)
            low = low + pltpu.roll(low, rank, 1)
            lowpart[r, h] = jnp.where(narrow, low[:quarter], low[quarter:])

    def batch_a(h):
        own_copy(h).wait()
        batch(h, [(k, 0) for k in range(4)])

    def batch_b(h, ks):
        batch(h, [(k, j) for k in ks for j in (1, 2)])

    def batch_c(h):
        batch(h, [(k, 3) for k in range(4)])

    subs = n // planes

    def target(way, step):
        return lax.rem(lane + planes + (step - hops if way == 0 else hops - step), planes)

    def low_copy(h, way, step):
        peer = below if way == 0 else above
        src, dst = lowsend.at[h, way, step], lowrecv.at[h, way, step]
        if step == 0:
            some = pl.ds(way * (subs // 2), subs // 2)
            src, dst = lowsend.at[h, way, step, some], lowrecv.at[h, way, step, some]
        return remote(src, dst, low_sent.at[h, way, step], low_got.at[h, way, step], tp=peer)

    def low_step(h, step):
        for way in range(2):
            if step:
                low_copy(h, way, step - 1).wait_recv()
            q = target(way, step)
            for sub in range(subs):
                mine = sub // (subs // 2) == way
                if step == 0 and not mine:
                    continue
                value = lowpart[q * subs + sub, h]
                if step > 1 or (step == 1 and mine):
                    value = value + lowrecv[h, way, step - 1, sub].astype(jnp.float32)
                lowsend[h, way, step, sub] = value.astype(jnp.bfloat16)
            low_copy(h, way, step).start()

    wing = columns // 2

    def main_copy(h, way, step, p):
        peer = below if way == 0 else above
        src, dst = sendbuf.at[h, way, step, p], recvbuf.at[h, way, step, p]
        if step == 0:
            side = pl.ds(way * wing, wing)
            src = sendbuf.at[h, way, step, p, :, :, side]
            dst = recvbuf.at[h, way, step, p, :, :, side]
        return remote(
            src, dst, main_sent.at[h, way, step, p], main_got.at[h, way, step, p], tp=peer
        )

    def main_step(h, step, p):
        for way in range(2):
            q = target(way, step)
            side = slice(way * wing, (way + 1) * wing)
            other = slice((1 - way) * wing, (2 - way) * wing)
            if step:
                main_copy(h, way, step - 1, p).wait_recv()
            for i in range(2):
                value = part[q * subs + 2 * p + i, whole(h)]
                if step == 0:
                    sendbuf[h, way, 0, p, i, :, side] = value[:, side].astype(jnp.bfloat16)
                elif step == 1:
                    came = recvbuf[h, way, 0, p, i, :, side].astype(jnp.float32)
                    sendbuf[h, way, 1, p, i, :, side] = (value[:, side] + came).astype(jnp.bfloat16)
                    sendbuf[h, way, 1, p, i, :, other] = value[:, other].astype(jnp.bfloat16)
                else:
                    came = recvbuf[h, way, step - 1, p, i].astype(jnp.float32)
                    sendbuf[h, way, step, p, i] = (value + came).astype(jnp.bfloat16)
            main_copy(h, way, step, p).start()

    def sum_mate():
        return remote(
            sumsend.at[0, 1 - core], sumrecv.at[0], sum_sent.at[0], sum_got.at[0], req=mate
        )

    def sum_axis(axis, d):
        peer = at(d, 0) if axis == 0 else at(0, d)
        i = 1 + 3 * axis + d - 1
        return remote(
            sumsend.at[1 + axis, 0], sumrecv.at[i], sum_sent.at[i], sum_got.at[i], req=peer
        )

    def sum_back():
        return remote(
            lowfull.at[core], lowfull.at[core], sum_sent.at[7], sum_got.at[7], req=mate
        )

    def low_end(h):
        for way in range(2):
            low_copy(h, way, hops - 1).wait_recv()
        for sub in range(subs):
            value = lowpart[lane * subs + sub, h]
            for way in range(2):
                value = value + lowrecv[h, way, hops - 1, sub].astype(jnp.float32)
            sumsend[0, h, pl.ds(quarter * sub, quarter)] = value.astype(jnp.bfloat16)

    def sum_first():
        sum_mate().wait_recv()
        value = sumsend[0, core].astype(jnp.float32) + sumrecv[0].astype(jnp.float32)
        sumsend[1, 0] = value.astype(jnp.bfloat16)
        for d in range(1, 4):
            sum_axis(0, d).start()

    def gathered(axis):
        value = sumsend[1 + axis, 0].astype(jnp.float32)
        for d in range(1, 4):
            sum_axis(axis, d).wait_recv()
            value = value + sumrecv[1 + 3 * axis + d - 1].astype(jnp.float32)
        return value.astype(jnp.bfloat16)

    def sum_second():
        sumsend[2, 0] = gathered(0)
        for d in range(1, 4):
            sum_axis(1, d).start()

    def sum_third():
        lowfull[core] = gathered(1)
        sum_back().start()

    def lora():
        arrived(lowfull.at[1 - core], sum_got.at[7])
        pieces, owners = [], []
        for sub in range(subs):
            for h in range(HALF_COUNT):
                packed = lowfull[h, pl.ds(quarter * sub, quarter)].astype(jnp.float32)
                turned = pltpu.roll(packed, rank, 1)
                pieces += [jnp.where(narrow, packed, turned), jnp.where(narrow, turned, packed)]
                owners.append(slot_column(lane * subs + sub, h))
        low = jnp.concatenate(pieces, axis=0)
        owner = jnp.concatenate(owners, axis=0)
        side = lax.broadcasted_iota(jnp.int32, low.shape, 1) // rank
        group = 8
        extra[...] = jnp.zeros(extra.shape, jnp.float32)

        def add(g, carry):
            wide = jnp.concatenate(
                [
                    jnp.where(owner == 2 * (g * group + m) + side, low, 0.0).astype(jnp.bfloat16)
                    for m in range(group)
                ],
                axis=1,
            )
            stored = upall[pl.ds(g * group, group)].reshape(group * planes * up_rows, columns)
            extra[...] += jnp.dot(wide, stored, preferred_element_type=jnp.float32)
            return carry

        lax.fori_loop(0, n // group, add, 0)

    pairs = requests // 2
    attend(0, pairs // 4)
    ring(3)
    attend(pairs // 4, pairs // 2)
    open_gather(0)
    attend(pairs // 2, pairs // 2 + 2)
    near(0)
    attend(pairs // 2 + 2, pairs // 2 + 4)
    turn(0, 0)
    far(0)
    attend(pairs // 2 + 4, pairs // 2 + 6)
    turn(0, 1)
    turn(0, 2)
    attend(pairs // 2 + 6, pairs)
    ring(4)
    open_gather(1)
    turn(0, 3)
    last(0, 0)
    batch_a(0)
    last(0, 1)
    near(1)
    batch_b(0, (0, 1))
    last(0, 2)
    last(0, 3)
    turn(1, 0)
    far(1)
    batch_b(0, (2, 3))
    turn(1, 1)
    batch_c(0)
    low_step(0, 0)
    main_step(0, 0, 0)
    main_step(0, 0, 1)
    turn(1, 2)
    low_step(0, 1)
    main_step(0, 1, 0)
    main_step(0, 1, 1)
    turn(1, 3)
    last(1, 0)
    batch_a(1)
    low_step(0, 2)
    main_step(0, 2, 0)
    last(1, 1)
    batch_b(1, (0, 1))
    main_step(0, 2, 1)
    low_step(0, 3)
    last(1, 2)
    last(1, 3)
    batch_b(1, (2, 3))
    main_step(0, 3, 0)
    main_step(0, 3, 1)
    batch_c(1)
    low_step(1, 0)
    low_end(0)
    main_step(1, 0, 0)
    main_step(1, 0, 1)
    low_step(1, 1)
    main_step(1, 1, 0)
    low_step(1, 2)
    main_step(1, 1, 1)
    low_step(1, 3)
    main_step(1, 2, 0)
    low_end(1)
    sum_mate().start()
    main_step(1, 2, 1)
    sum_first()
    main_step(1, 3, 0)
    sum_second()
    main_step(1, 3, 1)
    sum_third()
    lora()
    for h in range(HALF_COUNT):
        for sub in range(subs):
            p, i = sub // 2, sub % 2
            rows = pl.ds(sub * chunk_rows + h * half, half)
            value = part[lane * subs + sub, whole(h)] + extra[rows, :]
            for way in range(2):
                if i == 0:
                    main_copy(h, way, hops - 1, p).wait_recv()
                value = value + recvbuf[h, way, hops - 1, p, i].astype(jnp.float32)
            out[rows, :] = value.astype(out.dtype)

    for way in range(2):
        for hop in range(hops):
            ring_copy(way, hop).wait_send()
    for h in range(HALF_COUNT):
        for way in range(2):
            step_one(h, way).wait_send()
            step_one_half(h, way).wait_send()
            for k in range(4):
                step_two(h, k, way).wait_send()
                relay(h, k, way).wait_send()
            for step in range(hops):
                low_copy(h, way, step).wait_send()
                for p in range(2):
                    main_copy(h, way, step, p).wait_send()
        for k in range(4):
            for j in range(4):
                to_mate(h, k, j).wait_send()
    sum_mate().wait_send()
    for axis in range(2):
        for d in range(1, 4):
            sum_axis(axis, d).wait_send()
    sum_back().wait_send()


def layer(outbox, labels, local_table, lengths, queries, fresh, pages, up, weights, down, planes):
    rows, depth = queries.shape
    n, columns = labels.shape[0], weights.shape[1]
    hops, subs, half = planes // 2, n // planes, rows // HALF_COUNT
    hbm = pl.BlockSpec(memory_space=pltpu.HBM)
    vmem = pl.BlockSpec(memory_space=pltpu.VMEM)
    smem = pl.BlockSpec(memory_space=pltpu.SMEM)
    dma = pltpu.SemaphoreType.DMA
    bf16, f32, i32 = jnp.bfloat16, jnp.float32, jnp.int32
    hc = HALF_COUNT
    return pl.pallas_call(
        layer_kernel,
        out_shape=jax.ShapeDtypeStruct((n * rows // planes, columns), bf16),
        in_specs=[hbm, vmem, vmem, smem, vmem, vmem, hbm, hbm, vmem, vmem],
        out_specs=vmem,
        scratch_shapes=[
            pltpu.VMEM((pages.shape[0] + outbox.shape[0], PAGE_ROWS, HEAD_WIDTH), bf16),
            pltpu.VMEM(labels.shape, i32),
            pltpu.VMEM(local_table.shape, i32),
            pltpu.SMEM(local_table.shape, i32),
            pltpu.VMEM((rows, depth), f32),
            pltpu.VMEM((rows, depth), bf16),
            pltpu.VMEM((n, planes, up.shape[0] // planes, columns), bf16),
            pltpu.VMEM((n, rows, depth), bf16),
            pltpu.VMEM((n, rows, columns), f32),
            pltpu.VMEM((n, hc, half // 2, HEAD_WIDTH), f32),
            pltpu.VMEM((hc, 2, hops, 2, subs // 2, half, columns), bf16),
            pltpu.VMEM((hc, 2, hops, 2, subs // 2, half, columns), bf16),
            pltpu.VMEM((hc, 2, hops, subs, half // 2, HEAD_WIDTH), bf16),
            pltpu.VMEM((hc, 2, hops, subs, half // 2, HEAD_WIDTH), bf16),
            pltpu.VMEM((3, 2, rows, HEAD_WIDTH), bf16),
            pltpu.VMEM((7, rows, HEAD_WIDTH), bf16),
            pltpu.VMEM((2, rows, HEAD_WIDTH), bf16),
            pltpu.VMEM((n * rows // planes, columns), f32),
        ]
        + [dma((n - 1,))] * 6
        + [dma((2, hops))] * 2
        + [dma((5,))]
        + [dma((hc, 4))] * 2
        + [dma((hc, 4, 2))] * 4
        + [dma((hc, 4, 4))] * 2
        + [dma((hc, 2, hops, 2))] * 2
        + [dma((hc, 2, hops))] * 2
        + [dma((8,))] * 2,
        compiler_params=pltpu.CompilerParams(
            collective_id=0, has_side_effects=True, vmem_limit_bytes=VMEM_BYTES
        ),
        name="layer",
    )(outbox, labels, local_table, lengths, queries, fresh, pages, up, weights, down)


def on_device(
    queries,
    incoming_key_value,
    key_value_pages,
    page_request_home,
    lengths,
    request_adapter_index,
    adapter_storage_slot,
    adapter_down_factor,
    adapter_up_factor,
    output_projection_weight,
):
    n = lax.axis_size("req")
    tp_count = lax.axis_size("tp")
    me = lax.axis_index("req")
    per_dev = key_value_pages.shape[0]
    requests = lengths.shape[0]
    total = n * per_dev
    pages = key_value_pages.reshape(per_dev, PAGE_ROWS, HEAD_WIDTH)

    numbers = jnp.arange(per_dev, dtype=jnp.int32)
    peers = jnp.arange(n, dtype=jnp.int32)
    owner = page_request_home // per_dev
    match = (owner[:, None] == peers[None, :]) & (owner != me)[:, None]
    key = (numbers * total + page_request_home)[:, None]
    low_key = jnp.min(jnp.where(match, key, jnp.int32(2**30)), axis=0)
    high_key = jnp.max(jnp.where(match, key, -1), axis=0)
    keys = jnp.stack([low_key, high_key], axis=1)
    there = jnp.stack([high_key >= 0, high_key > low_key], axis=1)
    out_source = jnp.where(there, keys // total, 0).reshape(-1)
    out_label = jnp.where(there, keys % total, -1)

    slot_count = adapter_storage_slot.shape[0]
    slots = jnp.arange(slot_count, dtype=jnp.int32)
    own_slot = jnp.sum(
        jnp.where(
            request_adapter_index[:, None] == slots[None, :], adapter_storage_slot[None, :], 0
        ),
        axis=1,
    )
    token_slot = jnp.repeat(own_slot, STEP_COUNT)
    labels = (
        jnp.pad((out_label + 1) * 64, ((0, 0), (0, requests * STEP_COUNT - CAP)))
        + token_slot[None, :]
    ).reshape(n, 1, requests * STEP_COUNT)
    own_label = jnp.where(owner == me, page_request_home - me * per_dev, -1)
    local_table = jnp.sum(
        jnp.where(own_label[:, None] == numbers[None, :], numbers[:, None], 0), axis=0
    ).reshape(-1, HEAD_WIDTH)

    outbox = pick(out_source, pages)
    up = adapter_up_factor.reshape(-1, adapter_up_factor.shape[2])
    fresh = jnp.transpose(incoming_key_value, (1, 0, 2)).reshape(
        requests, 2 * STEP_COUNT, HEAD_WIDTH
    )
    fresh = jnp.pad(fresh, ((0, 0), (0, 8), (0, 0)))
    own_adapters, _, rank = adapter_down_factor.shape
    down = jnp.transpose(adapter_down_factor, (1, 0, 2)).reshape(-1, own_adapters * rank)
    return layer(
        outbox, labels, local_table, lengths, queries, fresh, pages, up,
        output_projection_weight, down, tp_count,
    )


def solution(mesh):
    return jax.shard_map(
        on_device,
        mesh=mesh,
        in_specs=(
            P("req", "tp"),
            P(None, "req", "tp"),
            P("req", None, None, "tp"),
            P("req"),
            P("req"),
            P("req"),
            P(),
            P("req", "tp", None),
            P("req", None, None),
            P("tp", "req"),
        ),
        out_specs=P("tp", "req"),
        check_vma=False,
    )
```

```python
import functools
import math

import jax
import jax.numpy as jnp
from jax import lax
from jax.experimental import pallas as pl
from jax.experimental.pallas import tpu as pltpu
from jax.sharding import PartitionSpec as P

QUERY_HEADS = 64
KEY_VALUE_HEADS = 8
GROUP = QUERY_HEADS // KEY_VALUE_HEADS
HEAD_WIDTH = 128
STEP_COUNT = 4
PAGE_LENGTH = 32
PAGE_ROWS = 2 * PAGE_LENGTH
MAXP = 16
CAP = 2
VMEM_BYTES = 60 * 1024 * 1024


HALF_COUNT = 2


def layer_kernel(
    home, home_s, adapter, storage, lengths, queries, incoming, pages, up, weights, down,
    out,
    cands, inbox, outbox, labels, inlab, sourcev, sources, tablev, table, outf, mixed, upall,
    everyone, part, lowpart, sendbuf, recvbuf, lowsend, lowrecv, sumsend, sumrecv, lowfull, extra,
    many_sent, many_got, ring_sent, ring_got, local_sem,
    s1_sent, s1_got, s2_sent, s2_got, relay_sent, relay_got, mate_sent, mate_got,
    main_sent, main_got, low_sent, low_got, sum_sent, sum_got,
):
    n, planes = upall.shape[0], upall.shape[1]
    me = lax.axis_index("req")
    lane = lax.axis_index("tp")
    core = lax.rem(me, 2)
    cx, cy = me // 8, lax.rem(me // 2, 4)
    first = cx * (1 - core) + cy * core
    second = cy * (1 - core) + cx * core
    above, below = lax.rem(lane + 1, planes), lax.rem(lane + planes - 1, planes)
    mate = me + 1 - 2 * core
    page_count = pages.shape[0]
    requests = lengths.shape[0]
    columns = out.shape[1]
    chunk_rows = queries.shape[0]
    half = chunk_rows // HALF_COUNT
    quarter = half // 2
    rank = HEAD_WIDTH // 2

    load = pltpu.make_async_copy(pages, cands.at[pl.ds(0, page_count)], local_sem.at[0])
    load.start()
    barrier = pltpu.get_barrier_semaphore()

    def greet(d, carry):
        pl.semaphore_signal(barrier, inc=1, device_id={"req": lax.rem(me + d, n)})
        return carry

    lax.fori_loop(1, n, greet, 0)
    pl.semaphore_signal(barrier, inc=1, device_id={"tp": above})
    pl.semaphore_signal(barrier, inc=1, device_id={"tp": below})

    def remote(src, dst, sent_sem, got_sem, **to):
        return pltpu.make_async_remote_copy(src, dst, sent_sem, got_sem, device_id=to)

    def arrived(ref, sem):
        pltpu.make_async_copy(ref, ref, sem).wait()

    shift = n * page_count
    bits = shift.bit_length() - 1
    page_bits = page_count.bit_length() - 1
    peer_row = lax.broadcasted_iota(jnp.int32, (n, HEAD_WIDTH), 0)
    lane_of = lax.broadcasted_iota(jnp.int32, (n, HEAD_WIDTH), 1)
    low_key = jnp.full((n, HEAD_WIDTH), 2 * page_count * shift, jnp.int32)
    high_key = jnp.full((n, HEAD_WIDTH), -1, jnp.int32)
    for i in range(page_count // HEAD_WIDTH):
        homes = jnp.broadcast_to(home[i : i + 1, :], (n, HEAD_WIDTH))
        match = (homes >> page_bits == peer_row) & (peer_row != me)
        key = (lane_of + i * HEAD_WIDTH) * shift + homes
        low_key = jnp.where(match, jnp.minimum(low_key, key), low_key)
        high_key = jnp.where(match, jnp.maximum(high_key, key), high_key)
    least = jnp.min(low_key, axis=1, keepdims=True)
    most = jnp.max(high_key, axis=1, keepdims=True)
    chosen = jnp.where(lane_of == 0, least, most)
    there = ((lane_of == 0) & (most >= 0)) | ((lane_of == 1) & (most > least))
    sourcev[...] = jnp.where(there, jnp.clip(chosen >> bits, 0, page_count - 1), 0)
    to_sources = pltpu.make_async_copy(sourcev, sources, local_sem.at[5])
    to_sources.start()
    words = jnp.where(there, ((chosen & (shift - 1)) + 1) * 64, 0)
    token_lane = lax.broadcasted_iota(jnp.int32, (1, HEAD_WIDTH), 1)
    slots = jnp.zeros((1, HEAD_WIDTH), jnp.int32)
    for i in range(requests):
        slots = jnp.where(token_lane // STEP_COUNT == i, storage[adapter[i]], slots)
    for i in range(n):
        labels[i] = words[i : i + 1] + slots
    inlab[me] = slots

    place = (
        lax.broadcasted_iota(jnp.int32, tablev.shape, 0) * HEAD_WIDTH
        + lax.broadcasted_iota(jnp.int32, tablev.shape, 1)
        + me * page_count
    )
    run = 16

    def enter_own(i, entries):
        for u in range(run):
            at_home = home_s[i // (HEAD_WIDTH // run), lax.rem(i, HEAD_WIDTH // run) * run + u]
            entries = jnp.where(place == at_home, i * run + u, entries)
        return entries

    own_table = lax.fori_loop(
        0, page_count // run, enter_own, jnp.zeros(tablev.shape, jnp.int32)
    )
    to_sources.wait()
    load.wait()

    def pick(d, carry):
        for k in range(CAP):
            outbox[d * CAP + k] = cands[sources[d, k]]
        return carry

    lax.fori_loop(0, n, pick, 0)
    pl.semaphore_wait(barrier, n + 1)

    up_rows = upall.shape[2]

    def up_part(peer):
        return up.at[
            pl.ds(pl.multiple_of(lane * up_rows, up_rows), up_rows),
            pl.ds(pl.multiple_of(peer * columns, columns), columns),
        ]

    def label_copy(d):
        peer = lax.rem(me + d, n)
        return remote(labels.at[peer], inlab.at[me], many_sent.at[0], many_got.at[0], req=peer)

    def page_copy(d):
        peer = lax.rem(me + d, n)
        return remote(
            outbox.at[pl.ds(peer * CAP, CAP)],
            inbox.at[pl.ds(me * CAP, CAP)],
            many_sent.at[1],
            many_got.at[1],
            req=peer,
        )

    def up_copy(d):
        peer = lax.rem(me + d, n)
        return remote(
            up_part(peer), upall.at[me, lane], many_sent.at[2], many_got.at[2], req=peer
        )

    own_up = pltpu.make_async_copy(up_part(me), upall.at[me, lane], local_sem.at[1])
    own_up.start()

    def begin_labels(d, carry):
        label_copy(d).start()
        return carry

    def begin_pages(d, carry):
        page_copy(d).start()
        return carry

    def begin_up(d, carry):
        up_copy(d).start()
        return carry

    lax.fori_loop(1, n, begin_labels, 0)
    lax.fori_loop(1, n, begin_pages, 0)
    lax.fori_loop(1, n, begin_up, 0)
    all_labels = inlab.at[pl.ds(0, n - 1)]
    all_pages = inbox.at[pl.ds(0, (n - 1) * CAP)]
    all_up = upall.at[pl.ds(0, n - 1), 0]

    hops = planes // 2

    def ring_copy(way, hop):
        peer = above if way == 0 else below
        origin = lax.rem(lane + planes + (hop if way == 1 else -hop), planes)
        piece = upall.at[:, origin]
        if hop == hops - 1:
            piece = upall.at[pl.ds(way * (n // 2), n // 2), origin]
        return pltpu.make_async_remote_copy(
            piece, piece, ring_sent.at[way, hop], ring_got.at[way, hop], device_id={"tp": peer}
        )

    def ring(hop):
        for way in range(2):
            if hop:
                ring_copy(way, hop - 1).wait_recv()
            if hop < hops:
                ring_copy(way, hop).start()

    arrived(all_labels, many_got.at[0])
    entries = own_table
    for source in range(n):
        word = inlab[source] >> 6
        for k in range(CAP):
            index = page_count + source * CAP + k
            entries = jnp.where(place + 1 == word[:, k : k + 1], index, entries)
    tablev[...] = entries
    to_scalar = pltpu.make_async_copy(tablev, table, local_sem.at[2])
    to_scalar.start()
    arrived(all_pages, many_got.at[1])
    take_in = pltpu.make_async_copy(
        inbox, cands.at[pl.ds(page_count, n * CAP)], local_sem.at[0]
    )
    take_in.start()
    arrived(all_up, many_got.at[2])
    own_up.wait()
    ring(0)
    to_scalar.wait()
    take_in.wait()

    old = MAXP * PAGE_ROWS
    width = old + HEAD_WIDTH
    rows_q = GROUP * STEP_COUNT
    column = lax.broadcasted_iota(jnp.int32, (rows_q, width), 1)
    step_of = lax.rem(lax.broadcasted_iota(jnp.int32, (rows_q, width), 0), STEP_COUNT)
    is_key = lax.rem(column, 2) == 0
    fresh_at = column - old
    keep_new = [
        (fresh_at >= k * STEP_COUNT) & (fresh_at - k * STEP_COUNT <= step_of) for k in range(2)
    ]
    position = jnp.where(is_key & (column < old), column // 2, 1 << 20)
    scale = 1.0 / math.sqrt(HEAD_WIDTH)
    filler = jnp.zeros((HEAD_WIDTH - 4 * STEP_COUNT, HEAD_WIDTH), cands.dtype)
    per_row = HEAD_WIDTH // MAXP

    def one(request, query, fresh, keep_fresh):
        pieces = []
        for j in range(MAXP):
            page = table[request // per_row, lax.rem(request, per_row) * MAXP + j]
            pieces.append(cands[page])
        pieces.append(fresh)
        pieces.append(filler)
        stored = jnp.concatenate(pieces, axis=0)
        scores = (
            lax.dot_general(
                query, stored, (((1,), (1,)), ((), ())), preferred_element_type=jnp.float32
            )
            * scale
        )
        keep = keep_fresh | (position < lengths[request])
        scores = jnp.where(keep, scores, -jnp.inf)
        top = jnp.max(scores, axis=1, keepdims=True)
        exps = jnp.exp(scores - top)
        probs = exps / jnp.sum(exps, axis=1, keepdims=True)
        probs = jnp.concatenate(
            [
                pltpu.roll(probs[:, :old], 1, 1),
                pltpu.roll(probs[:, old:], 2 * STEP_COUNT, 1),
            ],
            axis=1,
        ).astype(jnp.bfloat16)
        return jnp.dot(probs, stored, preferred_element_type=jnp.float32)

    def pair(index, carry):
        base = pl.multiple_of(index * 2 * STEP_COUNT, 2 * STEP_COUNT)
        both_q = queries[pl.ds(base, 2 * STEP_COUNT), :].astype(jnp.float32)
        fresh = jnp.concatenate(
            [incoming[i, pl.ds(base, 2 * STEP_COUNT), :].astype(jnp.float32) for i in range(2)],
            axis=0,
        ).astype(jnp.bfloat16)
        results = []
        for k in range(2):
            one_q = both_q[k * STEP_COUNT : (k + 1) * STEP_COUNT]
            query = jnp.concatenate(
                [one_q[:, h * HEAD_WIDTH : (h + 1) * HEAD_WIDTH] for h in range(GROUP)], axis=0
            ).astype(jnp.bfloat16)
            results.append(one(index * 2 + k, query, fresh, keep_new[k]))
        for h in range(GROUP):
            both = jnp.concatenate(
                [m[h * STEP_COUNT : (h + 1) * STEP_COUNT] for m in results], axis=0
            )
            outf[pl.ds(base, 2 * STEP_COUNT), h * HEAD_WIDTH : (h + 1) * HEAD_WIDTH] = both
        return carry

    def attend(start, stop):
        lax.fori_loop(start, stop, pair, 0)

    def spot(f, s, c):
        f, s = lax.rem(f + 8, 4), lax.rem(s + 8, 4)
        return f * (8 - 6 * c) + s * (2 + 6 * c) + c

    def at(df, ds):
        return spot(first + df, second + ds, core)

    def mate_at(df, ds):
        return spot(second + df, first + ds, 1 - core)

    OFFSET = (0, 1, -1, 2)
    DS = (0, -1, 1, 2)

    def whole(h):
        return pl.ds(h * half, half)

    def side_rows(h, way):
        return pl.ds(h * half + way * quarter, quarter)

    def step_one(h, way):
        to = at(1 if way == 0 else -1, 0)
        return remote(
            mixed.at[whole(h)], everyone.at[me, whole(h)],
            s1_sent.at[h, way], s1_got.at[h, way], req=to,
        )

    def step_one_half(h, way):
        ref = everyone.at[at(-1 if way == 0 else 1, 0), side_rows(h, way)]
        to = at(1 if way == 0 else -1, 0)
        return remote(ref, ref, s1_sent.at[h, 2 + way], s1_got.at[h, 2 + way], req=to)

    def step_two(h, k, way):
        ref = everyone.at[at(OFFSET[k], 0), whole(h)]
        src = mixed.at[whole(h)] if k == 0 else ref
        to = at(0, 1 if way == 0 else -1)
        return remote(src, ref, s2_sent.at[h, k, way], s2_got.at[h, k, way], req=to)

    def relay(h, k, way):
        ref = everyone.at[at(OFFSET[k], -1 if way == 0 else 1), side_rows(h, way)]
        to = at(0, 1 if way == 0 else -1)
        return remote(ref, ref, relay_sent.at[h, k, way], relay_got.at[h, k, way], req=to)

    def to_mate(h, k, j):
        ref = everyone.at[at(OFFSET[k], DS[j]), whole(h)]
        src = mixed.at[whole(h)] if k == 0 and j == 0 else ref
        return remote(src, ref, mate_sent.at[h, j, k], mate_got.at[h, j, k], req=mate)

    def got_mate(h, k, j):
        arrived(everyone.at[mate_at(OFFSET[k], DS[j]), whole(h)], mate_got.at[h, j, k])

    def own_copy(h):
        return pltpu.make_async_copy(
            mixed.at[whole(h)], everyone.at[me, whole(h)], local_sem.at[3 + h]
        )

    def open_gather(h):
        rows = pl.ds(h * half, half)
        mixed[rows, :] = outf[rows, :].astype(mixed.dtype)
        for way in range(2):
            step_one(h, way).start()
        for way in range(2):
            step_two(h, 0, way).start()
        to_mate(h, 0, 0).start()
        own_copy(h).start()

    def pass_on(h, k):
        step_two(h, k, 0).start()
        step_two(h, k, 1).start()
        to_mate(h, k, 0).start()

    def near(h):
        for way, k in ((0, 2), (1, 1)):
            arrived(everyone.at[at(OFFSET[k], 0), whole(h)], s1_got.at[h, way])
            step_one_half(h, way).start()
            pass_on(h, k)

    def far(h):
        for way in range(2):
            arrived(everyone.at[at(2, 0), side_rows(h, way)], s1_got.at[h, 2 + way])
        pass_on(h, 3)

    def turn(h, k):
        for way, j in ((0, 1), (1, 2)):
            arrived(everyone.at[at(OFFSET[k], DS[j]), whole(h)], s2_got.at[h, k, way])
            relay(h, k, way).start()
            to_mate(h, k, j).start()

    def last(h, k):
        for way in range(2):
            arrived(everyone.at[at(OFFSET[k], 2), side_rows(h, way)], relay_got.at[h, k, way])
        to_mate(h, k, 3).start()

    row64 = lax.broadcasted_iota(jnp.int32, (half, HEAD_WIDTH), 0)
    col64 = lax.broadcasted_iota(jnp.int32, (half, HEAD_WIDTH), 1)
    narrow = lax.broadcasted_iota(jnp.int32, (quarter, HEAD_WIDTH), 1) < rank
    upper = col64 // rank

    def slot_column(r, h):
        values = (inlab[r] & 63).astype(jnp.float32)
        values = jnp.where(row64 + h * half == col64, values, 0.0)
        return jnp.sum(values, axis=1, keepdims=True).astype(jnp.int32)

    def batch(h, kjs):
        for k, j in kjs:
            got_mate(h, k, j)
        owners = [at(OFFSET[k], DS[j]) for k, j in kjs]
        owners += [mate_at(OFFSET[k], DS[j]) for k, j in kjs]
        rows = jnp.concatenate([everyone[r, whole(h)] for r in owners], axis=0)
        product = jnp.dot(rows, weights[...], preferred_element_type=jnp.float32)
        lows = lax.dot_general(
            rows, down[...], (((1,), (1,)), ((), ())), preferred_element_type=jnp.float32
        )
        for i, r in enumerate(owners):
            cut = slice(i * half, (i + 1) * half)
            part[r, whole(h)] = product[cut]
            low = jnp.where(slot_column(r, h) == 2 * me + upper, lows[cut], 0.0)
            low = low + pltpu.roll(low, rank, 1)
            lowpart[r, h] = jnp.where(narrow, low[:quarter], low[quarter:])

    def batch_a(h):
        own_copy(h).wait()
        batch(h, [(k, 0) for k in range(4)])

    def batch_b(h, ks):
        batch(h, [(k, j) for k in ks for j in (1, 2)])

    def batch_c(h):
        batch(h, [(k, 3) for k in range(4)])

    subs = n // planes

    def target(way, step):
        return lax.rem(lane + planes + (step - hops if way == 0 else hops - step), planes)

    def low_copy(h, way, step):
        peer = below if way == 0 else above
        src, dst = lowsend.at[h, way, step], lowrecv.at[h, way, step]
        if step == 0:
            some = pl.ds(way * (subs // 2), subs // 2)
            src, dst = lowsend.at[h, way, step, some], lowrecv.at[h, way, step, some]
        return remote(src, dst, low_sent.at[h, way, step], low_got.at[h, way, step], tp=peer)

    def low_step(h, step):
        for way in range(2):
            if step:
                low_copy(h, way, step - 1).wait_recv()
            q = target(way, step)
            for sub in range(subs):
                mine = sub // (subs // 2) == way
                if step == 0 and not mine:
                    continue
                value = lowpart[q * subs + sub, h]
                if step > 1 or (step == 1 and mine):
                    value = value + lowrecv[h, way, step - 1, sub].astype(jnp.float32)
                lowsend[h, way, step, sub] = value.astype(jnp.bfloat16)
            low_copy(h, way, step).start()

    wing = columns // 2

    def main_copy(h, way, step, p):
        peer = below if way == 0 else above
        src, dst = sendbuf.at[h, way, step, p], recvbuf.at[h, way, step, p]
        if step == 0:
            side = pl.ds(way * wing, wing)
            src = sendbuf.at[h, way, step, p, :, :, side]
            dst = recvbuf.at[h, way, step, p, :, :, side]
        return remote(
            src, dst, main_sent.at[h, way, step, p], main_got.at[h, way, step, p], tp=peer
        )

    def main_step(h, step, p):
        for way in range(2):
            q = target(way, step)
            side = slice(way * wing, (way + 1) * wing)
            other = slice((1 - way) * wing, (2 - way) * wing)
            if step:
                main_copy(h, way, step - 1, p).wait_recv()
            for i in range(2):
                value = part[q * subs + 2 * p + i, whole(h)]
                if step == 0:
                    sendbuf[h, way, 0, p, i, :, side] = value[:, side].astype(jnp.bfloat16)
                elif step == 1:
                    came = recvbuf[h, way, 0, p, i, :, side].astype(jnp.float32)
                    sendbuf[h, way, 1, p, i, :, side] = (value[:, side] + came).astype(jnp.bfloat16)
                    sendbuf[h, way, 1, p, i, :, other] = value[:, other].astype(jnp.bfloat16)
                else:
                    came = recvbuf[h, way, step - 1, p, i].astype(jnp.float32)
                    sendbuf[h, way, step, p, i] = (value + came).astype(jnp.bfloat16)
            main_copy(h, way, step, p).start()

    def sum_mate():
        return remote(
            sumsend.at[0, 1 - core], sumrecv.at[0], sum_sent.at[0], sum_got.at[0], req=mate
        )

    def sum_axis(axis, d):
        peer = at(d, 0) if axis == 0 else at(0, d)
        i = 1 + 3 * axis + d - 1
        return remote(
            sumsend.at[1 + axis, 0], sumrecv.at[i], sum_sent.at[i], sum_got.at[i], req=peer
        )

    def sum_back():
        return remote(
            lowfull.at[core], lowfull.at[core], sum_sent.at[7], sum_got.at[7], req=mate
        )

    def low_end(h):
        for way in range(2):
            low_copy(h, way, hops - 1).wait_recv()
        for sub in range(subs):
            value = lowpart[lane * subs + sub, h]
            for way in range(2):
                value = value + lowrecv[h, way, hops - 1, sub].astype(jnp.float32)
            sumsend[0, h, pl.ds(quarter * sub, quarter)] = value.astype(jnp.bfloat16)

    def sum_first():
        sum_mate().wait_recv()
        value = sumsend[0, core].astype(jnp.float32) + sumrecv[0].astype(jnp.float32)
        sumsend[1, 0] = value.astype(jnp.bfloat16)
        for d in range(1, 4):
            sum_axis(0, d).start()

    def gathered(axis):
        value = sumsend[1 + axis, 0].astype(jnp.float32)
        for d in range(1, 4):
            sum_axis(axis, d).wait_recv()
            value = value + sumrecv[1 + 3 * axis + d - 1].astype(jnp.float32)
        return value.astype(jnp.bfloat16)

    def sum_second():
        sumsend[2, 0] = gathered(0)
        for d in range(1, 4):
            sum_axis(1, d).start()

    def sum_third():
        lowfull[core] = gathered(1)
        sum_back().start()

    def lora():
        arrived(lowfull.at[1 - core], sum_got.at[7])
        pieces, owners = [], []
        for sub in range(subs):
            for h in range(HALF_COUNT):
                packed = lowfull[h, pl.ds(quarter * sub, quarter)].astype(jnp.float32)
                turned = pltpu.roll(packed, rank, 1)
                pieces += [jnp.where(narrow, packed, turned), jnp.where(narrow, turned, packed)]
                owners.append(slot_column(lane * subs + sub, h))
        low = jnp.concatenate(pieces, axis=0)
        owner = jnp.concatenate(owners, axis=0)
        side = lax.broadcasted_iota(jnp.int32, low.shape, 1) // rank
        group = 8
        extra[...] = jnp.zeros(extra.shape, jnp.float32)

        def add(g, carry):
            wide = jnp.concatenate(
                [
                    jnp.where(owner == 2 * (g * group + m) + side, low, 0.0).astype(jnp.bfloat16)
                    for m in range(group)
                ],
                axis=1,
            )
            stored = upall[pl.ds(g * group, group)].reshape(group * planes * up_rows, columns)
            extra[...] += jnp.dot(wide, stored, preferred_element_type=jnp.float32)
            return carry

        lax.fori_loop(0, n // group, add, 0)

    pairs = requests // 2
    attend(0, pairs // 2)
    open_gather(0)
    ring(1)
    attend(pairs // 2, pairs // 2 + 2)
    near(0)
    attend(pairs // 2 + 2, pairs // 2 + 4)
    turn(0, 0)
    far(0)
    attend(pairs // 2 + 4, pairs // 2 + 6)
    turn(0, 1)
    turn(0, 2)
    attend(pairs // 2 + 6, pairs)
    open_gather(1)
    ring(2)
    turn(0, 3)
    last(0, 0)
    batch_a(0)
    last(0, 1)
    near(1)
    batch_b(0, (0, 1))
    ring(3)
    last(0, 2)
    last(0, 3)
    turn(1, 0)
    far(1)
    batch_b(0, (2, 3))
    turn(1, 1)
    batch_c(0)
    low_step(0, 0)
    main_step(0, 0, 0)
    main_step(0, 0, 1)
    turn(1, 2)
    low_step(0, 1)
    main_step(0, 1, 0)
    main_step(0, 1, 1)
    turn(1, 3)
    last(1, 0)
    batch_a(1)
    low_step(0, 2)
    main_step(0, 2, 0)
    last(1, 1)
    batch_b(1, (0, 1))
    main_step(0, 2, 1)
    low_step(0, 3)
    last(1, 2)
    last(1, 3)
    batch_b(1, (2, 3))
    main_step(0, 3, 0)
    main_step(0, 3, 1)
    batch_c(1)
    low_step(1, 0)
    low_end(0)
    main_step(1, 0, 0)
    main_step(1, 0, 1)
    low_step(1, 1)
    main_step(1, 1, 0)
    low_step(1, 2)
    main_step(1, 1, 1)
    low_step(1, 3)
    main_step(1, 2, 0)
    low_end(1)
    sum_mate().start()
    main_step(1, 2, 1)
    sum_first()
    main_step(1, 3, 0)
    sum_second()
    main_step(1, 3, 1)
    sum_third()
    ring(4)
    lora()
    for h in range(HALF_COUNT):
        for sub in range(subs):
            p, i = sub // 2, sub % 2
            rows = pl.ds(sub * chunk_rows + h * half, half)
            value = part[lane * subs + sub, whole(h)] + extra[rows, :]
            for way in range(2):
                if i == 0:
                    main_copy(h, way, hops - 1, p).wait_recv()
                value = value + recvbuf[h, way, hops - 1, p, i].astype(jnp.float32)
            out[rows, :] = value.astype(out.dtype)

    arrived(all_labels, many_sent.at[0])
    arrived(all_pages, many_sent.at[1])
    arrived(all_up, many_sent.at[2])
    for way in range(2):
        for hop in range(hops):
            ring_copy(way, hop).wait_send()
    for h in range(HALF_COUNT):
        for way in range(2):
            step_one(h, way).wait_send()
            step_one_half(h, way).wait_send()
            for k in range(4):
                step_two(h, k, way).wait_send()
                relay(h, k, way).wait_send()
            for step in range(hops):
                low_copy(h, way, step).wait_send()
                for p in range(2):
                    main_copy(h, way, step, p).wait_send()
        for k in range(4):
            for j in range(4):
                to_mate(h, k, j).wait_send()
    sum_mate().wait_send()
    for axis in range(2):
        for d in range(1, 4):
            sum_axis(axis, d).wait_send()
    sum_back().wait_send()


def layer(n, planes, home, adapter, storage, lengths, queries, incoming, pages, up, weights, down):
    rows, depth = queries.shape
    columns = weights.shape[1]
    hops, subs, half = planes // 2, n // planes, rows // HALF_COUNT
    hbm = pl.BlockSpec(memory_space=pltpu.HBM)
    vmem = pl.BlockSpec(memory_space=pltpu.VMEM)
    smem = pl.BlockSpec(memory_space=pltpu.SMEM)
    dma = pltpu.SemaphoreType.DMA
    bf16, f32, i32 = jnp.bfloat16, jnp.float32, jnp.int32
    hc = HALF_COUNT
    return pl.pallas_call(
        layer_kernel,
        out_shape=jax.ShapeDtypeStruct((n * rows // planes, columns), bf16),
        in_specs=[vmem, smem, smem, smem, smem, vmem, vmem, hbm, hbm, vmem, vmem],
        out_specs=vmem,
        scratch_shapes=[
            pltpu.VMEM((pages.shape[0] + n * CAP, PAGE_ROWS, HEAD_WIDTH), bf16),
            pltpu.VMEM((n * CAP, PAGE_ROWS, HEAD_WIDTH), bf16),
            pltpu.VMEM((n * CAP, PAGE_ROWS, HEAD_WIDTH), bf16),
            pltpu.VMEM((n, 1, HEAD_WIDTH), i32),
            pltpu.VMEM((n, 1, HEAD_WIDTH), i32),
            pltpu.VMEM((n, HEAD_WIDTH), i32),
            pltpu.SMEM((n, HEAD_WIDTH), i32),
            pltpu.VMEM(home.shape, i32),
            pltpu.SMEM(home.shape, i32),
            pltpu.VMEM((rows, depth), f32),
            pltpu.VMEM((rows, depth), bf16),
            pltpu.VMEM((n, planes, up.shape[0] // planes, columns), bf16),
            pltpu.VMEM((n, rows, depth), bf16),
            pltpu.VMEM((n, rows, columns), f32),
            pltpu.VMEM((n, hc, half // 2, HEAD_WIDTH), f32),
            pltpu.VMEM((hc, 2, hops, 2, subs // 2, half, columns), bf16),
            pltpu.VMEM((hc, 2, hops, 2, subs // 2, half, columns), bf16),
            pltpu.VMEM((hc, 2, hops, subs, half // 2, HEAD_WIDTH), bf16),
            pltpu.VMEM((hc, 2, hops, subs, half // 2, HEAD_WIDTH), bf16),
            pltpu.VMEM((3, 2, rows, HEAD_WIDTH), bf16),
            pltpu.VMEM((7, rows, HEAD_WIDTH), bf16),
            pltpu.VMEM((2, rows, HEAD_WIDTH), bf16),
            pltpu.VMEM((n * rows // planes, columns), f32),
        ]
        + [dma((3,))] * 2
        + [dma((2, hops))] * 2
        + [dma((6,))]
        + [dma((hc, 4))] * 2
        + [dma((hc, 4, 2))] * 4
        + [dma((hc, 4, 4))] * 2
        + [dma((hc, 2, hops, 2))] * 2
        + [dma((hc, 2, hops))] * 2
        + [dma((8,))] * 2,
        compiler_params=pltpu.CompilerParams(
            collective_id=0, has_side_effects=True, vmem_limit_bytes=VMEM_BYTES
        ),
        name="layer",
    )(home, home, adapter, storage, lengths, queries, incoming, pages, up, weights, down)


def on_device(
    queries,
    incoming_key_value,
    key_value_pages,
    page_request_home,
    lengths,
    request_adapter_index,
    adapter_storage_slot,
    adapter_down_factor,
    adapter_up_factor,
    output_projection_weight,
):
    per_dev = key_value_pages.shape[0]
    own_adapters, depth, rank = adapter_down_factor.shape
    return layer(
        lax.axis_size("req"),
        lax.axis_size("tp"),
        page_request_home.reshape(-1, HEAD_WIDTH),
        request_adapter_index,
        adapter_storage_slot,
        lengths,
        queries,
        incoming_key_value,
        key_value_pages.reshape(per_dev, PAGE_ROWS, HEAD_WIDTH),
        adapter_up_factor.reshape(-1, adapter_up_factor.shape[2]),
        output_projection_weight,
        jnp.transpose(adapter_down_factor, (0, 2, 1)).reshape(own_adapters * rank, depth),
    )


def solution(mesh):
    return jax.shard_map(
        on_device,
        mesh=mesh,
        in_specs=(
            P("req", "tp"),
            P(None, "req", "tp"),
            P("req", None, None, "tp"),
            P("req"),
            P("req"),
            P("req"),
            P(),
            P("req", "tp", None),
            P("req", None, None),
            P("tp", "req"),
        ),
        out_specs=P("tp", "req"),
        check_vma=False,
    )
```

```python
import functools
import math

import jax
import jax.numpy as jnp
from jax import lax
from jax.experimental import pallas as pl
from jax.experimental.pallas import tpu as pltpu
from jax.sharding import PartitionSpec as P

QUERY_HEADS = 64
KEY_VALUE_HEADS = 8
GROUP = QUERY_HEADS // KEY_VALUE_HEADS
HEAD_WIDTH = 128
STEP_COUNT = 4
PAGE_LENGTH = 32
PAGE_ROWS = 2 * PAGE_LENGTH
MAXP = 16
CAP = 2
VMEM_BYTES = 60 * 1024 * 1024


HALF_COUNT = 2


def layer_kernel(
    home, home_s, adapter, storage, lengths, queries, incoming, pages, up, weights, down,
    out,
    cands, inbox, outbox, labels, inlab, sourcev, sources, tablev, table, outf, mixed, upall,
    everyone, part, sendbuf, recvbuf, lowsend, lowrecv, lowsum, lowz, lowfull, extra,
    many_sent, many_got, ring_sent, ring_got, local_sem,
    s1_sent, s1_got, s2_sent, s2_got, relay_sent, relay_got, mate_sent, mate_got,
    main_sent, main_got, low_sent, low_got, full_got,
):
    n, planes = upall.shape[0], upall.shape[1]
    me = lax.axis_index("req")
    lane = lax.axis_index("tp")
    core = lax.rem(me, 2)
    cx, cy = me // 8, lax.rem(me // 2, 4)
    first = cx * (1 - core) + cy * core
    second = cy * (1 - core) + cx * core
    above, below = lax.rem(lane + 1, planes), lax.rem(lane + planes - 1, planes)
    mate = me + 1 - 2 * core
    page_count = pages.shape[0]
    requests = lengths.shape[0]
    columns = out.shape[1]
    chunk_rows = queries.shape[0]
    half = chunk_rows // HALF_COUNT
    quarter = half // 2
    rank = HEAD_WIDTH // 2

    load = pltpu.make_async_copy(pages, cands.at[pl.ds(0, page_count)], local_sem.at[0])
    load.start()
    barrier = pltpu.get_barrier_semaphore()

    def greet(d, carry):
        pl.semaphore_signal(barrier, inc=1, device_id={"req": lax.rem(me + d, n)})
        return carry

    lax.fori_loop(1, n, greet, 0)
    for d in range(1, planes):
        pl.semaphore_signal(barrier, inc=1, device_id={"tp": lax.rem(lane + d, planes)})

    def remote(src, dst, sent_sem, got_sem, **to):
        return pltpu.make_async_remote_copy(src, dst, sent_sem, got_sem, device_id=to)

    def arrived(ref, sem):
        pltpu.make_async_copy(ref, ref, sem).wait()

    shift = n * page_count
    bits = shift.bit_length() - 1
    page_bits = page_count.bit_length() - 1
    peer_row = lax.broadcasted_iota(jnp.int32, (n, HEAD_WIDTH), 0)
    lane_of = lax.broadcasted_iota(jnp.int32, (n, HEAD_WIDTH), 1)
    low_key = jnp.full((n, HEAD_WIDTH), 2 * page_count * shift, jnp.int32)
    high_key = jnp.full((n, HEAD_WIDTH), -1, jnp.int32)
    for i in range(page_count // HEAD_WIDTH):
        homes = jnp.broadcast_to(home[i : i + 1, :], (n, HEAD_WIDTH))
        match = (homes >> page_bits == peer_row) & (peer_row != me)
        key = (lane_of + i * HEAD_WIDTH) * shift + homes
        low_key = jnp.where(match, jnp.minimum(low_key, key), low_key)
        high_key = jnp.where(match, jnp.maximum(high_key, key), high_key)
    least = jnp.min(low_key, axis=1, keepdims=True)
    most = jnp.max(high_key, axis=1, keepdims=True)
    chosen = jnp.where(lane_of == 0, least, most)
    there = ((lane_of == 0) & (most >= 0)) | ((lane_of == 1) & (most > least))
    sourcev[...] = jnp.where(there, jnp.clip(chosen >> bits, 0, page_count - 1), 0)
    to_sources = pltpu.make_async_copy(sourcev, sources, local_sem.at[5])
    to_sources.start()
    words = jnp.where(there, ((chosen & (shift - 1)) + 1) * 64, 0)
    token_lane = lax.broadcasted_iota(jnp.int32, (1, HEAD_WIDTH), 1)
    slots = jnp.zeros((1, HEAD_WIDTH), jnp.int32)
    for i in range(requests):
        slots = jnp.where(token_lane // STEP_COUNT == i, storage[adapter[i]], slots)
    for i in range(n):
        labels[i] = words[i : i + 1] + slots
    inlab[me] = slots

    place = (
        lax.broadcasted_iota(jnp.int32, tablev.shape, 0) * HEAD_WIDTH
        + lax.broadcasted_iota(jnp.int32, tablev.shape, 1)
        + me * page_count
    )
    run = 16

    def enter_own(i, entries):
        for u in range(run):
            at_home = home_s[i // (HEAD_WIDTH // run), lax.rem(i, HEAD_WIDTH // run) * run + u]
            entries = jnp.where(place == at_home, i * run + u, entries)
        return entries

    own_table = lax.fori_loop(
        0, page_count // run, enter_own, jnp.zeros(tablev.shape, jnp.int32)
    )
    to_sources.wait()
    load.wait()

    def pick(d, carry):
        for k in range(CAP):
            outbox[d * CAP + k] = cands[sources[d, k]]
        return carry

    lax.fori_loop(0, n, pick, 0)
    pl.semaphore_wait(barrier, n + planes - 2)

    up_rows = upall.shape[2]

    def up_part(peer):
        return up.at[
            pl.ds(pl.multiple_of(lane * up_rows, up_rows), up_rows),
            pl.ds(pl.multiple_of(peer * columns, columns), columns),
        ]

    def label_copy(d):
        peer = lax.rem(me + d, n)
        return remote(labels.at[peer], inlab.at[me], many_sent.at[0], many_got.at[0], req=peer)

    def page_copy(d):
        peer = lax.rem(me + d, n)
        return remote(
            outbox.at[pl.ds(peer * CAP, CAP)],
            inbox.at[pl.ds(me * CAP, CAP)],
            many_sent.at[1],
            many_got.at[1],
            req=peer,
        )

    def up_copy(d):
        peer = lax.rem(me + d, n)
        return remote(
            up_part(peer), upall.at[me, lane], many_sent.at[2], many_got.at[2], req=peer
        )

    own_up = pltpu.make_async_copy(up_part(me), upall.at[me, lane], local_sem.at[1])

    def begin_labels(d, carry):
        label_copy(d).start()
        return carry

    def begin_pages(d, carry):
        page_copy(d).start()
        return carry

    def begin_up(d, carry):
        up_copy(d).start()
        return carry

    lax.fori_loop(1, n, begin_labels, 0)
    lax.fori_loop(1, n, begin_pages, 0)
    all_labels = inlab.at[pl.ds(0, n - 1)]
    all_pages = inbox.at[pl.ds(0, (n - 1) * CAP)]
    all_up = upall.at[pl.ds(0, n - 1), 0]

    hops = planes // 2

    def ring_copy(way, hop):
        peer = above if way == 0 else below
        origin = lax.rem(lane + planes + (hop if way == 1 else -hop), planes)
        piece = upall.at[:, origin]
        if hop == hops - 1:
            piece = upall.at[pl.ds(way * (n // 2), n // 2), origin]
        return pltpu.make_async_remote_copy(
            piece, piece, ring_sent.at[way, hop], ring_got.at[way, hop], device_id={"tp": peer}
        )

    def ring(hop):
        for way in range(2):
            if hop:
                ring_copy(way, hop - 1).wait_recv()
            if hop < hops:
                ring_copy(way, hop).start()

    arrived(all_labels, many_got.at[0])
    entries = own_table
    for source in range(n):
        word = inlab[source] >> 6
        for k in range(CAP):
            index = page_count + source * CAP + k
            entries = jnp.where(place + 1 == word[:, k : k + 1], index, entries)
    tablev[...] = entries
    to_scalar = pltpu.make_async_copy(tablev, table, local_sem.at[2])
    to_scalar.start()
    arrived(all_pages, many_got.at[1])
    take_in = pltpu.make_async_copy(
        inbox, cands.at[pl.ds(page_count, n * CAP)], local_sem.at[0]
    )
    take_in.start()
    own_up.start()
    lax.fori_loop(1, n, begin_up, 0)
    to_scalar.wait()
    take_in.wait()

    old = MAXP * PAGE_ROWS
    width = old + HEAD_WIDTH
    rows_q = GROUP * STEP_COUNT
    column = lax.broadcasted_iota(jnp.int32, (rows_q, width), 1)
    step_of = lax.rem(lax.broadcasted_iota(jnp.int32, (rows_q, width), 0), STEP_COUNT)
    is_key = lax.rem(column, 2) == 0
    fresh_at = column - old
    keep_new = [
        (fresh_at >= k * STEP_COUNT) & (fresh_at - k * STEP_COUNT <= step_of) for k in range(2)
    ]
    position = jnp.where(is_key & (column < old), column // 2, 1 << 20)
    scale = 1.0 / math.sqrt(HEAD_WIDTH)
    filler = jnp.zeros((HEAD_WIDTH - 4 * STEP_COUNT, HEAD_WIDTH), cands.dtype)
    per_row = HEAD_WIDTH // MAXP

    def one(request, query, fresh, keep_fresh):
        pieces = []
        for j in range(MAXP):
            page = table[request // per_row, lax.rem(request, per_row) * MAXP + j]
            pieces.append(cands[page])
        pieces.append(fresh)
        pieces.append(filler)
        stored = jnp.concatenate(pieces, axis=0)
        scores = (
            lax.dot_general(
                query, stored, (((1,), (1,)), ((), ())), preferred_element_type=jnp.float32
            )
            * scale
        )
        keep = keep_fresh | (position < lengths[request])
        scores = jnp.where(keep, scores, -jnp.inf)
        top = jnp.max(scores, axis=1, keepdims=True)
        exps = jnp.exp(scores - top)
        probs = exps / jnp.sum(exps, axis=1, keepdims=True)
        probs = jnp.concatenate(
            [
                pltpu.roll(probs[:, :old], 1, 1),
                pltpu.roll(probs[:, old:], 2 * STEP_COUNT, 1),
            ],
            axis=1,
        ).astype(jnp.bfloat16)
        return jnp.dot(probs, stored, preferred_element_type=jnp.float32)

    def pair(index, carry):
        base = pl.multiple_of(index * 2 * STEP_COUNT, 2 * STEP_COUNT)
        both_q = queries[pl.ds(base, 2 * STEP_COUNT), :].astype(jnp.float32)
        fresh = jnp.concatenate(
            [incoming[i, pl.ds(base, 2 * STEP_COUNT), :].astype(jnp.float32) for i in range(2)],
            axis=0,
        ).astype(jnp.bfloat16)
        results = []
        for k in range(2):
            one_q = both_q[k * STEP_COUNT : (k + 1) * STEP_COUNT]
            query = jnp.concatenate(
                [one_q[:, h * HEAD_WIDTH : (h + 1) * HEAD_WIDTH] for h in range(GROUP)], axis=0
            ).astype(jnp.bfloat16)
            results.append(one(index * 2 + k, query, fresh, keep_new[k]))
        for h in range(GROUP):
            both = jnp.concatenate(
                [m[h * STEP_COUNT : (h + 1) * STEP_COUNT] for m in results], axis=0
            )
            outf[pl.ds(base, 2 * STEP_COUNT), h * HEAD_WIDTH : (h + 1) * HEAD_WIDTH] = both
        return carry

    def attend(start, stop):
        lax.fori_loop(start, stop, pair, 0)

    def spot(f, s, c):
        f, s = lax.rem(f + 8, 4), lax.rem(s + 8, 4)
        return f * (8 - 6 * c) + s * (2 + 6 * c) + c

    def at(df, ds):
        return spot(first + df, second + ds, core)

    def mate_at(df, ds):
        return spot(second + df, first + ds, 1 - core)

    OFFSET = (0, 1, -1, 2)
    DS = (0, -1, 1, 2)

    def whole(h):
        return pl.ds(h * half, half)

    def side_rows(h, way):
        return pl.ds(h * half + way * quarter, quarter)

    def step_one(h, way):
        to = at(1 if way == 0 else -1, 0)
        return remote(
            mixed.at[whole(h)], everyone.at[me, whole(h)],
            s1_sent.at[h, way], s1_got.at[h, way], req=to,
        )

    def step_one_half(h, way):
        ref = everyone.at[at(-1 if way == 0 else 1, 0), side_rows(h, way)]
        to = at(1 if way == 0 else -1, 0)
        return remote(ref, ref, s1_sent.at[h, 2 + way], s1_got.at[h, 2 + way], req=to)

    def step_two(h, k, way):
        ref = everyone.at[at(OFFSET[k], 0), whole(h)]
        src = mixed.at[whole(h)] if k == 0 else ref
        to = at(0, 1 if way == 0 else -1)
        return remote(src, ref, s2_sent.at[h, k, way], s2_got.at[h, k, way], req=to)

    def relay(h, k, way):
        ref = everyone.at[at(OFFSET[k], -1 if way == 0 else 1), side_rows(h, way)]
        to = at(0, 1 if way == 0 else -1)
        return remote(ref, ref, relay_sent.at[h, k, way], relay_got.at[h, k, way], req=to)

    def to_mate(h, k, j):
        ref = everyone.at[at(OFFSET[k], DS[j]), whole(h)]
        src = mixed.at[whole(h)] if k == 0 and j == 0 else ref
        return remote(src, ref, mate_sent.at[h, j, k], mate_got.at[h, j, k], req=mate)

    def got_mate(h, k, j):
        arrived(everyone.at[mate_at(OFFSET[k], DS[j]), whole(h)], mate_got.at[h, j, k])

    def own_copy(h):
        return pltpu.make_async_copy(
            mixed.at[whole(h)], everyone.at[me, whole(h)], local_sem.at[3 + h]
        )

    def open_gather(h):
        rows = pl.ds(h * half, half)
        mixed[rows, :] = outf[rows, :].astype(mixed.dtype)
        for way in range(2):
            step_one(h, way).start()
        for way in range(2):
            step_two(h, 0, way).start()
        to_mate(h, 0, 0).start()
        own_copy(h).start()

    def pass_on(h, k):
        step_two(h, k, 0).start()
        step_two(h, k, 1).start()
        to_mate(h, k, 0).start()

    def near(h):
        for way, k in ((0, 2), (1, 1)):
            arrived(everyone.at[at(OFFSET[k], 0), whole(h)], s1_got.at[h, way])
            step_one_half(h, way).start()
            pass_on(h, k)

    def far(h):
        for way in range(2):
            arrived(everyone.at[at(2, 0), side_rows(h, way)], s1_got.at[h, 2 + way])
        pass_on(h, 3)

    def turn(h, k):
        for way, j in ((0, 1), (1, 2)):
            arrived(everyone.at[at(OFFSET[k], DS[j]), whole(h)], s2_got.at[h, k, way])
            relay(h, k, way).start()
            to_mate(h, k, j).start()

    def last(h, k):
        for way in range(2):
            arrived(everyone.at[at(OFFSET[k], 2), side_rows(h, way)], relay_got.at[h, k, way])
        to_mate(h, k, 3).start()

    row64 = lax.broadcasted_iota(jnp.int32, (half, HEAD_WIDTH), 0)
    col64 = lax.broadcasted_iota(jnp.int32, (half, HEAD_WIDTH), 1)
    narrow = lax.broadcasted_iota(jnp.int32, (quarter, HEAD_WIDTH), 1) < rank
    upper = col64 // rank

    def slot_column(r, h):
        values = (inlab[r] & 63).astype(jnp.float32)
        values = jnp.where(row64 + h * half == col64, values, 0.0)
        return jnp.sum(values, axis=1, keepdims=True).astype(jnp.int32)

    def low_home(h, r):
        return remote(
            lowsend.at[h, r], lowrecv.at[h, me], low_sent.at[0, h], low_got.at[0, h], req=r
        )

    def batch(h, kjs):
        for k, j in kjs:
            got_mate(h, k, j)
        owners = [at(OFFSET[k], DS[j]) for k, j in kjs]
        owners += [mate_at(OFFSET[k], DS[j]) for k, j in kjs]
        rows = jnp.concatenate([everyone[r, whole(h)] for r in owners], axis=0)
        product = jnp.dot(rows, weights[...], preferred_element_type=jnp.float32)
        lows = lax.dot_general(
            rows, down[...], (((1,), (1,)), ((), ())), preferred_element_type=jnp.float32
        )
        for i, r in enumerate(owners):
            cut = slice(i * half, (i + 1) * half)
            part[r, whole(h)] = product[cut]
            low = jnp.where(slot_column(r, h) == 2 * me + upper, lows[cut], 0.0)
            low = low + pltpu.roll(low, rank, 1)
            lowsend[h, r] = jnp.where(narrow, low[:quarter], low[quarter:]).astype(jnp.bfloat16)
            if kjs[0] != (0, 0) or i:
                low_home(h, r).start()

    def batch_a(h):
        own_copy(h).wait()
        batch(h, [(k, 0) for k in range(4)])

    def batch_b(h, ks):
        batch(h, [(k, j) for k in ks for j in (1, 2)])

    def batch_c(h):
        batch(h, [(k, 3) for k in range(4)])

    subs = n // planes

    def target(way, step):
        return lax.rem(lane + planes + (step - hops if way == 0 else hops - step), planes)

    wing = columns // 2

    def main_copy(h, way, step, p):
        peer = below if way == 0 else above
        src, dst = sendbuf.at[h, way, step, p], recvbuf.at[h, way, step, p]
        if step == 0:
            side = pl.ds(way * wing, wing)
            src = sendbuf.at[h, way, step, p, :, :, side]
            dst = recvbuf.at[h, way, step, p, :, :, side]
        return remote(
            src, dst, main_sent.at[h, way, step, p], main_got.at[h, way, step, p], tp=peer
        )

    def main_step(h, step, p):
        for way in range(2):
            q = target(way, step)
            side = slice(way * wing, (way + 1) * wing)
            other = slice((1 - way) * wing, (2 - way) * wing)
            if step:
                main_copy(h, way, step - 1, p).wait_recv()
            for i in range(2):
                value = part[q * subs + 2 * p + i, whole(h)]
                if step == 0:
                    sendbuf[h, way, 0, p, i, :, side] = value[:, side].astype(jnp.bfloat16)
                elif step == 1:
                    came = recvbuf[h, way, 0, p, i, :, side].astype(jnp.float32)
                    sendbuf[h, way, 1, p, i, :, side] = (value[:, side] + came).astype(jnp.bfloat16)
                    sendbuf[h, way, 1, p, i, :, other] = value[:, other].astype(jnp.bfloat16)
                else:
                    came = recvbuf[h, way, step - 1, p, i].astype(jnp.float32)
                    sendbuf[h, way, step, p, i] = (value + came).astype(jnp.bfloat16)
            main_copy(h, way, step, p).start()

    home_plane = me // subs

    def low_over(h):
        return remote(
            lowsum.at[h], lowz.at[h, lane], low_sent.at[1, h], low_got.at[1, h], tp=home_plane
        )

    def low_first(h):
        arrived(lowrecv.at[h, pl.ds(0, n - 1)], low_got.at[0, h])
        lowrecv[h, me] = lowsend[h, me]
        value = lowrecv[h, 0].astype(jnp.float32)
        for r in range(1, n):
            value = value + lowrecv[h, r].astype(jnp.float32)
        lowsum[h] = value.astype(jnp.bfloat16)

        @pl.when(lane != home_plane)
        def _():
            low_over(h).start()

    def low_spread(h, d):
        place_of = lax.rem(me, subs)
        return remote(
            lowfull.at[h, place_of],
            lowfull.at[h, place_of],
            low_sent.at[2, h],
            full_got.at[h, place_of],
            req=lax.rem(me + d, n),
        )

    def low_second(h):
        @pl.when(lane == home_plane)
        def _():
            arrived(lowz.at[h, pl.ds(0, planes - 1)], low_got.at[1, h])
            lowz[h, lane] = lowsum[h]
            value = lowz[h, 0].astype(jnp.float32)
            for t in range(1, planes):
                value = value + lowz[h, t].astype(jnp.float32)
            lowfull[h, lax.rem(me, subs)] = value.astype(jnp.bfloat16)

            def spread(d, carry):
                low_spread(h, d).start()
                return carry

            lax.fori_loop(1, n, spread, 0)

    def lora(h):
        for sub in range(subs):

            @pl.when(lane * subs + sub != me)
            def _():
                arrived(lowfull.at[h, sub], full_got.at[h, sub])

        pieces, owners = [], []
        for sub in range(subs):
            packed = lowfull[h, sub].astype(jnp.float32)
            turned = pltpu.roll(packed, rank, 1)
            pieces += [jnp.where(narrow, packed, turned), jnp.where(narrow, turned, packed)]
            owners.append(slot_column(lane * subs + sub, h))
        low = jnp.concatenate(pieces, axis=0)
        owner = jnp.concatenate(owners, axis=0)
        side = lax.broadcasted_iota(jnp.int32, low.shape, 1) // rank
        group = 8
        extra[h] = jnp.zeros(extra.shape[1:], jnp.float32)

        def add(g, carry):
            wide = jnp.concatenate(
                [
                    jnp.where(owner == 2 * (g * group + m) + side, low, 0.0).astype(jnp.bfloat16)
                    for m in range(group)
                ],
                axis=1,
            )
            stored = upall[pl.ds(g * group, group)].reshape(group * planes * up_rows, columns)
            extra[h] += jnp.dot(wide, stored, preferred_element_type=jnp.float32)
            return carry

        lax.fori_loop(0, n // group, add, 0)

    def finish(h):
        for sub in range(subs):
            p, i = sub // 2, sub % 2
            rows = pl.ds(sub * chunk_rows + h * half, half)
            value = part[lane * subs + sub, whole(h)] + extra[h, pl.ds(sub * half, half)]
            for way in range(2):
                if i == 0:
                    main_copy(h, way, hops - 1, p).wait_recv()
                value = value + recvbuf[h, way, hops - 1, p, i].astype(jnp.float32)
            out[rows, :] = value.astype(out.dtype)

    def mains(h, step):
        main_step(h, step, 0)
        main_step(h, step, 1)

    pairs = requests // 2
    attend(0, pairs // 4)
    arrived(all_up, many_got.at[2])
    own_up.wait()
    ring(0)
    attend(pairs // 4, pairs // 2)
    open_gather(0)
    attend(pairs // 2, pairs // 2 + 2)
    near(0)
    attend(pairs // 2 + 2, pairs // 2 + 4)
    ring(1)
    turn(0, 0)
    far(0)
    attend(pairs // 2 + 4, pairs // 2 + 6)
    turn(0, 1)
    turn(0, 2)
    attend(pairs // 2 + 6, pairs)
    open_gather(1)
    turn(0, 3)
    last(0, 0)
    last(0, 1)
    ring(2)
    batch_a(0)
    batch_b(0, (0, 1))
    near(1)
    last(0, 2)
    last(0, 3)
    turn(1, 0)
    batch_b(0, (2, 3))
    far(1)
    turn(1, 1)
    ring(3)
    batch_c(0)
    mains(0, 0)
    turn(1, 2)
    batch_a(1)
    turn(1, 3)
    last(1, 0)
    mains(0, 1)
    low_first(0)
    last(1, 1)
    batch_b(1, (0, 1))
    mains(0, 2)
    last(1, 2)
    last(1, 3)
    batch_b(1, (2, 3))
    low_second(0)
    batch_c(1)
    mains(1, 0)
    mains(0, 3)
    ring(4)
    lora(0)
    mains(1, 1)
    low_first(1)
    finish(0)
    mains(1, 2)
    low_second(1)
    mains(1, 3)
    lora(1)
    finish(1)

    arrived(all_labels, many_sent.at[0])
    arrived(all_pages, many_sent.at[1])
    arrived(all_up, many_sent.at[2])
    for way in range(2):
        for hop in range(hops):
            ring_copy(way, hop).wait_send()
    for h in range(HALF_COUNT):
        for way in range(2):
            step_one(h, way).wait_send()
            step_one_half(h, way).wait_send()
            for k in range(4):
                step_two(h, k, way).wait_send()
                relay(h, k, way).wait_send()
            for step in range(hops):
                for p in range(2):
                    main_copy(h, way, step, p).wait_send()
        for k in range(4):
            for j in range(4):
                to_mate(h, k, j).wait_send()
    for h in range(HALF_COUNT):
        arrived(lowsend.at[h, pl.ds(0, n - 1)], low_sent.at[0, h])

        @pl.when(lane != home_plane)
        def _():
            low_over(h).wait_send()

        @pl.when(lane == home_plane)
        def _():
            arrived(lowsend.at[h, pl.ds(0, n - 1)], low_sent.at[2, h])


def layer(n, planes, home, adapter, storage, lengths, queries, incoming, pages, up, weights, down):
    rows, depth = queries.shape
    columns = weights.shape[1]
    hops, subs, half = planes // 2, n // planes, rows // HALF_COUNT
    hbm = pl.BlockSpec(memory_space=pltpu.HBM)
    vmem = pl.BlockSpec(memory_space=pltpu.VMEM)
    smem = pl.BlockSpec(memory_space=pltpu.SMEM)
    dma = pltpu.SemaphoreType.DMA
    bf16, f32, i32 = jnp.bfloat16, jnp.float32, jnp.int32
    hc = HALF_COUNT
    return pl.pallas_call(
        layer_kernel,
        out_shape=jax.ShapeDtypeStruct((n * rows // planes, columns), bf16),
        in_specs=[vmem, smem, smem, smem, smem, vmem, vmem, hbm, hbm, vmem, vmem],
        out_specs=vmem,
        scratch_shapes=[
            pltpu.VMEM((pages.shape[0] + n * CAP, PAGE_ROWS, HEAD_WIDTH), bf16),
            pltpu.VMEM((n * CAP, PAGE_ROWS, HEAD_WIDTH), bf16),
            pltpu.VMEM((n * CAP, PAGE_ROWS, HEAD_WIDTH), bf16),
            pltpu.VMEM((n, 1, HEAD_WIDTH), i32),
            pltpu.VMEM((n, 1, HEAD_WIDTH), i32),
            pltpu.VMEM((n, HEAD_WIDTH), i32),
            pltpu.SMEM((n, HEAD_WIDTH), i32),
            pltpu.VMEM(home.shape, i32),
            pltpu.SMEM(home.shape, i32),
            pltpu.VMEM((rows, depth), f32),
            pltpu.VMEM((rows, depth), bf16),
            pltpu.VMEM((n, planes, up.shape[0] // planes, columns), bf16),
            pltpu.VMEM((n, rows, depth), bf16),
            pltpu.VMEM((n, rows, columns), f32),
            pltpu.VMEM((hc, 2, hops, 2, subs // 2, half, columns), bf16),
            pltpu.VMEM((hc, 2, hops, 2, subs // 2, half, columns), bf16),
            pltpu.VMEM((hc, n, half // 2, HEAD_WIDTH), bf16),
            pltpu.VMEM((hc, n, half // 2, HEAD_WIDTH), bf16),
            pltpu.VMEM((hc, half // 2, HEAD_WIDTH), bf16),
            pltpu.VMEM((hc, planes, half // 2, HEAD_WIDTH), bf16),
            pltpu.VMEM((hc, subs, half // 2, HEAD_WIDTH), bf16),
            pltpu.VMEM((hc, subs * half, columns), f32),
        ]
        + [dma((3,))] * 2
        + [dma((2, hops))] * 2
        + [dma((6,))]
        + [dma((hc, 4))] * 2
        + [dma((hc, 4, 2))] * 4
        + [dma((hc, 4, 4))] * 2
        + [dma((hc, 2, hops, 2))] * 2
        + [dma((3, hc))] * 2
        + [dma((hc, subs))],
        compiler_params=pltpu.CompilerParams(
            collective_id=0, has_side_effects=True, vmem_limit_bytes=VMEM_BYTES
        ),
        name="layer",
    )(home, home, adapter, storage, lengths, queries, incoming, pages, up, weights, down)


def on_device(
    queries,
    incoming_key_value,
    key_value_pages,
    page_request_home,
    lengths,
    request_adapter_index,
    adapter_storage_slot,
    adapter_down_factor,
    adapter_up_factor,
    output_projection_weight,
):
    per_dev = key_value_pages.shape[0]
    own_adapters, depth, rank = adapter_down_factor.shape
    return layer(
        lax.axis_size("req"),
        lax.axis_size("tp"),
        page_request_home.reshape(-1, HEAD_WIDTH),
        request_adapter_index,
        adapter_storage_slot,
        lengths,
        queries,
        incoming_key_value,
        key_value_pages.reshape(per_dev, PAGE_ROWS, HEAD_WIDTH),
        adapter_up_factor.reshape(-1, adapter_up_factor.shape[2]),
        output_projection_weight,
        jnp.transpose(adapter_down_factor, (0, 2, 1)).reshape(own_adapters * rank, depth),
    )


def solution(mesh):
    return jax.shard_map(
        on_device,
        mesh=mesh,
        in_specs=(
            P("req", "tp"),
            P(None, "req", "tp"),
            P("req", None, None, "tp"),
            P("req"),
            P("req"),
            P("req"),
            P(),
            P("req", "tp", None),
            P("req", None, None),
            P("tp", "req"),
        ),
        out_specs=P("tp", "req"),
        check_vma=False,
    )
```

```python
import functools
import math

import jax
import jax.numpy as jnp
from jax import lax
from jax.experimental import pallas as pl
from jax.experimental.pallas import tpu as pltpu
from jax.sharding import PartitionSpec as P

QUERY_HEADS = 64
KEY_VALUE_HEADS = 8
GROUP = QUERY_HEADS // KEY_VALUE_HEADS
HEAD_WIDTH = 128
STEP_COUNT = 4
PAGE_LENGTH = 32
PAGE_ROWS = 2 * PAGE_LENGTH
MAXP = 16
CAP = 2
VMEM_BYTES = 60 * 1024 * 1024


HALF_COUNT = 4


def layer_kernel(
    home, home_s, adapter, storage, lengths, queries, incoming, pages, up, weights, down,
    out,
    cands, inbox, outbox, labels, inlab, sourcev, sources, tablev, table, outf, mixed, upall,
    everyone, part, sendbuf, recvbuf, lowsend, lowrecv, lowsum, lowz, lowfull, extra,
    many_sent, many_got, ring_sent, ring_got, local_sem,
    s1_sent, s1_got, s2_sent, s2_got, relay_sent, relay_got, mate_sent, mate_got,
    main_sent, main_got, low_sent, low_got, full_got,
):
    n, planes = upall.shape[0], upall.shape[1]
    me = lax.axis_index("req")
    lane = lax.axis_index("tp")
    core = lax.rem(me, 2)
    cx, cy = me // 8, lax.rem(me // 2, 4)
    first = cx * (1 - core) + cy * core
    second = cy * (1 - core) + cx * core
    above, below = lax.rem(lane + 1, planes), lax.rem(lane + planes - 1, planes)
    mate = me + 1 - 2 * core
    page_count = pages.shape[0]
    requests = lengths.shape[0]
    columns = out.shape[1]
    chunk_rows = queries.shape[0]
    half = chunk_rows // HALF_COUNT
    quarter = half // 2
    rank = HEAD_WIDTH // 2

    load = pltpu.make_async_copy(pages, cands.at[pl.ds(0, page_count)], local_sem.at[0])
    load.start()
    barrier = pltpu.get_barrier_semaphore()

    def greet(d, carry):
        pl.semaphore_signal(barrier, inc=1, device_id={"req": lax.rem(me + d, n)})
        return carry

    lax.fori_loop(1, n, greet, 0)
    for d in range(1, planes):
        pl.semaphore_signal(barrier, inc=1, device_id={"tp": lax.rem(lane + d, planes)})

    def remote(src, dst, sent_sem, got_sem, **to):
        return pltpu.make_async_remote_copy(src, dst, sent_sem, got_sem, device_id=to)

    def arrived(ref, sem):
        pltpu.make_async_copy(ref, ref, sem).wait()

    shift = n * page_count
    bits = shift.bit_length() - 1
    page_bits = page_count.bit_length() - 1
    peer_row = lax.broadcasted_iota(jnp.int32, (n, HEAD_WIDTH), 0)
    lane_of = lax.broadcasted_iota(jnp.int32, (n, HEAD_WIDTH), 1)
    low_key = jnp.full((n, HEAD_WIDTH), 2 * page_count * shift, jnp.int32)
    high_key = jnp.full((n, HEAD_WIDTH), -1, jnp.int32)
    for i in range(page_count // HEAD_WIDTH):
        homes = jnp.broadcast_to(home[i : i + 1, :], (n, HEAD_WIDTH))
        match = (homes >> page_bits == peer_row) & (peer_row != me)
        key = (lane_of + i * HEAD_WIDTH) * shift + homes
        low_key = jnp.where(match, jnp.minimum(low_key, key), low_key)
        high_key = jnp.where(match, jnp.maximum(high_key, key), high_key)
    least = jnp.min(low_key, axis=1, keepdims=True)
    most = jnp.max(high_key, axis=1, keepdims=True)
    chosen = jnp.where(lane_of == 0, least, most)
    there = ((lane_of == 0) & (most >= 0)) | ((lane_of == 1) & (most > least))
    sourcev[...] = jnp.where(there, jnp.clip(chosen >> bits, 0, page_count - 1), 0)
    to_sources = pltpu.make_async_copy(sourcev, sources, local_sem.at[3 + HALF_COUNT])
    to_sources.start()
    words = jnp.where(there, ((chosen & (shift - 1)) + 1) * 64, 0)
    token_lane = lax.broadcasted_iota(jnp.int32, (1, HEAD_WIDTH), 1)
    slots = jnp.zeros((1, HEAD_WIDTH), jnp.int32)
    for i in range(requests):
        slots = jnp.where(token_lane // STEP_COUNT == i, storage[adapter[i]], slots)
    for i in range(n):
        labels[i] = words[i : i + 1] + slots
    inlab[me] = slots

    place = (
        lax.broadcasted_iota(jnp.int32, tablev.shape, 0) * HEAD_WIDTH
        + lax.broadcasted_iota(jnp.int32, tablev.shape, 1)
        + me * page_count
    )
    run = 16

    def enter_own(i, entries):
        for u in range(run):
            at_home = home_s[i // (HEAD_WIDTH // run), lax.rem(i, HEAD_WIDTH // run) * run + u]
            entries = jnp.where(place == at_home, i * run + u, entries)
        return entries

    own_table = lax.fori_loop(
        0, page_count // run, enter_own, jnp.zeros(tablev.shape, jnp.int32)
    )
    to_sources.wait()
    load.wait()

    def pick(d, carry):
        for k in range(CAP):
            outbox[d * CAP + k] = cands[sources[d, k]]
        return carry

    lax.fori_loop(0, n, pick, 0)
    pl.semaphore_wait(barrier, n + planes - 2)

    up_rows = upall.shape[2]

    def up_part(peer):
        return up.at[
            pl.ds(pl.multiple_of(lane * up_rows, up_rows), up_rows),
            pl.ds(pl.multiple_of(peer * columns, columns), columns),
        ]

    def label_copy(d):
        peer = lax.rem(me + d, n)
        return remote(labels.at[peer], inlab.at[me], many_sent.at[0], many_got.at[0], req=peer)

    def page_copy(d):
        peer = lax.rem(me + d, n)
        return remote(
            outbox.at[pl.ds(peer * CAP, CAP)],
            inbox.at[pl.ds(me * CAP, CAP)],
            many_sent.at[1],
            many_got.at[1],
            req=peer,
        )

    def up_copy(d):
        peer = lax.rem(me + d, n)
        return remote(
            up_part(peer), upall.at[me, lane], many_sent.at[2], many_got.at[2], req=peer
        )

    own_up = pltpu.make_async_copy(up_part(me), upall.at[me, lane], local_sem.at[1])

    def begin_labels(d, carry):
        label_copy(d).start()
        return carry

    def begin_pages(d, carry):
        page_copy(d).start()
        return carry

    def begin_up(d, carry):
        up_copy(d).start()
        return carry

    lax.fori_loop(1, n, begin_labels, 0)
    lax.fori_loop(1, n, begin_pages, 0)
    all_labels = inlab.at[pl.ds(0, n - 1)]
    all_pages = inbox.at[pl.ds(0, (n - 1) * CAP)]
    all_up = upall.at[pl.ds(0, n - 1), 0]

    hops = planes // 2

    def ring_copy(way, hop):
        peer = above if way == 0 else below
        origin = lax.rem(lane + planes + (hop if way == 1 else -hop), planes)
        piece = upall.at[:, origin]
        if hop == hops - 1:
            piece = upall.at[pl.ds(way * (n // 2), n // 2), origin]
        return pltpu.make_async_remote_copy(
            piece, piece, ring_sent.at[way, hop], ring_got.at[way, hop], device_id={"tp": peer}
        )

    def ring(hop):
        for way in range(2):
            if hop:
                ring_copy(way, hop - 1).wait_recv()
            if hop < hops:
                ring_copy(way, hop).start()

    arrived(all_labels, many_got.at[0])
    entries = own_table
    for source in range(n):
        word = inlab[source] >> 6
        for k in range(CAP):
            index = page_count + source * CAP + k
            entries = jnp.where(place + 1 == word[:, k : k + 1], index, entries)
    tablev[...] = entries
    to_scalar = pltpu.make_async_copy(tablev, table, local_sem.at[2])
    to_scalar.start()
    own_up.start()
    lax.fori_loop(1, n, begin_up, 0)
    arrived(all_pages, many_got.at[1])
    take_in = pltpu.make_async_copy(
        inbox, cands.at[pl.ds(page_count, n * CAP)], local_sem.at[0]
    )
    take_in.start()
    to_scalar.wait()
    take_in.wait()

    old = MAXP * PAGE_ROWS
    width = old + HEAD_WIDTH
    rows_q = GROUP * STEP_COUNT
    column = lax.broadcasted_iota(jnp.int32, (rows_q, width), 1)
    step_of = lax.rem(lax.broadcasted_iota(jnp.int32, (rows_q, width), 0), STEP_COUNT)
    is_key = lax.rem(column, 2) == 0
    fresh_at = column - old
    places = [
        jnp.where(
            (fresh_at >= k * STEP_COUNT) & (fresh_at - k * STEP_COUNT <= step_of),
            0,
            jnp.where(is_key & (column < old), column // 2, 1 << 20),
        )
        for k in range(2)
    ]
    scale = math.log2(math.e) / math.sqrt(HEAD_WIDTH)
    filler = jnp.zeros((HEAD_WIDTH - 4 * STEP_COUNT, HEAD_WIDTH), cands.dtype)
    per_row = HEAD_WIDTH // MAXP

    def one(request, query, fresh, position):
        pieces = []
        for j in range(MAXP):
            page = table[request // per_row, lax.rem(request, per_row) * MAXP + j]
            pieces.append(cands[page])
        pieces.append(fresh)
        pieces.append(filler)
        stored = jnp.concatenate(pieces, axis=0)
        scores = lax.dot_general(
            query, stored, (((1,), (1,)), ((), ())), preferred_element_type=jnp.float32
        )
        scores = jnp.where(position < lengths[request], scores, -jnp.inf)
        top = jnp.max(scores, axis=1, keepdims=True)
        exps = jnp.exp2((scores - top) * scale)
        probs = exps * (1.0 / jnp.sum(exps, axis=1, keepdims=True))
        probs = jnp.concatenate(
            [
                pltpu.roll(probs[:, :old], 1, 1),
                pltpu.roll(probs[:, old:], 2 * STEP_COUNT, 1),
            ],
            axis=1,
        ).astype(jnp.bfloat16)
        return jnp.dot(probs, stored, preferred_element_type=jnp.float32)

    def pair(index, carry):
        base = pl.multiple_of(index * 2 * STEP_COUNT, 2 * STEP_COUNT)
        both_q = queries[pl.ds(base, 2 * STEP_COUNT), :].astype(jnp.float32)
        fresh = jnp.concatenate(
            [incoming[i, pl.ds(base, 2 * STEP_COUNT), :].astype(jnp.float32) for i in range(2)],
            axis=0,
        ).astype(jnp.bfloat16)
        results = []
        for k in range(2):
            one_q = both_q[k * STEP_COUNT : (k + 1) * STEP_COUNT]
            query = jnp.concatenate(
                [one_q[:, h * HEAD_WIDTH : (h + 1) * HEAD_WIDTH] for h in range(GROUP)], axis=0
            ).astype(jnp.bfloat16)
            results.append(one(index * 2 + k, query, fresh, places[k]))
        for h in range(GROUP):
            both = jnp.concatenate(
                [m[h * STEP_COUNT : (h + 1) * STEP_COUNT] for m in results], axis=0
            )
            outf[pl.ds(base, 2 * STEP_COUNT), h * HEAD_WIDTH : (h + 1) * HEAD_WIDTH] = both
        return carry

    def attend(start, stop):
        lax.fori_loop(start, stop, pair, 0)

    def spot(f, s, c):
        f, s = lax.rem(f + 8, 4), lax.rem(s + 8, 4)
        return f * (8 - 6 * c) + s * (2 + 6 * c) + c

    def at(df, ds):
        return spot(first + df, second + ds, core)

    def mate_at(df, ds):
        return spot(second + df, first + ds, 1 - core)

    OFFSET = (0, 1, -1, 2)
    DS = (0, -1, 1, 2)

    def whole(h):
        return pl.ds(h * half, half)

    def side_rows(h, way):
        return pl.ds(h * half + way * quarter, quarter)

    def step_one(h, way):
        to = at(1 if way == 0 else -1, 0)
        return remote(
            mixed.at[whole(h)], everyone.at[me, whole(h)],
            s1_sent.at[h, way], s1_got.at[h, way], req=to,
        )

    def step_one_half(h, way):
        ref = everyone.at[at(-1 if way == 0 else 1, 0), side_rows(h, way)]
        to = at(1 if way == 0 else -1, 0)
        return remote(ref, ref, s1_sent.at[h, 2 + way], s1_got.at[h, 2 + way], req=to)

    def step_two(h, k, way):
        ref = everyone.at[at(OFFSET[k], 0), whole(h)]
        src = mixed.at[whole(h)] if k == 0 else ref
        to = at(0, 1 if way == 0 else -1)
        return remote(src, ref, s2_sent.at[h, k, way], s2_got.at[h, k, way], req=to)

    def relay(h, k, way):
        ref = everyone.at[at(OFFSET[k], -1 if way == 0 else 1), side_rows(h, way)]
        to = at(0, 1 if way == 0 else -1)
        return remote(ref, ref, relay_sent.at[h, k, way], relay_got.at[h, k, way], req=to)

    def to_mate(h, k, j):
        ref = everyone.at[at(OFFSET[k], DS[j]), whole(h)]
        src = mixed.at[whole(h)] if k == 0 and j == 0 else ref
        return remote(src, ref, mate_sent.at[h, j, k], mate_got.at[h, j, k], req=mate)

    def got_mate(h, k, j):
        arrived(everyone.at[mate_at(OFFSET[k], DS[j]), whole(h)], mate_got.at[h, j, k])

    def own_copy(h):
        return pltpu.make_async_copy(
            mixed.at[whole(h)], everyone.at[me, whole(h)], local_sem.at[3 + h]
        )

    def open_gather(h):
        rows = pl.ds(h * half, half)
        mixed[rows, :] = outf[rows, :].astype(mixed.dtype)
        for way in range(2):
            step_one(h, way).start()
        for way in range(2):
            step_two(h, 0, way).start()
        to_mate(h, 0, 0).start()
        own_copy(h).start()

    def pass_on(h, k):
        step_two(h, k, 0).start()
        step_two(h, k, 1).start()
        to_mate(h, k, 0).start()

    def near(h):
        for way, k in ((0, 2), (1, 1)):
            arrived(everyone.at[at(OFFSET[k], 0), whole(h)], s1_got.at[h, way])
            step_one_half(h, way).start()
            pass_on(h, k)

    def far(h):
        for way in range(2):
            arrived(everyone.at[at(2, 0), side_rows(h, way)], s1_got.at[h, 2 + way])
        pass_on(h, 3)

    def turn(h, k):
        for way, j in ((0, 1), (1, 2)):
            arrived(everyone.at[at(OFFSET[k], DS[j]), whole(h)], s2_got.at[h, k, way])
            relay(h, k, way).start()
            to_mate(h, k, j).start()

    def last(h, k):
        for way in range(2):
            arrived(everyone.at[at(OFFSET[k], 2), side_rows(h, way)], relay_got.at[h, k, way])
        to_mate(h, k, 3).start()

    row64 = lax.broadcasted_iota(jnp.int32, (half, HEAD_WIDTH), 0)
    col64 = lax.broadcasted_iota(jnp.int32, (half, HEAD_WIDTH), 1)
    narrow = lax.broadcasted_iota(jnp.int32, (quarter, HEAD_WIDTH), 1) < rank
    upper = col64 // rank

    def slot_column(r, h):
        values = (inlab[r] & 63).astype(jnp.float32)
        values = jnp.where(row64 + h * half == col64, values, 0.0)
        return jnp.sum(values, axis=1, keepdims=True).astype(jnp.int32)

    def low_home(h, r):
        return remote(
            lowsend.at[h, r], lowrecv.at[h, me], low_sent.at[0, h], low_got.at[0, h], req=r
        )

    def batch(h, kjs):
        for k, j in kjs:
            got_mate(h, k, j)
        owners = [at(OFFSET[k], DS[j]) for k, j in kjs]
        owners += [mate_at(OFFSET[k], DS[j]) for k, j in kjs]
        rows = jnp.concatenate([everyone[r, whole(h)] for r in owners], axis=0)
        product = jnp.dot(rows, weights[...], preferred_element_type=jnp.float32)
        lows = lax.dot_general(
            rows, down[...], (((1,), (1,)), ((), ())), preferred_element_type=jnp.float32
        )
        for i, r in enumerate(owners):
            cut = slice(i * half, (i + 1) * half)
            part[r, whole(h)] = product[cut]
            low = jnp.where(slot_column(r, h) == 2 * me + upper, lows[cut], 0.0)
            low = low + pltpu.roll(low, rank, 1)
            lowsend[h, r] = jnp.where(narrow, low[:quarter], low[quarter:]).astype(jnp.bfloat16)
        for i, r in enumerate(owners):
            if kjs[0] != (0, 0) or i:
                low_home(h, r).start()

    def batch_a(h):
        own_copy(h).wait()
        batch(h, [(k, 0) for k in range(4)])

    def batch_b(h, ks):
        batch(h, [(k, j) for k in ks for j in (1, 2)])

    def batch_c(h):
        batch(h, [(k, 3) for k in range(4)])

    subs = n // planes

    def target(way, step):
        return lax.rem(lane + planes + (step - hops if way == 0 else hops - step), planes)

    wing = columns // 2

    def main_copy(h, way, step, p):
        peer = below if way == 0 else above
        src, dst = sendbuf.at[h, way, step, p], recvbuf.at[h, way, step, p]
        if step == 0:
            side = pl.ds(way * wing, wing)
            src = sendbuf.at[h, way, step, p, :, :, side]
            dst = recvbuf.at[h, way, step, p, :, :, side]
        return remote(
            src, dst, main_sent.at[h, way, step, p], main_got.at[h, way, step, p], tp=peer
        )

    def main_step(h, step, p):
        for way in range(2):
            q = target(way, step)
            side = slice(way * wing, (way + 1) * wing)
            other = slice((1 - way) * wing, (2 - way) * wing)
            if step:
                main_copy(h, way, step - 1, p).wait_recv()
            for i in range(2):
                value = part[q * subs + 2 * p + i, whole(h)]
                if step == 0:
                    sendbuf[h, way, 0, p, i, :, side] = value[:, side].astype(jnp.bfloat16)
                elif step == 1:
                    came = recvbuf[h, way, 0, p, i, :, side].astype(jnp.float32)
                    sendbuf[h, way, 1, p, i, :, side] = (value[:, side] + came).astype(jnp.bfloat16)
                    sendbuf[h, way, 1, p, i, :, other] = value[:, other].astype(jnp.bfloat16)
                else:
                    came = recvbuf[h, way, step - 1, p, i].astype(jnp.float32)
                    sendbuf[h, way, step, p, i] = (value + came).astype(jnp.bfloat16)
            main_copy(h, way, step, p).start()

    home_plane = me // subs

    def low_over(h):
        return remote(
            lowsum.at[h], lowz.at[h, lane], low_sent.at[1, h], low_got.at[1, h], tp=home_plane
        )

    def low_first(h):
        arrived(lowrecv.at[h, pl.ds(0, n - 1)], low_got.at[0, h])
        lowrecv[h, me] = lowsend[h, me]
        value = lowrecv[h, 0].astype(jnp.float32)
        for r in range(1, n):
            value = value + lowrecv[h, r].astype(jnp.float32)
        lowsum[h] = value.astype(jnp.bfloat16)

        @pl.when(lane != home_plane)
        def _():
            low_over(h).start()

    def low_spread(h, d):
        place_of = lax.rem(me, subs)
        return remote(
            lowfull.at[h, place_of],
            lowfull.at[h, place_of],
            low_sent.at[2, h],
            full_got.at[h, place_of],
            req=lax.rem(me + d, n),
        )

    def low_second(h):
        @pl.when(lane == home_plane)
        def _():
            arrived(lowz.at[h, pl.ds(0, planes - 1)], low_got.at[1, h])
            lowz[h, lane] = lowsum[h]
            value = lowz[h, 0].astype(jnp.float32)
            for t in range(1, planes):
                value = value + lowz[h, t].astype(jnp.float32)
            lowfull[h, lax.rem(me, subs)] = value.astype(jnp.bfloat16)

            def spread(d, carry):
                low_spread(h, d).start()
                return carry

            lax.fori_loop(1, n, spread, 0)

    def lora(h):
        for sub in range(subs):

            @pl.when(lane * subs + sub != me)
            def _():
                arrived(lowfull.at[h, sub], full_got.at[h, sub])

        pieces, owners = [], []
        for sub in range(subs):
            packed = lowfull[h, sub].astype(jnp.float32)
            turned = pltpu.roll(packed, rank, 1)
            pieces += [jnp.where(narrow, packed, turned), jnp.where(narrow, turned, packed)]
            owners.append(slot_column(lane * subs + sub, h))
        low = jnp.concatenate(pieces, axis=0)
        owner = jnp.concatenate(owners, axis=0)
        side = lax.broadcasted_iota(jnp.int32, low.shape, 1) // rank
        group = 8
        extra[h] = jnp.zeros(extra.shape[1:], jnp.float32)

        def add(g, carry):
            wide = jnp.concatenate(
                [
                    jnp.where(owner == 2 * (g * group + m) + side, low, 0.0).astype(jnp.bfloat16)
                    for m in range(group)
                ],
                axis=1,
            )
            stored = upall[pl.ds(g * group, group)].reshape(group * planes * up_rows, columns)
            extra[h] += jnp.dot(wide, stored, preferred_element_type=jnp.float32)
            return carry

        lax.fori_loop(0, n // group, add, 0)

    def finish(h):
        for sub in range(subs):
            p, i = sub // 2, sub % 2
            rows = pl.ds(sub * chunk_rows + h * half, half)
            value = part[lane * subs + sub, whole(h)] + extra[h, pl.ds(sub * half, half)]
            for way in range(2):
                if i == 0:
                    main_copy(h, way, hops - 1, p).wait_recv()
                value = value + recvbuf[h, way, hops - 1, p, i].astype(jnp.float32)
            out[rows, :] = value.astype(out.dtype)

    def mains(h, step):
        main_step(h, step, 0)
        main_step(h, step, 1)

    def mains(h, step):
        main_step(h, step, 0)
        main_step(h, step, 1)

    attend(0, 4)
    arrived(all_up, many_got.at[2])
    own_up.wait()
    ring(0)
    open_gather(0)
    attend(4, 8)
    near(0)
    turn(0, 0)
    open_gather(1)
    attend(8, 12)
    far(0)
    turn(0, 1)
    turn(0, 2)
    ring(1)
    near(1)
    last(0, 0)
    open_gather(2)
    attend(12, 14)
    turn(1, 0)
    attend(14, 16)
    last(0, 1)
    last(0, 2)
    turn(0, 3)
    far(1)
    near(2)
    turn(1, 2)
    open_gather(3)
    batch_a(0)
    batch_b(0, (0, 1))
    turn(1, 1)
    turn(2, 0)
    last(1, 0)
    batch_b(0, (2, 3))
    last(0, 3)
    ring(2)
    far(2)
    batch_a(1)
    turn(1, 3)
    near(3)
    batch_b(1, (0, 1))
    turn(2, 2)
    batch_c(0)
    last(1, 2)
    turn(2, 1)
    mains(0, 0)
    batch_a(2)
    far(3)
    batch_b(1, (2, 3))
    turn(3, 0)
    last(1, 1)
    last(2, 0)
    turn(2, 3)
    batch_b(2, (0, 1))
    last(1, 3)
    batch_a(3)
    turn(3, 2)
    ring(3)
    turn(3, 1)
    batch_b(2, (2, 3))
    last(2, 2)
    mains(0, 1)
    last(2, 1)
    batch_c(1)
    mains(1, 0)
    turn(3, 3)
    last(3, 0)
    low_first(0)
    batch_b(3, (0, 1))
    last(2, 3)
    last(3, 2)
    last(3, 1)
    batch_b(3, (2, 3))
    last(3, 3)
    ring(4)
    batch_c(2)
    mains(2, 0)
    mains(0, 2)
    low_second(0)
    mains(1, 1)
    batch_c(3)
    mains(3, 0)
    mains(2, 1)
    low_first(1)
    mains(0, 3)
    mains(1, 2)
    mains(3, 1)
    lora(0)
    low_second(1)
    low_first(2)
    mains(2, 2)
    finish(0)
    low_first(3)
    mains(1, 3)
    mains(3, 2)
    low_second(2)
    mains(2, 3)
    low_second(3)
    lora(1)
    finish(1)
    mains(3, 3)
    lora(2)
    finish(2)
    lora(3)
    finish(3)

    arrived(all_labels, many_sent.at[0])
    arrived(all_pages, many_sent.at[1])
    arrived(all_up, many_sent.at[2])
    for way in range(2):
        for hop in range(hops):
            ring_copy(way, hop).wait_send()
    for h in range(HALF_COUNT):
        for way in range(2):
            step_one(h, way).wait_send()
            step_one_half(h, way).wait_send()
            for k in range(4):
                step_two(h, k, way).wait_send()
                relay(h, k, way).wait_send()
            for step in range(hops):
                for p in range(2):
                    main_copy(h, way, step, p).wait_send()
        for k in range(4):
            for j in range(4):
                to_mate(h, k, j).wait_send()
    for h in range(HALF_COUNT):
        arrived(lowsend.at[h, pl.ds(0, n - 1)], low_sent.at[0, h])

        @pl.when(lane != home_plane)
        def _():
            low_over(h).wait_send()

        @pl.when(lane == home_plane)
        def _():
            arrived(lowsend.at[h, pl.ds(0, n - 1)], low_sent.at[2, h])


def layer(n, planes, home, adapter, storage, lengths, queries, incoming, pages, up, weights, down):
    rows, depth = queries.shape
    columns = weights.shape[1]
    hops, subs, half = planes // 2, n // planes, rows // HALF_COUNT
    hbm = pl.BlockSpec(memory_space=pltpu.HBM)
    vmem = pl.BlockSpec(memory_space=pltpu.VMEM)
    smem = pl.BlockSpec(memory_space=pltpu.SMEM)
    dma = pltpu.SemaphoreType.DMA
    bf16, f32, i32 = jnp.bfloat16, jnp.float32, jnp.int32
    hc = HALF_COUNT
    return pl.pallas_call(
        layer_kernel,
        out_shape=jax.ShapeDtypeStruct((n * rows // planes, columns), bf16),
        in_specs=[vmem, smem, smem, smem, smem, vmem, vmem, hbm, hbm, vmem, vmem],
        out_specs=vmem,
        scratch_shapes=[
            pltpu.VMEM((pages.shape[0] + n * CAP, PAGE_ROWS, HEAD_WIDTH), bf16),
            pltpu.VMEM((n * CAP, PAGE_ROWS, HEAD_WIDTH), bf16),
            pltpu.VMEM((n * CAP, PAGE_ROWS, HEAD_WIDTH), bf16),
            pltpu.VMEM((n, 1, HEAD_WIDTH), i32),
            pltpu.VMEM((n, 1, HEAD_WIDTH), i32),
            pltpu.VMEM((n, HEAD_WIDTH), i32),
            pltpu.SMEM((n, HEAD_WIDTH), i32),
            pltpu.VMEM(home.shape, i32),
            pltpu.SMEM(home.shape, i32),
            pltpu.VMEM((rows, depth), f32),
            pltpu.VMEM((rows, depth), bf16),
            pltpu.VMEM((n, planes, up.shape[0] // planes, columns), bf16),
            pltpu.VMEM((n, rows, depth), bf16),
            pltpu.VMEM((n, rows, columns), f32),
            pltpu.VMEM((hc, 2, hops, 2, subs // 2, half, columns), bf16),
            pltpu.VMEM((hc, 2, hops, 2, subs // 2, half, columns), bf16),
            pltpu.VMEM((hc, n, half // 2, HEAD_WIDTH), bf16),
            pltpu.VMEM((hc, n, half // 2, HEAD_WIDTH), bf16),
            pltpu.VMEM((hc, half // 2, HEAD_WIDTH), bf16),
            pltpu.VMEM((hc, planes, half // 2, HEAD_WIDTH), bf16),
            pltpu.VMEM((hc, subs, half // 2, HEAD_WIDTH), bf16),
            pltpu.VMEM((hc, subs * half, columns), f32),
        ]
        + [dma((3,))] * 2
        + [dma((2, hops))] * 2
        + [dma((4 + HALF_COUNT,))]
        + [dma((hc, 4))] * 2
        + [dma((hc, 4, 2))] * 4
        + [dma((hc, 4, 4))] * 2
        + [dma((hc, 2, hops, 2))] * 2
        + [dma((3, hc))] * 2
        + [dma((hc, subs))],
        compiler_params=pltpu.CompilerParams(
            collective_id=0, has_side_effects=True, vmem_limit_bytes=VMEM_BYTES
        ),
        name="layer",
    )(home, home, adapter, storage, lengths, queries, incoming, pages, up, weights, down)


def on_device(
    queries,
    incoming_key_value,
    key_value_pages,
    page_request_home,
    lengths,
    request_adapter_index,
    adapter_storage_slot,
    adapter_down_factor,
    adapter_up_factor,
    output_projection_weight,
):
    per_dev = key_value_pages.shape[0]
    own_adapters, depth, rank = adapter_down_factor.shape
    return layer(
        lax.axis_size("req"),
        lax.axis_size("tp"),
        page_request_home.reshape(-1, HEAD_WIDTH),
        request_adapter_index,
        adapter_storage_slot,
        lengths,
        queries,
        incoming_key_value,
        key_value_pages.reshape(per_dev, PAGE_ROWS, HEAD_WIDTH),
        adapter_up_factor.reshape(-1, adapter_up_factor.shape[2]),
        output_projection_weight,
        jnp.transpose(adapter_down_factor, (0, 2, 1)).reshape(own_adapters * rank, depth),
    )


def solution(mesh):
    return jax.shard_map(
        on_device,
        mesh=mesh,
        in_specs=(
            P("req", "tp"),
            P(None, "req", "tp"),
            P("req", None, None, "tp"),
            P("req"),
            P("req"),
            P("req"),
            P(),
            P("req", "tp", None),
            P("req", None, None),
            P("tp", "req"),
        ),
        out_specs=P("tp", "req"),
        check_vma=False,
    )
```

```python
import functools
import math

import jax
import jax.numpy as jnp
from jax import lax
from jax.experimental import pallas as pl
from jax.experimental.pallas import tpu as pltpu
from jax.sharding import PartitionSpec as P

QUERY_HEADS = 64
KEY_VALUE_HEADS = 8
GROUP = QUERY_HEADS // KEY_VALUE_HEADS
HEAD_WIDTH = 128
STEP_COUNT = 4
PAGE_LENGTH = 32
PAGE_ROWS = 2 * PAGE_LENGTH
MAXP = 16
CAP = 2
VMEM_BYTES = 60 * 1024 * 1024


HALF_COUNT = 4


def layer_kernel(
    home, home_s, adapter, storage, lengths, queries, incoming, pages, up, weights, down,
    out,
    cands, inbox, outbox, labels, inlab, sourcev, sources, tablev, table, outf, mixed, upall,
    everyone, part, sendbuf, recvbuf, lowsend, lowrecv, lowsum, lowz, lowfull, extra,
    many_sent, many_got, ring_sent, ring_got, local_sem,
    s1_sent, s1_got, s2_sent, s2_got, relay_sent, relay_got, mate_sent, mate_got,
    main_sent, main_got, low_sent, low_got, full_got,
):
    n, planes = upall.shape[0], upall.shape[1]
    me = lax.axis_index("req")
    lane = lax.axis_index("tp")
    core = lax.rem(me, 2)
    cx, cy = me // 8, lax.rem(me // 2, 4)
    first = cx * (1 - core) + cy * core
    second = cy * (1 - core) + cx * core
    above, below = lax.rem(lane + 1, planes), lax.rem(lane + planes - 1, planes)
    mate = me + 1 - 2 * core
    page_count = pages.shape[0]
    requests = lengths.shape[0]
    columns = out.shape[1]
    chunk_rows = queries.shape[0]
    half = chunk_rows // HALF_COUNT
    quarter = half // 2
    rank = HEAD_WIDTH // 2

    load = pltpu.make_async_copy(pages, cands.at[pl.ds(0, page_count)], local_sem.at[0])
    load.start()
    barrier = pltpu.get_barrier_semaphore()

    def greet(d, carry):
        pl.semaphore_signal(barrier, inc=1, device_id={"req": lax.rem(me + d, n)})
        return carry

    lax.fori_loop(1, n, greet, 0)
    for d in range(1, planes):
        pl.semaphore_signal(barrier, inc=1, device_id={"tp": lax.rem(lane + d, planes)})

    def remote(src, dst, sent_sem, got_sem, **to):
        return pltpu.make_async_remote_copy(src, dst, sent_sem, got_sem, device_id=to)

    def arrived(ref, sem):
        pltpu.make_async_copy(ref, ref, sem).wait()

    shift = n * page_count
    bits = shift.bit_length() - 1
    page_bits = page_count.bit_length() - 1
    peer_row = lax.broadcasted_iota(jnp.int32, (n, HEAD_WIDTH), 0)
    lane_of = lax.broadcasted_iota(jnp.int32, (n, HEAD_WIDTH), 1)
    low_key = jnp.full((n, HEAD_WIDTH), 2 * page_count * shift, jnp.int32)
    high_key = jnp.full((n, HEAD_WIDTH), -1, jnp.int32)
    for i in range(page_count // HEAD_WIDTH):
        homes = jnp.broadcast_to(home[i : i + 1, :], (n, HEAD_WIDTH))
        match = (homes >> page_bits == peer_row) & (peer_row != me)
        key = (lane_of + i * HEAD_WIDTH) * shift + homes
        low_key = jnp.where(match, jnp.minimum(low_key, key), low_key)
        high_key = jnp.where(match, jnp.maximum(high_key, key), high_key)
    least = jnp.min(low_key, axis=1, keepdims=True)
    most = jnp.max(high_key, axis=1, keepdims=True)
    chosen = jnp.where(lane_of == 0, least, most)
    there = ((lane_of == 0) & (most >= 0)) | ((lane_of == 1) & (most > least))
    sourcev[...] = jnp.where(there, jnp.clip(chosen >> bits, 0, page_count - 1), 0)
    to_sources = pltpu.make_async_copy(sourcev, sources, local_sem.at[3 + HALF_COUNT])
    to_sources.start()
    words = jnp.where(there, ((chosen & (shift - 1)) + 1) * 64, 0)
    token_lane = lax.broadcasted_iota(jnp.int32, (1, HEAD_WIDTH), 1)
    slots = jnp.zeros((1, HEAD_WIDTH), jnp.int32)
    for i in range(requests):
        slots = jnp.where(token_lane // STEP_COUNT == i, storage[adapter[i]], slots)
    for i in range(n):
        labels[i] = words[i : i + 1] + slots
    inlab[me] = slots

    place = (
        lax.broadcasted_iota(jnp.int32, tablev.shape, 0) * HEAD_WIDTH
        + lax.broadcasted_iota(jnp.int32, tablev.shape, 1)
        + me * page_count
    )
    run = 16

    def enter_own(i, entries):
        for u in range(run):
            at_home = home_s[i // (HEAD_WIDTH // run), lax.rem(i, HEAD_WIDTH // run) * run + u]
            entries = jnp.where(place == at_home, i * run + u, entries)
        return entries

    own_table = lax.fori_loop(
        0, page_count // run, enter_own, jnp.zeros(tablev.shape, jnp.int32)
    )
    to_sources.wait()
    load.wait()

    def pick(d, carry):
        for k in range(CAP):
            outbox[d * CAP + k] = cands[sources[d, k]]
        return carry

    lax.fori_loop(0, n, pick, 0)
    pl.semaphore_wait(barrier, n + planes - 2)

    up_rows = upall.shape[2]

    def up_part(peer):
        return up.at[
            pl.ds(pl.multiple_of(lane * up_rows, up_rows), up_rows),
            pl.ds(pl.multiple_of(peer * columns, columns), columns),
        ]

    def label_copy(d):
        peer = lax.rem(me + d, n)
        return remote(labels.at[peer], inlab.at[me], many_sent.at[0], many_got.at[0], req=peer)

    def page_copy(d):
        peer = lax.rem(me + d, n)
        return remote(
            outbox.at[pl.ds(peer * CAP, CAP)],
            inbox.at[pl.ds(me * CAP, CAP)],
            many_sent.at[1],
            many_got.at[1],
            req=peer,
        )

    def up_copy(d):
        peer = lax.rem(me + d, n)
        return remote(
            up_part(peer), upall.at[me, lane], many_sent.at[2], many_got.at[2], req=peer
        )

    own_up = pltpu.make_async_copy(up_part(me), upall.at[me, lane], local_sem.at[1])

    def begin_labels(d, carry):
        label_copy(d).start()
        return carry

    def begin_pages(d, carry):
        page_copy(d).start()
        return carry

    def begin_up(d, carry):
        up_copy(d).start()
        return carry

    lax.fori_loop(1, n, begin_labels, 0)
    lax.fori_loop(1, n, begin_pages, 0)
    all_labels = inlab.at[pl.ds(0, n - 1)]
    all_pages = inbox.at[pl.ds(0, (n - 1) * CAP)]
    all_up = upall.at[pl.ds(0, n - 1), 0]

    hops = planes // 2

    def ring_copy(way, hop):
        peer = above if way == 0 else below
        origin = lax.rem(lane + planes + (hop if way == 1 else -hop), planes)
        piece = upall.at[:, origin]
        if hop == hops - 1:
            piece = upall.at[pl.ds(way * (n // 2), n // 2), origin]
        return pltpu.make_async_remote_copy(
            piece, piece, ring_sent.at[way, hop], ring_got.at[way, hop], device_id={"tp": peer}
        )

    def ring(hop):
        for way in range(2):
            if hop:
                ring_copy(way, hop - 1).wait_recv()
            if hop < hops:
                ring_copy(way, hop).start()

    arrived(all_labels, many_got.at[0])
    entries = own_table
    for source in range(n):
        word = inlab[source] >> 6
        for k in range(CAP):
            index = page_count + source * CAP + k
            entries = jnp.where(place + 1 == word[:, k : k + 1], index, entries)
    tablev[...] = entries
    to_scalar = pltpu.make_async_copy(tablev, table, local_sem.at[2])
    to_scalar.start()
    own_up.start()
    lax.fori_loop(1, n, begin_up, 0)
    arrived(all_pages, many_got.at[1])
    take_in = pltpu.make_async_copy(
        inbox, cands.at[pl.ds(page_count, n * CAP)], local_sem.at[0]
    )
    take_in.start()
    to_scalar.wait()
    take_in.wait()

    old = MAXP * PAGE_ROWS
    width = old + HEAD_WIDTH
    rows_q = GROUP * STEP_COUNT
    column = lax.broadcasted_iota(jnp.int32, (rows_q, width), 1)
    step_of = lax.rem(lax.broadcasted_iota(jnp.int32, (rows_q, width), 0), STEP_COUNT)
    is_key = lax.rem(column, 2) == 0
    fresh_at = column - old
    places = [
        jnp.where(
            (fresh_at >= k * STEP_COUNT) & (fresh_at - k * STEP_COUNT <= step_of),
            0,
            jnp.where(is_key & (column < old), column // 2, 1 << 20),
        )
        for k in range(2)
    ]
    scale = math.log2(math.e) / math.sqrt(HEAD_WIDTH)
    filler = jnp.zeros((HEAD_WIDTH - 4 * STEP_COUNT, HEAD_WIDTH), cands.dtype)
    per_row = HEAD_WIDTH // MAXP

    def one(request, query, fresh, position):
        pieces = []
        for j in range(MAXP):
            page = table[request // per_row, lax.rem(request, per_row) * MAXP + j]
            pieces.append(cands[page])
        pieces.append(fresh)
        pieces.append(filler)
        stored = jnp.concatenate(pieces, axis=0)
        scores = lax.dot_general(
            query, stored, (((1,), (1,)), ((), ())), preferred_element_type=jnp.float32
        )
        scores = jnp.where(position < lengths[request], scores, -jnp.inf)
        top = jnp.max(scores, axis=1, keepdims=True)
        exps = jnp.exp2((scores - top) * scale)
        probs = exps * (1.0 / jnp.sum(exps, axis=1, keepdims=True))
        probs = jnp.concatenate(
            [
                pltpu.roll(probs[:, :old], 1, 1),
                pltpu.roll(probs[:, old:], 2 * STEP_COUNT, 1),
            ],
            axis=1,
        ).astype(jnp.bfloat16)
        return jnp.dot(probs, stored, preferred_element_type=jnp.float32)

    def pair(index, carry):
        base = pl.multiple_of(index * 2 * STEP_COUNT, 2 * STEP_COUNT)
        both_q = queries[pl.ds(base, 2 * STEP_COUNT), :].astype(jnp.float32)
        fresh = jnp.concatenate(
            [incoming[i, pl.ds(base, 2 * STEP_COUNT), :].astype(jnp.float32) for i in range(2)],
            axis=0,
        ).astype(jnp.bfloat16)
        results = []
        for k in range(2):
            one_q = both_q[k * STEP_COUNT : (k + 1) * STEP_COUNT]
            query = jnp.concatenate(
                [one_q[:, h * HEAD_WIDTH : (h + 1) * HEAD_WIDTH] for h in range(GROUP)], axis=0
            ).astype(jnp.bfloat16)
            results.append(one(index * 2 + k, query, fresh, places[k]))
        for h in range(GROUP):
            both = jnp.concatenate(
                [m[h * STEP_COUNT : (h + 1) * STEP_COUNT] for m in results], axis=0
            )
            outf[pl.ds(base, 2 * STEP_COUNT), h * HEAD_WIDTH : (h + 1) * HEAD_WIDTH] = both
        return carry

    def attend(start, stop):
        lax.fori_loop(start, stop, pair, 0)

    def spot(f, s, c):
        f, s = lax.rem(f + 8, 4), lax.rem(s + 8, 4)
        return f * (8 - 6 * c) + s * (2 + 6 * c) + c

    def at(df, ds):
        return spot(first + df, second + ds, core)

    def mate_at(df, ds):
        return spot(second + df, first + ds, 1 - core)

    OFFSET = (0, 1, -1, 2)
    DS = (0, -1, 1, 2)

    def whole(h):
        return pl.ds(h * half, half)

    def side_rows(h, way):
        return pl.ds(h * half + way * quarter, quarter)

    def step_one(h, way):
        to = at(1 if way == 0 else -1, 0)
        return remote(
            mixed.at[whole(h)], everyone.at[me, whole(h)],
            s1_sent.at[h, way], s1_got.at[h, way], req=to,
        )

    def step_one_half(h, way):
        ref = everyone.at[at(-1 if way == 0 else 1, 0), side_rows(h, way)]
        to = at(1 if way == 0 else -1, 0)
        return remote(ref, ref, s1_sent.at[h, 2 + way], s1_got.at[h, 2 + way], req=to)

    def step_two(h, k, way):
        ref = everyone.at[at(OFFSET[k], 0), whole(h)]
        src = mixed.at[whole(h)] if k == 0 else ref
        to = at(0, 1 if way == 0 else -1)
        return remote(src, ref, s2_sent.at[h, k, way], s2_got.at[h, k, way], req=to)

    def relay(h, k, way):
        ref = everyone.at[at(OFFSET[k], -1 if way == 0 else 1), side_rows(h, way)]
        to = at(0, 1 if way == 0 else -1)
        return remote(ref, ref, relay_sent.at[h, k, way], relay_got.at[h, k, way], req=to)

    def to_mate(h, k, j):
        ref = everyone.at[at(OFFSET[k], DS[j]), whole(h)]
        src = mixed.at[whole(h)] if k == 0 and j == 0 else ref
        return remote(src, ref, mate_sent.at[h, j, k], mate_got.at[h, j, k], req=mate)

    def got_mate(h, k, j):
        arrived(everyone.at[mate_at(OFFSET[k], DS[j]), whole(h)], mate_got.at[h, j, k])

    def own_copy(h):
        return pltpu.make_async_copy(
            mixed.at[whole(h)], everyone.at[me, whole(h)], local_sem.at[3 + h]
        )

    def open_gather(h):
        rows = pl.ds(h * half, half)
        mixed[rows, :] = outf[rows, :].astype(mixed.dtype)
        for way in range(2):
            step_one(h, way).start()
        for way in range(2):
            step_two(h, 0, way).start()
        to_mate(h, 0, 0).start()
        own_copy(h).start()

    def pass_on(h, k):
        step_two(h, k, 0).start()
        step_two(h, k, 1).start()
        to_mate(h, k, 0).start()

    def near(h):
        for way, k in ((0, 2), (1, 1)):
            arrived(everyone.at[at(OFFSET[k], 0), whole(h)], s1_got.at[h, way])
            step_one_half(h, way).start()
            pass_on(h, k)

    def far(h):
        for way in range(2):
            arrived(everyone.at[at(2, 0), side_rows(h, way)], s1_got.at[h, 2 + way])
        pass_on(h, 3)

    def turn(h, k):
        for way, j in ((0, 1), (1, 2)):
            arrived(everyone.at[at(OFFSET[k], DS[j]), whole(h)], s2_got.at[h, k, way])
            relay(h, k, way).start()
            to_mate(h, k, j).start()

    def last(h, k):
        for way in range(2):
            arrived(everyone.at[at(OFFSET[k], 2), side_rows(h, way)], relay_got.at[h, k, way])
        to_mate(h, k, 3).start()

    row64 = lax.broadcasted_iota(jnp.int32, (half, HEAD_WIDTH), 0)
    col64 = lax.broadcasted_iota(jnp.int32, (half, HEAD_WIDTH), 1)
    narrow = lax.broadcasted_iota(jnp.int32, (quarter, HEAD_WIDTH), 1) < rank
    upper = col64 // rank

    def slot_column(r, h):
        values = (inlab[r] & 63).astype(jnp.float32)
        values = jnp.where(row64 + h * half == col64, values, 0.0)
        return jnp.sum(values, axis=1, keepdims=True).astype(jnp.int32)

    def low_home(h, r):
        return remote(
            lowsend.at[h, r], lowrecv.at[h, me], low_sent.at[0, h], low_got.at[0, h], req=r
        )

    def batch(h, kjs):
        for k, j in kjs:
            got_mate(h, k, j)
        owners = [at(OFFSET[k], DS[j]) for k, j in kjs]
        owners += [mate_at(OFFSET[k], DS[j]) for k, j in kjs]
        rows = jnp.concatenate([everyone[r, whole(h)] for r in owners], axis=0)
        product = jnp.dot(rows, weights[...], preferred_element_type=jnp.float32)
        lows = lax.dot_general(
            rows, down[...], (((1,), (1,)), ((), ())), preferred_element_type=jnp.float32
        )
        for i, r in enumerate(owners):
            cut = slice(i * half, (i + 1) * half)
            part[r, whole(h)] = product[cut]
            low = jnp.where(slot_column(r, h) == 2 * me + upper, lows[cut], 0.0)
            low = low + pltpu.roll(low, rank, 1)
            lowsend[h, r] = jnp.where(narrow, low[:quarter], low[quarter:]).astype(jnp.bfloat16)
        for i, r in enumerate(owners):
            if kjs[0] != (0, 0) or i:
                low_home(h, r).start()

    def batch_a(h):
        own_copy(h).wait()
        batch(h, [(k, 0) for k in range(4)])

    def batch_b(h, ks):
        batch(h, [(k, j) for k in ks for j in (1, 2)])

    def batch_c(h):
        batch(h, [(k, 3) for k in range(4)])

    subs = n // planes

    def target(way, step):
        return lax.rem(lane + planes + (step - hops if way == 0 else hops - step), planes)

    wing = columns // 2

    def main_copy(h, way, step, p):
        peer = below if way == 0 else above
        src, dst = sendbuf.at[h, way, step, p], recvbuf.at[h, way, step, p]
        if step == 0:
            side = pl.ds(way * wing, wing)
            src = sendbuf.at[h, way, step, p, :, :, side]
            dst = recvbuf.at[h, way, step, p, :, :, side]
        return remote(
            src, dst, main_sent.at[h, way, step, p], main_got.at[h, way, step, p], tp=peer
        )

    def main_step(h, step, p):
        for way in range(2):
            q = target(way, step)
            side = slice(way * wing, (way + 1) * wing)
            other = slice((1 - way) * wing, (2 - way) * wing)
            if step:
                main_copy(h, way, step - 1, p).wait_recv()
            for i in range(2):
                value = part[q * subs + 2 * p + i, whole(h)]
                if step == 0:
                    sendbuf[h, way, 0, p, i, :, side] = value[:, side].astype(jnp.bfloat16)
                elif step == 1:
                    came = recvbuf[h, way, 0, p, i, :, side].astype(jnp.float32)
                    sendbuf[h, way, 1, p, i, :, side] = (value[:, side] + came).astype(jnp.bfloat16)
                    sendbuf[h, way, 1, p, i, :, other] = value[:, other].astype(jnp.bfloat16)
                else:
                    came = recvbuf[h, way, step - 1, p, i].astype(jnp.float32)
                    sendbuf[h, way, step, p, i] = (value + came).astype(jnp.bfloat16)
            main_copy(h, way, step, p).start()

    home_plane = me // subs

    def low_over(h):
        return remote(
            lowsum.at[h], lowz.at[h, lane], low_sent.at[1, h], low_got.at[1, h], tp=home_plane
        )

    def low_first(h):
        arrived(lowrecv.at[h, pl.ds(0, n - 1)], low_got.at[0, h])
        lowrecv[h, me] = lowsend[h, me]
        value = lowrecv[h, 0].astype(jnp.float32)
        for r in range(1, n):
            value = value + lowrecv[h, r].astype(jnp.float32)
        lowsum[h] = value.astype(jnp.bfloat16)

        @pl.when(lane != home_plane)
        def _():
            low_over(h).start()

    def low_spread(h, d):
        place_of = lax.rem(me, subs)
        return remote(
            lowfull.at[h, place_of],
            lowfull.at[h, place_of],
            low_sent.at[2, h],
            full_got.at[h, place_of],
            req=lax.rem(me + d, n),
        )

    def low_second(h):
        @pl.when(lane == home_plane)
        def _():
            arrived(lowz.at[h, pl.ds(0, planes - 1)], low_got.at[1, h])
            lowz[h, lane] = lowsum[h]
            value = lowz[h, 0].astype(jnp.float32)
            for t in range(1, planes):
                value = value + lowz[h, t].astype(jnp.float32)
            lowfull[h, lax.rem(me, subs)] = value.astype(jnp.bfloat16)

            def spread(d, carry):
                low_spread(h, d).start()
                return carry

            lax.fori_loop(1, n, spread, 0)

    def lora(h):
        for sub in range(subs):

            @pl.when(lane * subs + sub != me)
            def _():
                arrived(lowfull.at[h, sub], full_got.at[h, sub])

        pieces, owners = [], []
        for sub in range(subs):
            packed = lowfull[h, sub].astype(jnp.float32)
            turned = pltpu.roll(packed, rank, 1)
            pieces += [jnp.where(narrow, packed, turned), jnp.where(narrow, turned, packed)]
            owners.append(slot_column(lane * subs + sub, h))
        low = jnp.concatenate(pieces, axis=0)
        owner = jnp.concatenate(owners, axis=0)
        side = lax.broadcasted_iota(jnp.int32, low.shape, 1) // rank
        group = 8
        extra[h] = jnp.zeros(extra.shape[1:], jnp.float32)

        def add(g, carry):
            wide = jnp.concatenate(
                [
                    jnp.where(owner == 2 * (g * group + m) + side, low, 0.0).astype(jnp.bfloat16)
                    for m in range(group)
                ],
                axis=1,
            )
            stored = upall[pl.ds(g * group, group)].reshape(group * planes * up_rows, columns)
            extra[h] += jnp.dot(wide, stored, preferred_element_type=jnp.float32)
            return carry

        lax.fori_loop(0, n // group, add, 0)

    def finish(h):
        for sub in range(subs):
            p, i = sub // 2, sub % 2
            rows = pl.ds(sub * chunk_rows + h * half, half)
            value = part[lane * subs + sub, whole(h)] + extra[h, pl.ds(sub * half, half)]
            for way in range(2):
                if i == 0:
                    main_copy(h, way, hops - 1, p).wait_recv()
                value = value + recvbuf[h, way, hops - 1, p, i].astype(jnp.float32)
            out[rows, :] = value.astype(out.dtype)

    def mains(h, step):
        main_step(h, step, 0)
        main_step(h, step, 1)

    def mains(h, step):
        main_step(h, step, 0)
        main_step(h, step, 1)

    attend(0, 4)
    arrived(all_up, many_got.at[2])
    own_up.wait()
    ring(0)
    open_gather(0)
    attend(4, 8)
    near(0)
    turn(0, 0)
    open_gather(1)
    attend(8, 12)
    far(0)
    turn(0, 1)
    turn(0, 2)
    ring(1)
    near(1)
    last(0, 0)
    open_gather(2)
    attend(12, 14)
    turn(1, 0)
    attend(14, 16)
    last(0, 1)
    last(0, 2)
    turn(0, 3)
    far(1)
    near(2)
    turn(1, 2)
    open_gather(3)
    batch_a(0)
    batch_b(0, (0, 1))
    turn(1, 1)
    turn(2, 0)
    last(1, 0)
    batch_b(0, (2, 3))
    last(0, 3)
    ring(2)
    far(2)
    batch_a(1)
    turn(1, 3)
    near(3)
    batch_b(1, (0, 1))
    turn(2, 2)
    batch_c(0)
    last(1, 2)
    turn(2, 1)
    mains(0, 0)
    batch_a(2)
    far(3)
    batch_b(1, (2, 3))
    turn(3, 0)
    last(1, 1)
    last(2, 0)
    turn(2, 3)
    batch_b(2, (0, 1))
    last(1, 3)
    batch_a(3)
    turn(3, 2)
    ring(3)
    turn(3, 1)
    batch_b(2, (2, 3))
    last(2, 2)
    mains(0, 1)
    last(2, 1)
    batch_c(1)
    mains(1, 0)
    turn(3, 3)
    last(3, 0)
    low_first(0)
    batch_b(3, (0, 1))
    last(2, 3)
    last(3, 2)
    last(3, 1)
    batch_b(3, (2, 3))
    last(3, 3)
    ring(4)
    batch_c(2)
    mains(2, 0)
    mains(0, 2)
    low_second(0)
    mains(1, 1)
    batch_c(3)
    mains(3, 0)
    low_first(1)
    mains(2, 1)
    mains(0, 3)
    mains(1, 2)
    low_second(1)
    low_first(2)
    mains(3, 1)
    low_first(3)
    lora(0)
    finish(0)
    low_second(2)
    mains(2, 2)
    mains(1, 3)
    low_second(3)
    mains(3, 2)
    mains(2, 3)
    lora(1)
    finish(1)
    mains(3, 3)
    lora(2)
    lora(3)
    finish(2)
    finish(3)

    arrived(all_labels, many_sent.at[0])
    arrived(all_pages, many_sent.at[1])
    arrived(all_up, many_sent.at[2])
    for way in range(2):
        for hop in range(hops):
            ring_copy(way, hop).wait_send()
    for h in range(HALF_COUNT):
        for way in range(2):
            step_one(h, way).wait_send()
            step_one_half(h, way).wait_send()
            for k in range(4):
                step_two(h, k, way).wait_send()
                relay(h, k, way).wait_send()
            for step in range(hops):
                for p in range(2):
                    main_copy(h, way, step, p).wait_send()
        for k in range(4):
            for j in range(4):
                to_mate(h, k, j).wait_send()
    for h in range(HALF_COUNT):
        arrived(lowsend.at[h, pl.ds(0, n - 1)], low_sent.at[0, h])

        @pl.when(lane != home_plane)
        def _():
            low_over(h).wait_send()

        @pl.when(lane == home_plane)
        def _():
            arrived(lowsend.at[h, pl.ds(0, n - 1)], low_sent.at[2, h])


def layer(n, planes, home, adapter, storage, lengths, queries, incoming, pages, up, weights, down):
    rows, depth = queries.shape
    columns = weights.shape[1]
    hops, subs, half = planes // 2, n // planes, rows // HALF_COUNT
    hbm = pl.BlockSpec(memory_space=pltpu.HBM)
    vmem = pl.BlockSpec(memory_space=pltpu.VMEM)
    smem = pl.BlockSpec(memory_space=pltpu.SMEM)
    dma = pltpu.SemaphoreType.DMA
    bf16, f32, i32 = jnp.bfloat16, jnp.float32, jnp.int32
    hc = HALF_COUNT
    return pl.pallas_call(
        layer_kernel,
        out_shape=jax.ShapeDtypeStruct((n * rows // planes, columns), bf16),
        in_specs=[vmem, smem, smem, smem, smem, vmem, vmem, hbm, hbm, vmem, vmem],
        out_specs=vmem,
        scratch_shapes=[
            pltpu.VMEM((pages.shape[0] + n * CAP, PAGE_ROWS, HEAD_WIDTH), bf16),
            pltpu.VMEM((n * CAP, PAGE_ROWS, HEAD_WIDTH), bf16),
            pltpu.VMEM((n * CAP, PAGE_ROWS, HEAD_WIDTH), bf16),
            pltpu.VMEM((n, 1, HEAD_WIDTH), i32),
            pltpu.VMEM((n, 1, HEAD_WIDTH), i32),
            pltpu.VMEM((n, HEAD_WIDTH), i32),
            pltpu.SMEM((n, HEAD_WIDTH), i32),
            pltpu.VMEM(home.shape, i32),
            pltpu.SMEM(home.shape, i32),
            pltpu.VMEM((rows, depth), f32),
            pltpu.VMEM((rows, depth), bf16),
            pltpu.VMEM((n, planes, up.shape[0] // planes, columns), bf16),
            pltpu.VMEM((n, rows, depth), bf16),
            pltpu.VMEM((n, rows, columns), f32),
            pltpu.VMEM((hc, 2, hops, 2, subs // 2, half, columns), bf16),
            pltpu.VMEM((hc, 2, hops, 2, subs // 2, half, columns), bf16),
            pltpu.VMEM((hc, n, half // 2, HEAD_WIDTH), bf16),
            pltpu.VMEM((hc, n, half // 2, HEAD_WIDTH), bf16),
            pltpu.VMEM((hc, half // 2, HEAD_WIDTH), bf16),
            pltpu.VMEM((hc, planes, half // 2, HEAD_WIDTH), bf16),
            pltpu.VMEM((hc, subs, half // 2, HEAD_WIDTH), bf16),
            pltpu.VMEM((hc, subs * half, columns), f32),
        ]
        + [dma((3,))] * 2
        + [dma((2, hops))] * 2
        + [dma((4 + HALF_COUNT,))]
        + [dma((hc, 4))] * 2
        + [dma((hc, 4, 2))] * 4
        + [dma((hc, 4, 4))] * 2
        + [dma((hc, 2, hops, 2))] * 2
        + [dma((3, hc))] * 2
        + [dma((hc, subs))],
        compiler_params=pltpu.CompilerParams(
            collective_id=0, has_side_effects=True, vmem_limit_bytes=VMEM_BYTES
        ),
        name="layer",
    )(home, home, adapter, storage, lengths, queries, incoming, pages, up, weights, down)


def on_device(
    queries,
    incoming_key_value,
    key_value_pages,
    page_request_home,
    lengths,
    request_adapter_index,
    adapter_storage_slot,
    adapter_down_factor,
    adapter_up_factor,
    output_projection_weight,
):
    per_dev = key_value_pages.shape[0]
    own_adapters, depth, rank = adapter_down_factor.shape
    return layer(
        lax.axis_size("req"),
        lax.axis_size("tp"),
        page_request_home.reshape(-1, HEAD_WIDTH),
        request_adapter_index,
        adapter_storage_slot,
        lengths,
        queries,
        incoming_key_value,
        key_value_pages.reshape(per_dev, PAGE_ROWS, HEAD_WIDTH),
        adapter_up_factor.reshape(-1, adapter_up_factor.shape[2]),
        output_projection_weight,
        jnp.transpose(adapter_down_factor, (0, 2, 1)).reshape(own_adapters * rank, depth),
    )


def solution(mesh):
    return jax.shard_map(
        on_device,
        mesh=mesh,
        in_specs=(
            P("req", "tp"),
            P(None, "req", "tp"),
            P("req", None, None, "tp"),
            P("req"),
            P("req"),
            P("req"),
            P(),
            P("req", "tp", None),
            P("req", None, None),
            P("tp", "req"),
        ),
        out_specs=P("tp", "req"),
        check_vma=False,
    )
```
